32 devices in a mesh: blk: 8 (over y, x, core), feat: 4 (over z).
Axes of the slice: x: 2, y: 2, z: 4, core: 2. Of those that a mesh axis runs over, the one named last changes fastest.
Arguments:
- node_feats: bfloat16 [8192, 512], P('blk', 'feat'), may hold values from -6 to 6
- weight: bfloat16 [512, 512], P(None, 'feat'), may hold values from -0.25 to 0.25
- tile_value: bfloat16 [8, 5, 8, 128, 128], P('blk'), may hold values from -0.75 to 0.75
- tile_row: int32 [8, 5, 8], P('blk'), may hold values from 0 to 7
- tile_col: int32 [8, 5, 8], P('blk'), may hold values from 0 to 7
- tile_count: int32 [8, 5], P('blk'), may hold values from 2 to 8, as said below
- grad_out: bfloat16 [8192, 512], P('blk', 'feat'), may hold values from -6 to 6
Outputs:
- output_y: bfloat16 [8192, 512], P('blk', 'feat')
- grad_x: bfloat16 [8192, 512], P('blk', 'feat')
- grad_w: float32 [512, 512], P(None, 'feat')
The draws below stay inside these ranges and needn't reach their ends.
Inputs may be any that keep to these rules, and one draw needn't show every extreme that they name: `tile_count`: in every draw one owner has all 8 slots live for every distance; owners differ in how many tiles they hold.
All inputs are finite; a program needn't handle non-finite values.
Results may differ from the reference program's by a relative error of at most 0.0062.
Values may be sent and summed in bfloat16 or wider, within the bound.
A program may use at most 64 MiB of HBM per device.

```python
import jax
import jax.numpy as jnp
from jax import lax

D = 512
TB = 128
RB = 8
REACH = 2
SLOTS = 8
OFFS = 5
OWNERS = 8
NODES = 8192


def draw_tile_count(key, part):
    key_base, key_heavy, key_full = jax.random.split(key, 3)
    base_count = jax.random.randint(key_base, (OWNERS, OFFS), SLOTS // 4, SLOTS * 5 // 8 + 1)
    heavy_owner = jax.random.randint(key_heavy, (OWNERS, 1), 0, 4) == 0
    counts_all = jnp.where(heavy_owner, jnp.minimum(base_count * 2, SLOTS), base_count)
    full_owner = jax.random.randint(key_full, (), 0, OWNERS)
    owner_ids = jnp.arange(OWNERS)[:, None]
    counts_all = jnp.where(owner_ids == full_owner, SLOTS, counts_all)
    return counts_all.astype(jnp.int32)


def with_ends(array, own_key, smallest, high):
    place = [jax.random.randint(jax.random.fold_in(own_key, axis), (), 0, length) for axis, length in enumerate(array.shape)]
    longest = array.shape.index(max(array.shape))
    neighbour = place[:longest] + [(place[longest] + 1) % array.shape[longest]] + place[longest + 1:]
    return array.at[tuple(place)].set(smallest).at[tuple(neighbour)].set(high)


def block_scale(stream_key, dims, shards, least, largest):
    def one(axis_at, shards_of):
        heights = jax.random.uniform(jax.random.fold_in(jax.random.fold_in(stream_key, 6), axis_at), (shards_of,), jnp.float32, least / len(shards), largest / len(shards))
        return jnp.repeat(jnp.exp(heights), dims[axis_at] // shards_of).reshape((-1,) + (1,) * (len(dims) - axis_at - 1))

    gain = one(*shards[0])
    for cut in shards[1:]:
        gain = gain * one(*cut)
    return gain


def noise(stream_key, dims, width, reach, pieces=(), kind=jnp.bfloat16):
    gain = block_scale(stream_key, dims, pieces, -0.22, 0.18) if pieces else 1.0
    array = jax.random.normal(stream_key, dims, jnp.float32) * width * gain
    return jnp.minimum(jnp.maximum(array, -reach), reach).astype(kind)


def setup_inputs(seed: int = 0) -> dict:
    arg_keys = jax.random.split(jax.random.key(seed), 8)
    return {
        "node_feats": noise(arg_keys[0], (NODES, D), 1.0, 6.0, ((0, 8), (1, 4))),
        "weight": noise(arg_keys[1], (D, D), D ** -0.5, 0.25, ((1, 4),)),
        "tile_value": noise(arg_keys[2], (OWNERS, OFFS, SLOTS, TB, TB), ((3 * TB) ** -0.5), 0.75, ((0, 8),)),
        "tile_row": with_ends(jax.random.randint(arg_keys[3], (OWNERS, OFFS, SLOTS), 0, RB), jax.random.fold_in(arg_keys[3], 1), 0, RB - 1).astype(jnp.int32),
        "tile_col": with_ends(jax.random.randint(arg_keys[4], (OWNERS, OFFS, SLOTS), 0, RB), jax.random.fold_in(arg_keys[4], 1), 0, RB - 1).astype(jnp.int32),
        "tile_count": draw_tile_count(jax.random.fold_in(arg_keys[7], 71), 0),
        "grad_out": noise(arg_keys[6], (NODES, D), 1.0, 6.0, ((0, 8), (1, 4))),
    }


def reference(node_feats, weight, tile_value, tile_row, tile_col, tile_count, grad_out):
    hidden = jnp.dot(node_feats, weight, preferred_element_type=jnp.float32).astype(jnp.bfloat16)
    hidden_blocks = hidden.reshape(OWNERS, RB, TB, D)
    slot_ids = jnp.arange(SLOTS, dtype=jnp.int32)
    block_ids = jnp.arange(RB, dtype=jnp.int32)

    def forward_one(owner):
        accum_total = jnp.zeros((RB, TB, D), jnp.float32)
        for offset in range(OFFS):
            source = ((owner + offset - REACH) % OWNERS).astype(jnp.int32)
            panel_block = lax.dynamic_index_in_dim(hidden_blocks, source, 0, keepdims=False)
            tile_block = tile_value[owner, offset].astype(jnp.float32)
            picked = jnp.take(panel_block, tile_col[owner, offset], axis=0).astype(jnp.float32)
            product = jnp.einsum('sij,sjf->sif', tile_block, picked, precision=lax.Precision.HIGHEST)
            live_slots = slot_ids < tile_count[owner, offset]
            onehot = ((tile_row[owner, offset][None, :] == block_ids[:, None]) & live_slots[None, :]).astype(jnp.float32)
            accum_total = accum_total + jnp.einsum('rs,sif->rif', onehot, product, precision=lax.Precision.HIGHEST)
        return accum_total

    aggregated = lax.map(forward_one, jnp.arange(OWNERS, dtype=jnp.int32)).reshape(NODES, D)
    preact = aggregated + hidden.astype(jnp.float32)
    output_y = jax.nn.silu(preact).astype(jnp.bfloat16)
    sigmoid_pre = jax.nn.sigmoid(preact)
    slope_term = sigmoid_pre * (1.0 + preact * (1.0 - sigmoid_pre))
    grad_pre = (grad_out.astype(jnp.float32) * slope_term).astype(jnp.bfloat16)
    grad_blocks = grad_pre.reshape(OWNERS, RB, TB, D)

    def backward_one(target):
        accum_total = jnp.zeros((RB, TB, D), jnp.float32)
        for offset in range(OFFS):
            owner = ((target - offset + REACH) % OWNERS).astype(jnp.int32)
            tile_block = lax.dynamic_index_in_dim(tile_value[:, offset], owner, 0, keepdims=False).astype(jnp.float32)
            rows_here = lax.dynamic_index_in_dim(tile_row[:, offset], owner, 0, keepdims=False)
            cols_here = lax.dynamic_index_in_dim(tile_col[:, offset], owner, 0, keepdims=False)
            count_here = lax.dynamic_index_in_dim(tile_count[:, offset], owner, 0, keepdims=False)
            owner_grads = lax.dynamic_index_in_dim(grad_blocks, owner, 0, keepdims=False)
            picked = jnp.take(owner_grads, rows_here, axis=0).astype(jnp.float32)
            product = jnp.einsum('sji,sjf->sif', tile_block, picked, precision=lax.Precision.HIGHEST)
            live_slots = slot_ids < count_here
            onehot = ((cols_here[None, :] == block_ids[:, None]) & live_slots[None, :]).astype(jnp.float32)
            accum_total = accum_total + jnp.einsum('cs,sif->cif', onehot, product, precision=lax.Precision.HIGHEST)
        return accum_total

    transposed = lax.map(backward_one, jnp.arange(OWNERS, dtype=jnp.int32)).reshape(NODES, D)
    grad_hidden = (grad_pre.astype(jnp.float32) + transposed).astype(jnp.bfloat16)
    grad_w = jnp.dot(node_feats.T, grad_hidden, preferred_element_type=jnp.float32)
    grad_x = jnp.dot(grad_hidden, weight.T, preferred_element_type=jnp.float32).astype(jnp.bfloat16)
    return (output_y, grad_x, grad_w)
```

```python
import functools

import jax
import jax.numpy as jnp
from jax import lax
from jax.experimental import pallas as pl
from jax.experimental.pallas import tpu as pltpu
from jax.sharding import PartitionSpec as P

MESH = pl.DeviceIdType.MESH
BF = jnp.bfloat16
F32 = jnp.float32


def stage_factors(count, rows):
    factors = []
    while count > 1:
        size = max(f for f in range(2, 17) if count % f == 0 and rows % (16 * f) == 0)
        factors.append(size)
        count //= size
    return factors


def remote(src, dst, send, recv, where):
    return pltpu.make_async_remote_copy(
        src_ref=src, dst_ref=dst, send_sem=send, recv_sem=recv, device_id=where, device_id_type=MESH
    )


def layer_kernel(
    dims, x, w_in, tv_in, tr, tc, cnt, go_in, y, gx, gw,
    xg, wg, tv, go, tt, prod, acc, gp, sent, got, gg, gwb, pe, ge, *rest
):
    nb, nz, offs, slots, blocks, side, width, ow, factors = dims
    stages = len(factors)
    hid, rest = rest[:offs], rest[offs:]
    gathered, summed = rest[:stages], rest[stages : 2 * stages]
    (xs, xr, xl, xb, hs, hr, gs, gr, zs, zr, es, ges, ger, ws, wr, ks, kr, near) = rest[2 * stages : 2 * stages + 18]
    psems = rest[2 * stages + 18 :]
    reach = (offs - 1) // 2
    half = nz // 2
    me = lax.axis_index("feat")
    own = lax.axis_index("blk")
    core = lax.rem(own, 2)
    turn = 1 - 2 * core
    OWN, PAIR, CROSS, AHEAD, BEHIND = range(5)
    lean = (0, 1, -1, 2, -2)
    lower = me < half
    inner = jnp.where(lower, half - 1, half)
    other = nz - 1 - inner
    is_inner = me == inner
    ends = range(1, half)
    relayed = (blocks // 2 - 1, blocks // 2)

    def end_at(j):
        return jnp.where(lower, half - 1 - j, half + j)

    def in_relay(b):
        return (b >= relayed[0]) & (b <= relayed[1])

    def offset_of(role):
        return reach + lean[role] * turn

    def owner_at(role):
        return {"blk": lax.rem(own + lean[role] * turn + nb, nb)}

    def rows(b):
        return pl.ds(pl.multiple_of(b * side, side), side)

    def xcols(z):
        return pl.ds(pl.multiple_of(z * width, width), width)

    def ocols(z):
        return pl.ds(pl.multiple_of(z * ow, ow), ow)

    local = [
        pltpu.make_async_copy(w_in, wg.at[:, ocols(me)], near.at[0]),
        pltpu.make_async_copy(x, xg.at[:, xcols(me)], near.at[1]),
        pltpu.make_async_copy(tv_in.at[0], tv, near.at[2]),
        pltpu.make_async_copy(go_in, go, near.at[3]),
    ]
    for copy in local:
        copy.start()

    def stage_peer(stage, step):
        stride = 1
        for f in factors[:stage]:
            stride *= f
        size = factors[stage]
        digit = lax.rem(own // stride, size)
        there = lax.rem(digit + step, size)
        return digit, there, own + (there - digit) * stride

    barrier = pltpu.get_barrier_semaphore()
    greeted = 0
    for step in range(1, nz):
        pl.semaphore_signal(barrier, inc=1, device_id={"feat": lax.rem(me + step, nz)}, device_id_type=MESH)
        greeted += 1
    for role in (PAIR, AHEAD, BEHIND) if stages > 1 else ():
        pl.semaphore_signal(barrier, inc=1, device_id=owner_at(role), device_id_type=MESH)
        greeted += 1
    for stage in range(stages):
        for step in range(1, factors[stage]):
            _, _, peer = stage_peer(stage, step)
            pl.semaphore_signal(barrier, inc=1, device_id={"blk": peer}, device_id_type=MESH)
            greeted += 1
    pl.semaphore_wait(barrier, greeted)

    depth = w_in.shape[0]

    def part_of(piece):
        return pl.ds(pl.multiple_of(piece * (depth // 2), depth // 2), depth // 2)

    def x_copy(way, b):
        return remote(
            x.at[rows(b), :], xg.at[rows(b), xcols(me)], xs.at[way, b], xr.at[me, b], {"feat": (inner, other)[way]}
        )

    def x_relay(e, b):
        piece = xg.at[rows(b), xcols(e)]
        return remote(piece, piece, xl.at[e, b], xr.at[e, b], {"feat": other})

    def x_back(s, e, j, b):
        piece = xg.at[rows(b), xcols(s)]
        return remote(piece, piece, xb.at[j - 1, s, b], xr.at[s, b], {"feat": e})

    def x_wait(s, b):
        piece = xg.at[rows(b), xcols(s)]
        remote(piece, piece, xl.at[s, b], xr.at[s, b], {"feat": other}).wait_recv()

    def w_up():
        return remote(w_in.at[part_of(core), :], wg.at[part_of(core), ocols(me)], ws.at[0, 0], wr.at[me, core], {"feat": inner})

    def w_across(e):
        piece = wg.at[part_of(core), ocols(e)]
        return remote(piece, piece, ws.at[1, e], wr.at[e, core], owner_at(PAIR))

    def w_wait(e, piece):
        ref = wg.at[part_of(piece), ocols(e)]
        remote(ref, ref, ws.at[1, e], wr.at[e, piece], owner_at(PAIR)).wait_recv()

    def w_swap(sending):
        there = jnp.where(lower, half, 0)
        here = half - there
        r, c = (there, here) if sending else (here, there)
        piece = wg.at[
            pl.ds(pl.multiple_of(r * width, width), half * width), pl.ds(pl.multiple_of(c * ow, ow), half * ow)
        ]
        return remote(piece, piece, ks.at[0], kr.at[0], {"feat": other})

    @pl.when(is_inner)
    def _():
        for b in range(min(4, blocks)):
            x_copy(1, b).start()

    @pl.when(jnp.logical_not(is_inner))
    def _():
        for b in range(blocks):
            if b not in relayed:
                x_copy(1, b).start()
            x_copy(0, b).start()
            if b == 0:
                w_up().start()

    for copy in local[:3]:
        copy.wait()

    landing = {PAIR: PAIR, AHEAD: BEHIND, BEHIND: AHEAD}

    def hid_copy(role, b):
        return remote(hid[OWN].at[b], hid[landing[role]].at[b], hs.at[role, b], hr.at[landing[role], b], owner_at(role))

    def hid_wait(role, b):
        remote(hid[role].at[b], hid[role].at[b], hs.at[role, b], hr.at[role, b], owner_at(PAIR)).wait_recv()

    def hid_passed(b):
        return remote(hid[AHEAD].at[b], hid[CROSS].at[b], hs.at[CROSS, b], hr.at[CROSS, b], owner_at(PAIR))

    def hid_relay(b):
        hid_wait(AHEAD, b)
        hid_passed(b).start()

    def hid_down(j, b):
        return remote(pe.at[j - 1, b], hid[OWN].at[b], es.at[j - 1, b], hr.at[OWN, b], {"feat": end_at(j)})

    def spread(b):
        hid_copy(AHEAD, b).start()
        hid_copy(BEHIND, b).start()
        hid_copy(PAIR, b).start()

    lag = 2

    def forward_step(b, carry):
        @pl.when(is_inner)
        def _():
            @pl.when(b + 4 < blocks)
            def _():
                x_copy(1, b + 4).start()

            @pl.when(in_relay(b + 2))
            def _():
                for j in ends:
                    x_wait(end_at(j), b + 2)
                    x_relay(end_at(j), b + 2).start()

        per_block = slots // blocks
        for role in range(offs):
            for s in range(per_block):
                slot = b * per_block + s
                tt[role, slot] = tv[offset_of(role), slot].T

        @pl.when(is_inner)
        def _():
            for j in ends:
                @pl.when(jnp.logical_not(in_relay(b)))
                def _():
                    x_wait(end_at(j), b)
            for j in range(half):
                x_wait(nz - 1 - end_at(j), b)
            hid[OWN][b] = jnp.dot(xg[rows(b), :], wg[:, ocols(me)], preferred_element_type=F32).astype(BF)
            spread(b)

            @pl.when(b == 0)
            def _():
                for j in ends:
                    w_wait(end_at(j), core)
                    w_across(end_at(j)).start()
                for j in ends:
                    w_wait(end_at(j), 1 - core)

            for j in ends:
                pe[j - 1, b] = jnp.dot(xg[rows(b), :], wg[:, ocols(end_at(j))], preferred_element_type=F32).astype(BF)
                hid_down(j, b).start()
                x_back(me, end_at(j), j, b).start()

        @pl.when(jnp.logical_not(is_inner))
        def _():
            hid_wait(OWN, b)
            spread(b)

        @pl.when(b >= lag)
        def _():
            hid_relay(b - lag)

        return carry

    lax.fori_loop(0, blocks, forward_step, 0)

    def forward_products(role):
        k = offset_of(role)
        for s in range(slots):
            prod[role, s] = jnp.dot(tv[k, s], hid[role][tc[k, 0, s]], preferred_element_type=F32)

    def weight_of(table, k, s, b):
        return jnp.where((table[k, 0, s] == b) & (s < cnt[0, k]), 1.0, 0.0).astype(F32)

    def row_sum(role, b, total):
        for s in range(slots):
            total = total + prod[role, s] * weight_of(tr, offset_of(role), s, b)
        return total

    def gather_role(role):
        forward_products(role)

        def add(b, carry):
            start = hid[OWN][b].astype(F32) if role == OWN else acc[b]
            acc[b] = row_sum(role, b, start)
            return carry

        lax.fori_loop(0, blocks, add, 0)

    gather_role(OWN)
    for b in range(blocks):
        hid_wait(PAIR, b)
    gather_role(PAIR)
    for b in range(max(blocks - lag, 0), blocks):
        hid_relay(b)

    @pl.when(is_inner)
    def _():
        w_swap(True).start()
        for j in ends:
            for b in range(blocks):
                for step in range(1, nz):
                    s = lax.rem(me + step, nz)

                    @pl.when(s != end_at(j))
                    def _():
                        x_back(s, end_at(j), j, b).start()

    gather_role(AHEAD)
    for b in range(blocks):
        hid_wait(BEHIND, b)
    gather_role(BEHIND)
    local[3].wait()
    for b in range(blocks):
        hid_wait(CROSS, b)
    forward_products(CROSS)

    def pointwise(b, carry):
        v = row_sum(CROSS, b, acc[b])
        sigma = jax.nn.sigmoid(v)
        y[rows(b), :] = (v * sigma).astype(BF)
        slope = sigma * (1.0 + v * (1.0 - sigma))
        gp[b] = (go[rows(b), :].astype(F32) * slope).astype(BF)
        return carry

    lax.fori_loop(0, blocks, pointwise, 0)

    def backward_products(role):
        for s in range(slots):
            prod[role, s] = jnp.dot(tt[role, s], gp[tr[offset_of(role), 0, s]], preferred_element_type=F32)

    def column_sum(role, c, start):
        total = start
        for s in range(slots):
            term = prod[role, s] * weight_of(tc, offset_of(role), s, c)
            total = term if total is None else total + term
        return total

    target = {PAIR: PAIR, CROSS: PAIR, AHEAD: AHEAD, BEHIND: BEHIND}
    arrives = {PAIR: PAIR, CROSS: CROSS, AHEAD: BEHIND, BEHIND: AHEAD}

    def sum_copy(role, c):
        return remote(
            sent.at[role, c], got.at[arrives[role], c], gs.at[role, c], gr.at[arrives[role], c], owner_at(target[role])
        )

    def sum_wait(role, c):
        remote(got.at[role, c], got.at[role, c], gs.at[role, c], gr.at[role, c], owner_at(PAIR)).wait_recv()

    def send_sum(role, c):
        sent[role, c] = column_sum(role, c, None).astype(BF)
        sum_copy(role, c).start()

    def send_joint(c):
        sum_wait(CROSS, c)
        sent[AHEAD, c] = column_sum(AHEAD, c, got[CROSS, c].astype(F32)).astype(BF)
        sum_copy(AHEAD, c).start()

    def loop(step):
        def body(c, carry):
            step(c)
            return carry

        lax.fori_loop(0, blocks, body, 0)

    backward_products(CROSS)
    loop(lambda c: send_sum(CROSS, c))
    backward_products(BEHIND)
    backward_products(AHEAD)

    def send_far(c):
        send_sum(BEHIND, c)
        send_joint(c)

    loop(send_far)
    backward_products(PAIR)
    loop(lambda c: send_sum(PAIR, c))
    backward_products(OWN)

    gw[...] = jnp.zeros_like(gw)

    def g_copy(way, b):
        piece = gg.at[rows(b), ocols(me)]
        return remote(piece, piece, zs.at[way, b], zr.at[me, b], {"feat": (inner, other)[way]})

    def g_wait(s, b):
        piece = gg.at[rows(b), ocols(s)]
        remote(piece, piece, zs.at[0, b], zr.at[s, b], {"feat": other}).wait_recv()

    def make_grad(b):
        total = column_sum(OWN, b, gp[b].astype(F32))
        for role in (PAIR, BEHIND, AHEAD):
            sum_wait(role, b)
            total = total + got[role, b].astype(F32)
        grad = total.astype(BF)
        gg[rows(b), ocols(me)] = grad
        g_copy(1, b).start()

        @pl.when(jnp.logical_not(is_inner))
        def _():
            g_copy(0, b).start()
            for step in range(1, nz):
                x_wait(lax.rem(me + step, nz), b)

        gw[...] += lax.dot_general(xg[rows(b), :], grad, (((0,), (0,)), ((), ())), preferred_element_type=F32)

    def gx_down(j, b):
        return remote(ge.at[j - 1, b], gx.at[rows(b), :], ges.at[j - 1, b], ger.at[b], {"feat": end_at(j)})

    def finish(b):
        @pl.when(is_inner)
        def _():
            @pl.when(b == 0)
            def _():
                w_swap(False).wait_recv()

            for step in range(1, nz):
                g_wait(lax.rem(me + step, nz), b)

            def grad_of(z):
                return lax.dot_general(
                    gg[rows(b), :], wg[xcols(z), :], (((1,), (1,)), ((), ())), preferred_element_type=F32
                ).astype(BF)

            for j in ends:
                ge[j - 1, b] = grad_of(end_at(j))
                gx_down(j, b).start()
            gx[rows(b), :] = grad_of(me)

    behind = 3

    def backward_step(c, carry):
        make_grad(c)

        @pl.when(c >= behind)
        def _():
            finish(c - behind)

        return carry

    lax.fori_loop(0, blocks, backward_step, 0)

    gwb[...] = gw[...].astype(BF)
    height = gw.shape[0]
    for stage in range(stages):
        size = factors[stage]
        chunk = height // size
        src, buf, out = gwb if stage == 0 else summed[stage - 1], gathered[stage], summed[stage]
        rs_s, rs_r, ag_s, ag_r = psems[4 * stage : 4 * stage + 4]

        def part(q):
            return pl.ds(pl.multiple_of(q * chunk, chunk), chunk)

        for step in range(1, size):
            _, there, peer = stage_peer(stage, step)
            remote(src.at[part(there), :], buf.at[step], rs_s.at[step], rs_r.at[step], {"blk": peer}).start()
        if stage == 0:
            for b in range(blocks - behind, blocks - 1):
                finish(b)
        digit, _, _ = stage_peer(stage, 1)
        if stage == 0:
            total = gw[part(digit), :]
        else:
            total = src[part(digit), :].astype(F32)
        for step in range(1, size):
            _, _, peer = stage_peer(stage, step)
            remote(buf.at[step], buf.at[step], rs_s.at[step], rs_r.at[step], {"blk": peer}).wait_recv()
            total = total + buf[step].astype(F32)
        out[part(digit), :] = total.astype(BF)
        for step in range(1, size):
            _, _, peer = stage_peer(stage, step)
            piece = out.at[part(digit), :]
            remote(piece, piece, ag_s.at[step], ag_r.at[step], {"blk": peer}).start()
        if stage == 0:
            finish(blocks - 1)
        for step in range(1, size):
            _, there, peer = stage_peer(stage, size - step)
            piece = out.at[part(there), :]
            remote(piece, piece, ag_s.at[step], ag_r.at[step], {"blk": peer}).wait_recv()
    gw[...] = (summed[-1] if stages else gwb)[...].astype(F32)

    for stage in range(stages):
        size = factors[stage]
        buf = gathered[stage]
        rs_s, rs_r, ag_s, ag_r = psems[4 * stage : 4 * stage + 4]
        for step in range(1, size):
            _, _, peer = stage_peer(stage, step)
            remote(buf.at[step], buf.at[step], rs_s.at[step], rs_r.at[step], {"blk": peer}).wait_send()
            remote(buf.at[step], buf.at[step], ag_s.at[step], ag_r.at[step], {"blk": peer}).wait_send()

    def drain(b, carry):
        g_copy(1, b).wait_send()

        @pl.when(is_inner)
        def _():
            x_copy(1, b).wait_send()
            for j in ends:
                @pl.when(in_relay(b))
                def _():
                    x_relay(end_at(j), b).wait_send()

                hid_down(j, b).wait_send()
                gx_down(j, b).wait_send()
                for step in range(nz):
                    s = lax.rem(me + step, nz)

                    @pl.when(s != end_at(j))
                    def _():
                        x_back(s, end_at(j), j, b).wait_send()

        @pl.when(jnp.logical_not(is_inner))
        def _():
            @pl.when(jnp.logical_not(in_relay(b)))
            def _():
                x_copy(1, b).wait_send()

            x_copy(0, b).wait_send()
            g_copy(0, b).wait_send()
            remote(gx.at[rows(b), :], gx.at[rows(b), :], ges.at[0, b], ger.at[b], {"feat": inner}).wait_recv()

        for role in (PAIR, AHEAD, BEHIND):
            hid_copy(role, b).wait_send()
        hid_passed(b).wait_send()
        for role in (PAIR, CROSS, AHEAD, BEHIND):
            sum_copy(role, b).wait_send()
        return carry

    lax.fori_loop(0, blocks, drain, 0)

    @pl.when(is_inner)
    def _():
        w_swap(True).wait_send()
        for j in ends:
            w_across(end_at(j)).wait_send()

    @pl.when(jnp.logical_not(is_inner))
    def _():
        w_up().wait_send()


def on_device(nb, nz, x, w, tv, tr, tc, cnt, go):
    offs, slots, side = tv.shape[1], tv.shape[2], tv.shape[-1]
    height, width = x.shape
    blocks = height // side
    depth, ow = w.shape
    factors = stage_factors(nb, depth)
    dims = (nb, nz, offs, slots, blocks, side, width, ow, tuple(factors))
    spare = max(nz // 2 - 1, 1)
    vmem = pl.BlockSpec(memory_space=pltpu.VMEM)
    hbm = pl.BlockSpec(memory_space=pltpu.HBM)
    smem = pl.BlockSpec(memory_space=pltpu.SMEM)
    dma = pltpu.SemaphoreType.DMA
    psems = []
    for f in factors:
        psems += [dma((f,))] * 4
    banded = [dma((offs, blocks))] * 2
    block = (side, ow)
    return pl.pallas_call(
        functools.partial(layer_kernel, dims),
        out_shape=(
            jax.ShapeDtypeStruct((height, ow), BF),
            jax.ShapeDtypeStruct((height, width), BF),
            jax.ShapeDtypeStruct((depth, ow), F32),
        ),
        in_specs=[hbm, hbm, hbm, smem, smem, smem, hbm],
        out_specs=(vmem, vmem, vmem),
        scratch_shapes=[
            pltpu.VMEM((height, nz * width), BF),
            pltpu.VMEM((depth, nz * ow), BF),
            pltpu.VMEM((offs, slots, side, side), BF),
            pltpu.VMEM((height, ow), BF),
            pltpu.VMEM((offs, slots, side, side), BF),
            pltpu.VMEM((offs, slots, *block), F32),
            pltpu.VMEM((blocks, *block), F32),
            pltpu.VMEM((blocks, *block), BF),
            pltpu.VMEM((offs, blocks, *block), BF),
            pltpu.VMEM((offs, blocks, *block), BF),
            pltpu.VMEM((height, nz * ow), BF),
            pltpu.VMEM((depth, ow), BF),
            pltpu.VMEM((spare, blocks, *block), BF),
            pltpu.VMEM((spare, blocks, side, width), BF),
        ]
        + [pltpu.VMEM((blocks, *block), BF)] * offs
        + [pltpu.VMEM((f, depth // f, ow), BF) for f in factors]
        + [pltpu.VMEM((depth, ow), BF) for f in factors]
        + [dma((2, blocks)), dma((nz, blocks)), dma((nz, blocks)), dma((spare, nz, blocks))]
        + banded
        + banded
        + [dma((2, blocks)), dma((nz, blocks))]
        + [dma((spare, blocks)), dma((spare, blocks)), dma((blocks,))]
        + [dma((2, nz)), dma((nz, 2)), dma((1,)), dma((1,)), dma((4,))]
        + psems,
        compiler_params=pltpu.CompilerParams(
            collective_id=0, has_side_effects=True, vmem_limit_bytes=63 * 1024 * 1024
        ),
    )(x, w, tv, jnp.swapaxes(tr, 0, 1), jnp.swapaxes(tc, 0, 1), cnt, go)


def solution(mesh):
    return jax.shard_map(
        functools.partial(on_device, mesh.shape["blk"], mesh.shape["feat"]),
        mesh=mesh,
        in_specs=(
            P("blk", "feat"),
            P(None, "feat"),
            P("blk", None, None, None, None),
            P("blk", None, None),
            P("blk", None, None),
            P("blk", None),
            P("blk", "feat"),
        ),
        out_specs=(P("blk", "feat"), P("blk", "feat"), P(None, "feat")),
        check_vma=False,
    )
```

```python
import functools

import jax
import jax.numpy as jnp
from jax import lax
from jax.experimental import pallas as pl
from jax.experimental.pallas import tpu as pltpu
from jax.sharding import PartitionSpec as P

MESH = pl.DeviceIdType.MESH
BF = jnp.bfloat16
F32 = jnp.float32


def stage_factors(count, rows):
    factors = []
    while count > 1:
        size = max(f for f in range(2, 17) if count % f == 0 and rows % (16 * f) == 0)
        factors.append(size)
        count //= size
    return factors


def remote(src, dst, send, recv, where):
    return pltpu.make_async_remote_copy(
        src_ref=src, dst_ref=dst, send_sem=send, recv_sem=recv, device_id=where, device_id_type=MESH
    )


def layer_kernel(
    dims, x, w_in, tv_in, tr_in, tc_in, cnt_in, go_in, y, gx, gw,
    tr, tc, cnt, xg, wg, tv, go, tt, prod, acc, gp, sent, got, gg, gwb, pe, ge, *rest
):
    nb, nz, offs, slots, blocks, side, width, ow, factors = dims
    stages = len(factors)
    hid, rest = rest[:offs], rest[offs:]
    gathered, summed = rest[:stages], rest[stages : 2 * stages]
    (xs, xr, xe, xl, xb, hs, hr, hall, gs, gr, zs, zr, es, ges, ger, ws, wr, ks, kr, near) = rest[2 * stages : 2 * stages + 20]
    psems = rest[2 * stages + 20 :]
    reach = (offs - 1) // 2
    half = nz // 2
    me = lax.axis_index("feat")
    own = lax.axis_index("blk")
    core = lax.rem(own, 2)
    turn = 1 - 2 * core
    OWN, PAIR, CROSS, AHEAD, BEHIND = range(5)
    lean = (0, 1, -1, 2, -2)
    lower = me < half
    inner = jnp.where(lower, half - 1, half)
    other = nz - 1 - inner
    is_inner = me == inner
    ends = range(1, half)
    relayed = (blocks // 2 - 1, blocks // 2)

    def end_at(j):
        return jnp.where(lower, half - 1 - j, half + j)

    def in_relay(b):
        return (b >= relayed[0]) & (b <= relayed[1])

    def offset_of(role):
        return reach + lean[role] * turn

    def owner_at(role):
        return {"blk": lax.rem(own + lean[role] * turn + nb, nb)}

    def rows(b):
        return pl.ds(pl.multiple_of(b * side, side), side)

    def xcols(z):
        return pl.ds(pl.multiple_of(z * width, width), width)

    def ocols(z):
        return pl.ds(pl.multiple_of(z * ow, ow), ow)

    local = [
        pltpu.make_async_copy(w_in, wg.at[:, ocols(me)], near.at[0]),
        pltpu.make_async_copy(x, xg.at[:, xcols(me)], near.at[1]),
        pltpu.make_async_copy(tv_in.at[0], tv, near.at[2]),
        pltpu.make_async_copy(go_in, go, near.at[3]),
        pltpu.make_async_copy(tr_in, tr, near.at[4]),
        pltpu.make_async_copy(tc_in, tc, near.at[5]),
        pltpu.make_async_copy(cnt_in, cnt, near.at[6]),
    ]
    for copy in local:
        copy.start()

    def stage_peer(stage, step):
        stride = 1
        for f in factors[:stage]:
            stride *= f
        size = factors[stage]
        digit = lax.rem(own // stride, size)
        there = lax.rem(digit + step, size)
        return digit, there, own + (there - digit) * stride

    barrier = pltpu.get_barrier_semaphore()
    greeted = 0
    for step in range(1, nz):
        pl.semaphore_signal(barrier, inc=1, device_id={"feat": lax.rem(me + step, nz)}, device_id_type=MESH)
        greeted += 1
    for role in (PAIR, AHEAD, BEHIND) if stages > 1 else ():
        pl.semaphore_signal(barrier, inc=1, device_id=owner_at(role), device_id_type=MESH)
        greeted += 1
    for stage in range(stages):
        for step in range(1, factors[stage]):
            _, _, peer = stage_peer(stage, step)
            pl.semaphore_signal(barrier, inc=1, device_id={"blk": peer}, device_id_type=MESH)
            greeted += 1
    pl.semaphore_wait(barrier, greeted)

    depth = w_in.shape[0]

    def part_of(piece):
        return pl.ds(pl.multiple_of(piece * (depth // 2), depth // 2), depth // 2)

    def x_copy(way, b):
        landed = xe.at[me, b - relayed[0]] if way == 0 and b in relayed else xr.at[b]
        return remote(
            x.at[rows(b), :], xg.at[rows(b), xcols(me)], xs.at[way], landed, {"feat": (inner, other)[way]}
        )

    def x_relay(e, b):
        piece = xg.at[rows(b), xcols(e)]
        return remote(piece, piece, xl.at[0], xr.at[b], {"feat": other})

    def x_back(s, e, j, b):
        piece = xg.at[rows(b), xcols(s)]
        return remote(piece, piece, xb.at[j - 1], xr.at[b], {"feat": e})

    def x_early(e, b):
        piece = xg.at[rows(b), xcols(e)]
        remote(piece, piece, xl.at[0], xe.at[e, b - relayed[0]], {"feat": other}).wait_recv()

    def x_wait(count, b):
        piece = xg.at[rows(b), pl.ds(0, count * width)]
        remote(piece, piece, xl.at[0], xr.at[b], {"feat": other}).wait_recv()

    def w_up():
        return remote(w_in.at[part_of(core), :], wg.at[part_of(core), ocols(me)], ws.at[0, 0], wr.at[me, core], {"feat": inner})

    def w_across(e):
        piece = wg.at[part_of(core), ocols(e)]
        return remote(piece, piece, ws.at[1, e], wr.at[e, core], owner_at(PAIR))

    def w_wait(e, piece):
        ref = wg.at[part_of(piece), ocols(e)]
        remote(ref, ref, ws.at[1, e], wr.at[e, piece], owner_at(PAIR)).wait_recv()

    def w_swap(sending):
        there = jnp.where(lower, half, 0)
        here = half - there
        r, c = (there, here) if sending else (here, there)
        piece = wg.at[
            pl.ds(pl.multiple_of(r * width, width), half * width), pl.ds(pl.multiple_of(c * ow, ow), half * ow)
        ]
        return remote(piece, piece, ks.at[0], kr.at[0], {"feat": other})

    @pl.when(is_inner)
    def _():
        for b in range(min(4, blocks)):
            x_copy(1, b).start()

    @pl.when(jnp.logical_not(is_inner))
    def _():
        for b in range(blocks):
            if b not in relayed:
                x_copy(1, b).start()
            x_copy(0, b).start()
            if b == 0:
                w_up().start()

    for copy in local[:3]:
        copy.wait()

    landing = {PAIR: PAIR, AHEAD: BEHIND, BEHIND: AHEAD}

    def hid_copy(role, b):
        landed = hr.at[0, b] if role == BEHIND else hall.at[landing[role]]
        return remote(hid[OWN].at[b], hid[landing[role]].at[b], hs.at[role], landed, owner_at(role))

    def hid_wait(role, b):
        remote(hid[role].at[b], hid[role].at[b], hs.at[role], hr.at[int(role == OWN), b], owner_at(PAIR)).wait_recv()

    def hid_whole(role):
        remote(hid[role], hid[role], hs.at[role], hall.at[role], owner_at(PAIR)).wait_recv()

    def hid_passed(b):
        return remote(hid[AHEAD].at[b], hid[CROSS].at[b], hs.at[CROSS], hall.at[CROSS], owner_at(PAIR))

    def hid_relay(b):
        hid_wait(AHEAD, b)
        hid_passed(b).start()

    def hid_down(j, b):
        return remote(pe.at[j - 1, b], hid[OWN].at[b], es.at[j - 1], hr.at[1, b], {"feat": end_at(j)})

    def spread(b):
        hid_copy(AHEAD, b).start()
        hid_copy(BEHIND, b).start()
        hid_copy(PAIR, b).start()

    lag = 2

    def forward_step(b, carry):
        @pl.when(is_inner)
        def _():
            @pl.when(b + 4 < blocks)
            def _():
                x_copy(1, b + 4).start()

            @pl.when(in_relay(b + 2))
            def _():
                for j in ends:
                    x_early(end_at(j), b + 2)
                    x_relay(end_at(j), b + 2).start()

        per_block = slots // blocks
        for role in range(offs):
            for s in range(per_block):
                slot = b * per_block + s
                tt[role, slot] = tv[offset_of(role), slot].T

        @pl.when(is_inner)
        def _():
            @pl.when(in_relay(b))
            def _():
                x_wait(half, b)

            @pl.when(jnp.logical_not(in_relay(b)))
            def _():
                x_wait(nz - 1, b)

            hid[OWN][b] = jnp.dot(xg[rows(b), :], wg[:, ocols(me)], preferred_element_type=F32).astype(BF)
            spread(b)

            @pl.when(b == 0)
            def _():
                for j in ends:
                    w_wait(end_at(j), core)
                    w_across(end_at(j)).start()
                for j in ends:
                    w_wait(end_at(j), 1 - core)

            for j in ends:
                pe[j - 1, b] = jnp.dot(xg[rows(b), :], wg[:, ocols(end_at(j))], preferred_element_type=F32).astype(BF)
                hid_down(j, b).start()
                x_back(me, end_at(j), j, b).start()

        @pl.when(jnp.logical_not(is_inner))
        def _():
            hid_wait(OWN, b)
            spread(b)

        @pl.when(b >= lag)
        def _():
            hid_relay(b - lag)

        return carry

    lax.fori_loop(0, blocks, forward_step, 0)
    for copy in local[4:]:
        copy.wait()

    def forward_products(role):
        k = offset_of(role)
        for s in range(slots):
            prod[role, s] = jnp.dot(tv[k, s], hid[role][tc[k, 0, s]], preferred_element_type=F32)

    def weight_of(table, k, s, b):
        return jnp.where((table[k, 0, s] == b) & (s < cnt[0, k]), 1.0, 0.0).astype(F32)

    def row_sum(role, b, total):
        for s in range(slots):
            total = total + prod[role, s] * weight_of(tr, offset_of(role), s, b)
        return total

    def gather_role(role):
        forward_products(role)

        def add(b, carry):
            start = hid[OWN][b].astype(F32) if role == OWN else acc[b]
            acc[b] = row_sum(role, b, start)
            return carry

        lax.fori_loop(0, blocks, add, 0)

    gather_role(OWN)
    hid_whole(PAIR)
    gather_role(PAIR)
    for b in range(max(blocks - lag, 0), blocks):
        hid_relay(b)

    @pl.when(is_inner)
    def _():
        w_swap(True).start()
        for j in ends:
            for b in range(blocks):
                for step in range(1, nz):
                    s = lax.rem(me + step, nz)

                    @pl.when(s != end_at(j))
                    def _():
                        x_back(s, end_at(j), j, b).start()

    gather_role(AHEAD)
    hid_whole(BEHIND)
    gather_role(BEHIND)
    local[3].wait()
    hid_whole(CROSS)
    forward_products(CROSS)

    def pointwise(b, carry):
        v = row_sum(CROSS, b, acc[b])
        sigma = jax.nn.sigmoid(v)
        y[rows(b), :] = (v * sigma).astype(BF)
        slope = sigma * (1.0 + v * (1.0 - sigma))
        gp[b] = (go[rows(b), :].astype(F32) * slope).astype(BF)
        return carry

    lax.fori_loop(0, blocks, pointwise, 0)

    def backward_products(role):
        for s in range(slots):
            prod[role, s] = jnp.dot(tt[role, s], gp[tr[offset_of(role), 0, s]], preferred_element_type=F32)

    def column_sum(role, c, start):
        total = start
        for s in range(slots):
            term = prod[role, s] * weight_of(tc, offset_of(role), s, c)
            total = term if total is None else total + term
        return total

    target = {PAIR: PAIR, CROSS: PAIR, AHEAD: AHEAD, BEHIND: BEHIND}
    arrives = {PAIR: PAIR, CROSS: CROSS, AHEAD: BEHIND, BEHIND: AHEAD}

    def sum_copy(role, c):
        return remote(
            sent.at[role, c], got.at[arrives[role], c], gs.at[role], gr.at[int(role == CROSS), c], owner_at(target[role])
        )

    def cross_wait(c):
        piece = got.at[CROSS, c]
        remote(piece, piece, gs.at[CROSS], gr.at[1, c], owner_at(PAIR)).wait_recv()

    def sums_wait(c):
        piece = got.at[pl.ds(0, 3), c]
        remote(piece, piece, gs.at[PAIR], gr.at[0, c], owner_at(PAIR)).wait_recv()

    def send_sum(role, c):
        sent[role, c] = column_sum(role, c, None).astype(BF)
        sum_copy(role, c).start()

    def send_joint(c):
        cross_wait(c)
        sent[AHEAD, c] = column_sum(AHEAD, c, got[CROSS, c].astype(F32)).astype(BF)
        sum_copy(AHEAD, c).start()

    def loop(step):
        def body(c, carry):
            step(c)
            return carry

        lax.fori_loop(0, blocks, body, 0)

    backward_products(CROSS)
    loop(lambda c: send_sum(CROSS, c))
    backward_products(BEHIND)
    backward_products(AHEAD)

    def send_far(c):
        send_sum(BEHIND, c)
        send_joint(c)

    loop(send_far)
    backward_products(PAIR)
    loop(lambda c: send_sum(PAIR, c))
    backward_products(OWN)

    gw[...] = jnp.zeros_like(gw)

    def g_copy(way, b):
        piece = gg.at[rows(b), ocols(me)]
        return remote(piece, piece, zs.at[way], zr.at[b], {"feat": (inner, other)[way]})

    def g_wait(b):
        piece = gg.at[rows(b), pl.ds(0, (nz - 1) * ow)]
        remote(piece, piece, zs.at[0], zr.at[b], {"feat": other}).wait_recv()

    def make_grad(b):
        total = column_sum(OWN, b, gp[b].astype(F32))
        sums_wait(b)
        for role in (PAIR, BEHIND, AHEAD):
            total = total + got[role, b].astype(F32)
        grad = total.astype(BF)
        gg[rows(b), ocols(me)] = grad
        g_copy(1, b).start()

        @pl.when(jnp.logical_not(is_inner))
        def _():
            g_copy(0, b).start()
            x_wait(nz - 1, b)

        gw[...] += lax.dot_general(xg[rows(b), :], grad, (((0,), (0,)), ((), ())), preferred_element_type=F32)

    def gx_down(j, b):
        return remote(ge.at[j - 1, b], gx.at[rows(b), :], ges.at[j - 1], ger.at[0], {"feat": end_at(j)})

    def finish(b):
        @pl.when(is_inner)
        def _():
            @pl.when(b == 0)
            def _():
                w_swap(False).wait_recv()

            g_wait(b)

            def grad_of(z):
                return lax.dot_general(
                    gg[rows(b), :], wg[xcols(z), :], (((1,), (1,)), ((), ())), preferred_element_type=F32
                ).astype(BF)

            for j in ends:
                ge[j - 1, b] = grad_of(end_at(j))
                gx_down(j, b).start()
            gx[rows(b), :] = grad_of(me)

    behind = 3

    def backward_step(c, carry):
        make_grad(c)

        @pl.when(c >= behind)
        def _():
            finish(c - behind)

        return carry

    lax.fori_loop(0, blocks, backward_step, 0)

    gwb[...] = gw[...].astype(BF)
    height = gw.shape[0]
    for stage in range(stages):
        size = factors[stage]
        chunk = height // size
        src, buf, out = gwb if stage == 0 else summed[stage - 1], gathered[stage], summed[stage]
        rs_s, rs_r, ag_s, ag_r = psems[4 * stage : 4 * stage + 4]

        def part(q):
            return pl.ds(pl.multiple_of(q * chunk, chunk), chunk)

        for step in range(1, size):
            _, there, peer = stage_peer(stage, step)
            remote(src.at[part(there), :], buf.at[step - 1], rs_s.at[0], rs_r.at[0], {"blk": peer}).start()
        if stage == 0:
            for b in range(blocks - behind, blocks - 1):
                finish(b)
        digit, _, _ = stage_peer(stage, 1)
        if stage == 0:
            total = gw[part(digit), :]
        else:
            total = src[part(digit), :].astype(F32)
        remote(buf, buf, rs_s.at[0], rs_r.at[0], owner_at(PAIR)).wait_recv()
        for step in range(1, size):
            total = total + buf[step - 1].astype(F32)
        out[part(digit), :] = total.astype(BF)
        for step in range(1, size):
            _, _, peer = stage_peer(stage, step)
            piece = out.at[part(digit), :]
            remote(piece, piece, ag_s.at[0], ag_r.at[0], {"blk": peer}).start()
        if stage == 0:
            finish(blocks - 1)
        piece = out.at[pl.ds(0, height - chunk), :]
        remote(piece, piece, ag_s.at[0], ag_r.at[0], owner_at(PAIR)).wait_recv()
    gw[...] = (summed[-1] if stages else gwb)[...].astype(F32)

    for stage in range(stages):
        buf, out = gathered[stage], summed[stage]
        rs_s, rs_r, ag_s, ag_r = psems[4 * stage : 4 * stage + 4]
        remote(buf, buf, rs_s.at[0], rs_r.at[0], owner_at(PAIR)).wait_send()
        piece = out.at[pl.ds(0, height - height // factors[stage]), :]
        remote(piece, piece, ag_s.at[0], ag_r.at[0], owner_at(PAIR)).wait_send()

    def sent_all(ref, sem):
        remote(ref, ref, sem, ger.at[0], owner_at(PAIR)).wait_send()

    sent_all(gg.at[:, ocols(me)], zs.at[1])

    @pl.when(is_inner)
    def _():
        sent_all(x, xs.at[1])
        if half > 1:
            sent_all(xg.at[pl.ds(0, len(relayed) * side), pl.ds(0, (half - 1) * width)], xl.at[0])
        for j in ends:
            sent_all(pe.at[j - 1], es.at[j - 1])
            sent_all(ge.at[j - 1], ges.at[j - 1])
            sent_all(xg.at[:, pl.ds(0, (nz - 1) * width)], xb.at[j - 1])

    @pl.when(jnp.logical_not(is_inner))
    def _():
        sent_all(x.at[pl.ds(0, (blocks - len(relayed)) * side), :], xs.at[1])
        sent_all(x, xs.at[0])
        sent_all(gg.at[:, ocols(me)], zs.at[0])
        remote(gx, gx, ges.at[0], ger.at[0], {"feat": inner}).wait_recv()

    for role in (PAIR, CROSS, AHEAD, BEHIND):
        sent_all(hid[role], hs.at[role])
        sent_all(sent.at[role], gs.at[role])

    @pl.when(is_inner)
    def _():
        w_swap(True).wait_send()
        for j in ends:
            w_across(end_at(j)).wait_send()

    @pl.when(jnp.logical_not(is_inner))
    def _():
        w_up().wait_send()


def write_out(*refs):
    count = (len(refs) - 1) // 2
    done = refs[-1]
    copies = [pltpu.make_async_copy(refs[i], refs[count + i], done.at[i]) for i in range(count)]
    for copy in copies:
        copy.start()
    for copy in copies:
        copy.wait()


def on_device(nb, nz, x, w, tv, tr, tc, cnt, go):
    offs, slots, side = tv.shape[1], tv.shape[2], tv.shape[-1]
    height, width = x.shape
    blocks = height // side
    depth, ow = w.shape
    factors = stage_factors(nb, depth)
    dims = (nb, nz, offs, slots, blocks, side, width, ow, tuple(factors))
    spare = max(nz // 2 - 1, 1)
    vmem = pl.BlockSpec(memory_space=pltpu.VMEM)
    hbm = pl.BlockSpec(memory_space=pltpu.HBM)
    dma = pltpu.SemaphoreType.DMA
    psems = []
    for f in factors:
        psems += [dma((1,))] * 4
    block = (side, ow)
    results = pl.pallas_call(
        functools.partial(layer_kernel, dims),
        out_shape=(
            pltpu.VMEM((height, ow), BF),
            pltpu.VMEM((height, width), BF),
            pltpu.VMEM((depth, ow), F32),
        ),
        in_specs=[hbm] * 7,
        out_specs=(vmem, vmem, vmem),
        scratch_shapes=[
            pltpu.SMEM((offs, 1, slots), tr.dtype),
            pltpu.SMEM((offs, 1, slots), tc.dtype),
            pltpu.SMEM(cnt.shape, cnt.dtype),
            pltpu.VMEM((height, nz * width), BF),
            pltpu.VMEM((depth, nz * ow), BF),
            pltpu.VMEM((offs, slots, side, side), BF),
            pltpu.VMEM((height, ow), BF),
            pltpu.VMEM((offs, slots, side, side), BF),
            pltpu.VMEM((offs, slots, *block), F32),
            pltpu.VMEM((blocks, *block), F32),
            pltpu.VMEM((blocks, *block), BF),
            pltpu.VMEM((offs, blocks, *block), BF),
            pltpu.VMEM((offs, blocks, *block), BF),
            pltpu.VMEM((height, nz * ow), BF),
            pltpu.VMEM((depth, ow), BF),
            pltpu.VMEM((spare, blocks, *block), BF),
            pltpu.VMEM((spare, blocks, side, width), BF),
        ]
        + [pltpu.VMEM((blocks, *block), BF)] * offs
        + [pltpu.VMEM((f - 1, depth // f, ow), BF) for f in factors]
        + [pltpu.VMEM((depth, ow), BF) for f in factors]
        + [dma((2,)), dma((blocks,)), dma((nz, 2)), dma((1,)), dma((spare,))]
        + [dma((offs,)), dma((2, blocks)), dma((offs,))]
        + [dma((offs,)), dma((2, blocks))]
        + [dma((2,)), dma((blocks,))]
        + [dma((spare,)), dma((spare,)), dma((1,))]
        + [dma((2, nz)), dma((nz, 2)), dma((1,)), dma((1,)), dma((7,))]
        + psems,
        compiler_params=pltpu.CompilerParams(
            collective_id=0, has_side_effects=True, vmem_limit_bytes=32 * 1024 * 1024
        ),
    )(*[pltpu.with_memory_space_constraint(a, pltpu.HBM) for a in (x, w, tv, jnp.swapaxes(tr, 0, 1), jnp.swapaxes(tc, 0, 1), cnt, go)])
    return pl.pallas_call(
        write_out,
        out_shape=tuple(jax.ShapeDtypeStruct(r.shape, r.dtype) for r in results),
        in_specs=[vmem] * len(results),
        out_specs=(hbm,) * len(results),
        scratch_shapes=[dma((len(results),))],
    )(*[pltpu.with_memory_space_constraint(r, pltpu.VMEM) for r in results])


def solution(mesh):
    return jax.shard_map(
        functools.partial(on_device, mesh.shape["blk"], mesh.shape["feat"]),
        mesh=mesh,
        in_specs=(
            P("blk", "feat"),
            P(None, "feat"),
            P("blk", None, None, None, None),
            P("blk", None, None),
            P("blk", None, None),
            P("blk", None),
            P("blk", "feat"),
        ),
        out_specs=(P("blk", "feat"), P("blk", "feat"), P(None, "feat")),
        check_vma=False,
    )
```

```python
import functools

import jax
import jax.numpy as jnp
from jax import lax
from jax.experimental import pallas as pl
from jax.experimental.pallas import tpu as pltpu
from jax.sharding import PartitionSpec as P

MESH = pl.DeviceIdType.MESH
BF = jnp.bfloat16
F32 = jnp.float32


def stage_factors(count, rows):
    factors = []
    while count > 1:
        size = max(f for f in range(2, 17) if count % f == 0 and rows % (16 * f) == 0)
        factors.append(size)
        count //= size
    return factors


def remote(src, dst, send, recv, where):
    return pltpu.make_async_remote_copy(
        src_ref=src, dst_ref=dst, send_sem=send, recv_sem=recv, device_id=where, device_id_type=MESH
    )


def layer_kernel(
    dims, x, w_in, tv_in, tr_in, tc_in, cnt_in, go_in, y, gx, gw,
    tr, tc, cnt, xg, wg, tv, go, tt, prod, acc, gp, sent, got, gg, gwb, pe, ge, *rest
):
    nb, nz, offs, slots, blocks, side, width, ow, factors = dims
    stages = len(factors)
    hid, rest = rest[:offs], rest[offs:]
    gathered, summed = rest[:stages], rest[stages : 2 * stages]
    (xs, xr, xb, hs, hr, hall, gs, gr, zs, zr, es, ges, ger, ws, wr, ks, kr, near) = rest[2 * stages : 2 * stages + 18]
    psems = rest[2 * stages + 18 :]
    reach = (offs - 1) // 2
    half = nz // 2
    me = lax.axis_index("feat")
    own = lax.axis_index("blk")
    core = lax.rem(own, 2)
    turn = 1 - 2 * core
    OWN, PAIR, CROSS, AHEAD, BEHIND = range(5)
    lean = (0, 1, -1, 2, -2)
    lower = me < half
    inner = jnp.where(lower, half - 1, half)
    other = nz - 1 - inner
    is_inner = me == inner
    ends = range(1, half)

    def end_at(j):
        return jnp.where(lower, half - 1 - j, half + j)

    def offset_of(role):
        return reach + lean[role] * turn

    def owner_at(role):
        return {"blk": lax.rem(own + lean[role] * turn + nb, nb)}

    def rows(b):
        return pl.ds(pl.multiple_of(b * side, side), side)

    def xcols(z):
        return pl.ds(pl.multiple_of(z * width, width), width)

    def ocols(z):
        return pl.ds(pl.multiple_of(z * ow, ow), ow)

    local = [
        pltpu.make_async_copy(w_in, wg.at[:, ocols(me)], near.at[0]),
        pltpu.make_async_copy(x, xg.at[:, xcols(me)], near.at[1]),
        pltpu.make_async_copy(tv_in.at[0], tv, near.at[2]),
        pltpu.make_async_copy(go_in, go, near.at[3]),
        pltpu.make_async_copy(tr_in, tr, near.at[4]),
        pltpu.make_async_copy(tc_in, tc, near.at[5]),
        pltpu.make_async_copy(cnt_in, cnt, near.at[6]),
    ]
    for copy in local:
        copy.start()

    def stage_peer(stage, step):
        stride = 1
        for f in factors[:stage]:
            stride *= f
        size = factors[stage]
        digit = lax.rem(own // stride, size)
        there = lax.rem(digit + step, size)
        return digit, there, own + (there - digit) * stride

    barrier = pltpu.get_barrier_semaphore()
    greeted = 0
    for step in range(1, nz):
        pl.semaphore_signal(barrier, inc=1, device_id={"feat": lax.rem(me + step, nz)}, device_id_type=MESH)
        greeted += 1
    for role in (PAIR, AHEAD, BEHIND) if stages > 1 else ():
        pl.semaphore_signal(barrier, inc=1, device_id=owner_at(role), device_id_type=MESH)
        greeted += 1
    for stage in range(stages):
        for step in range(1, factors[stage]):
            _, _, peer = stage_peer(stage, step)
            pl.semaphore_signal(barrier, inc=1, device_id={"blk": peer}, device_id_type=MESH)
            greeted += 1
    pl.semaphore_wait(barrier, greeted)

    depth = w_in.shape[0]

    def part_of(piece):
        return pl.ds(pl.multiple_of(piece * (depth // 2), depth // 2), depth // 2)

    def x_copy(way, b):
        return remote(
            x.at[rows(b), :], xg.at[rows(b), xcols(me)], xs.at[way], xr.at[b], {"feat": (inner, other)[way]}
        )

    def x_back(s, e, j, b):
        piece = xg.at[rows(b), xcols(s)]
        return remote(piece, piece, xb.at[j - 1], xr.at[b], {"feat": e})

    def x_wait(b):
        piece = xg.at[rows(b), pl.ds(0, (nz - 1) * width)]
        remote(piece, piece, xs.at[0], xr.at[b], {"feat": other}).wait_recv()

    def w_up():
        return remote(w_in.at[part_of(core), :], wg.at[part_of(core), ocols(me)], ws.at[0, 0], wr.at[me, core], {"feat": inner})

    def w_across(e):
        piece = wg.at[part_of(core), ocols(e)]
        return remote(piece, piece, ws.at[1, e], wr.at[e, core], owner_at(PAIR))

    def w_wait(e, piece):
        ref = wg.at[part_of(piece), ocols(e)]
        remote(ref, ref, ws.at[1, e], wr.at[e, piece], owner_at(PAIR)).wait_recv()

    def w_swap(sending):
        there = jnp.where(lower, half, 0)
        here = half - there
        r, c = (there, here) if sending else (here, there)
        piece = wg.at[
            pl.ds(pl.multiple_of(r * width, width), half * width), pl.ds(pl.multiple_of(c * ow, ow), half * ow)
        ]
        return remote(piece, piece, ks.at[0], kr.at[0], {"feat": other})

    @pl.when(is_inner)
    def _():
        for b in range(min(4, blocks)):
            x_copy(1, b).start()

    @pl.when(jnp.logical_not(is_inner))
    def _():
        for b in range(blocks):
            x_copy(1, b).start()
            x_copy(0, b).start()
            if b == 0:
                w_up().start()

    for copy in local[:3]:
        copy.wait()

    landing = {PAIR: PAIR, AHEAD: BEHIND, BEHIND: AHEAD}

    def hid_copy(role, b):
        landed = hr.at[0, b] if role == BEHIND else hall.at[landing[role]]
        return remote(hid[OWN].at[b], hid[landing[role]].at[b], hs.at[role], landed, owner_at(role))

    def hid_wait(role, b):
        remote(hid[role].at[b], hid[role].at[b], hs.at[role], hr.at[int(role == OWN), b], owner_at(PAIR)).wait_recv()

    def hid_whole(role):
        remote(hid[role], hid[role], hs.at[role], hall.at[role], owner_at(PAIR)).wait_recv()

    def hid_passed(b):
        return remote(hid[AHEAD].at[b], hid[CROSS].at[b], hs.at[CROSS], hall.at[CROSS], owner_at(PAIR))

    def hid_relay(b):
        hid_wait(AHEAD, b)
        hid_passed(b).start()

    def hid_down(j, b):
        return remote(pe.at[j - 1, b], hid[OWN].at[b], es.at[j - 1], hr.at[1, b], {"feat": end_at(j)})

    def spread(b):
        hid_copy(PAIR, b).start()
        hid_copy(AHEAD, b).start()
        hid_copy(BEHIND, b).start()

    def hidden_of(z, b):
        return jnp.dot(xg[rows(b), :], wg[:, ocols(z)], preferred_element_type=F32).astype(BF)

    def serve_ends(b):
        for j in ends:
            pe[j - 1, b] = hidden_of(end_at(j), b)
            hid_down(j, b).start()
            x_back(me, end_at(j), j, b).start()

    lag = 4

    def forward_step(b, carry):
        @pl.when(is_inner)
        def _():
            @pl.when(b + 4 < blocks)
            def _():
                x_copy(1, b + 4).start()

        per_block = slots // blocks
        for role in range(offs):
            for s in range(per_block):
                slot = b * per_block + s
                tt[role, slot] = tv[offset_of(role), slot].T

        @pl.when(is_inner)
        def _():
            x_wait(b)

            @pl.when(b >= 1)
            def _():
                serve_ends(b)

            hid[OWN][b] = hidden_of(me, b)
            spread(b)

            @pl.when(b == 0)
            def _():
                for j in ends:
                    w_wait(end_at(j), core)
                    w_across(end_at(j)).start()
                for j in ends:
                    w_wait(end_at(j), 1 - core)
                serve_ends(0)

        @pl.when(jnp.logical_not(is_inner))
        def _():
            hid_wait(OWN, b)
            spread(b)

        @pl.when(b >= lag)
        def _():
            hid_relay(b - lag)

        return carry

    lax.fori_loop(0, blocks, forward_step, 0)
    for copy in local[4:]:
        copy.wait()

    def forward_products(role):
        k = offset_of(role)
        for s in range(slots):
            prod[role, s] = jnp.dot(tv[k, s], hid[role][tc[k, 0, s]], preferred_element_type=F32)

    def weight_of(table, k, s, b):
        return jnp.where((table[k, 0, s] == b) & (s < cnt[0, k]), 1.0, 0.0).astype(F32)

    def row_sum(role, b, total):
        for s in range(slots):
            total = total + prod[role, s] * weight_of(tr, offset_of(role), s, b)
        return total

    def gather_role(role):
        forward_products(role)

        def add(b, carry):
            start = hid[OWN][b].astype(F32) if role == OWN else acc[b]
            acc[b] = row_sum(role, b, start)
            return carry

        lax.fori_loop(0, blocks, add, 0)

    gather_role(OWN)
    hid_whole(PAIR)
    gather_role(PAIR)
    for b in range(max(blocks - lag, 0), blocks):
        hid_relay(b)

    @pl.when(is_inner)
    def _():
        w_swap(True).start()
        for j in ends:
            for b in range(blocks):
                for step in range(1, nz):
                    s = lax.rem(me + step, nz)

                    @pl.when(s != end_at(j))
                    def _():
                        x_back(s, end_at(j), j, b).start()

    gather_role(AHEAD)
    hid_whole(BEHIND)
    gather_role(BEHIND)
    local[3].wait()
    hid_whole(CROSS)
    forward_products(CROSS)

    def pointwise(b, carry):
        v = row_sum(CROSS, b, acc[b])
        sigma = jax.nn.sigmoid(v)
        y[rows(b), :] = (v * sigma).astype(BF)
        slope = sigma * (1.0 + v * (1.0 - sigma))
        gp[b] = (go[rows(b), :].astype(F32) * slope).astype(BF)
        return carry

    lax.fori_loop(0, blocks, pointwise, 0)

    def backward_products(role):
        for s in range(slots):
            prod[role, s] = jnp.dot(tt[role, s], gp[tr[offset_of(role), 0, s]], preferred_element_type=F32)

    def column_sum(role, c, start):
        total = start
        for s in range(slots):
            term = prod[role, s] * weight_of(tc, offset_of(role), s, c)
            total = term if total is None else total + term
        return total

    target = {PAIR: PAIR, CROSS: PAIR, AHEAD: AHEAD, BEHIND: BEHIND}
    arrives = {PAIR: PAIR, CROSS: CROSS, AHEAD: BEHIND, BEHIND: AHEAD}

    def sum_copy(role, c):
        return remote(
            sent.at[role, c], got.at[arrives[role], c], gs.at[role], gr.at[int(role == CROSS), c], owner_at(target[role])
        )

    def cross_wait(c):
        piece = got.at[CROSS, c]
        remote(piece, piece, gs.at[CROSS], gr.at[1, c], owner_at(PAIR)).wait_recv()

    def sums_wait(c):
        piece = got.at[pl.ds(0, 3), c]
        remote(piece, piece, gs.at[PAIR], gr.at[0, c], owner_at(PAIR)).wait_recv()

    def send_sum(role, c):
        sent[role, c] = column_sum(role, c, None).astype(BF)
        sum_copy(role, c).start()

    def send_joint(c):
        cross_wait(c)
        sent[AHEAD, c] = column_sum(AHEAD, c, got[CROSS, c].astype(F32)).astype(BF)
        sum_copy(AHEAD, c).start()

    def loop(step):
        def body(c, carry):
            step(c)
            return carry

        lax.fori_loop(0, blocks, body, 0)

    backward_products(CROSS)
    loop(lambda c: send_sum(CROSS, c))
    backward_products(BEHIND)
    backward_products(AHEAD)

    def send_far(c):
        send_sum(BEHIND, c)
        send_joint(c)

    loop(send_far)
    backward_products(PAIR)
    loop(lambda c: send_sum(PAIR, c))
    backward_products(OWN)

    gw[...] = jnp.zeros_like(gw)

    def g_copy(way, b):
        piece = gg.at[rows(b), ocols(me)]
        return remote(piece, piece, zs.at[way], zr.at[b], {"feat": (inner, other)[way]})

    def g_wait(b):
        piece = gg.at[rows(b), pl.ds(0, (nz - 1) * ow)]
        remote(piece, piece, zs.at[0], zr.at[b], {"feat": other}).wait_recv()

    def make_grad(b):
        total = column_sum(OWN, b, gp[b].astype(F32))
        sums_wait(b)
        for role in (PAIR, BEHIND, AHEAD):
            total = total + got[role, b].astype(F32)
        grad = total.astype(BF)
        gg[rows(b), ocols(me)] = grad
        g_copy(1, b).start()

        @pl.when(jnp.logical_not(is_inner))
        def _():
            g_copy(0, b).start()
            x_wait(b)

        gw[...] += lax.dot_general(xg[rows(b), :], grad, (((0,), (0,)), ((), ())), preferred_element_type=F32)

    def gx_down(j, b):
        return remote(ge.at[j - 1, b], gx.at[rows(b), :], ges.at[j - 1], ger.at[0], {"feat": end_at(j)})

    def finish(b):
        @pl.when(is_inner)
        def _():
            @pl.when(b == 0)
            def _():
                w_swap(False).wait_recv()

            g_wait(b)

            def grad_of(z):
                return lax.dot_general(
                    gg[rows(b), :], wg[xcols(z), :], (((1,), (1,)), ((), ())), preferred_element_type=F32
                ).astype(BF)

            for j in ends:
                ge[j - 1, b] = grad_of(end_at(j))
                gx_down(j, b).start()
            gx[rows(b), :] = grad_of(me)

    loop(make_grad)
    gwb[...] = gw[...].astype(BF)
    height = gw.shape[0]
    for stage in range(stages):
        size = factors[stage]
        chunk = height // size
        src, buf, out = gwb if stage == 0 else summed[stage - 1], gathered[stage], summed[stage]
        rs_s, rs_r, ag_s, ag_r = psems[4 * stage : 4 * stage + 4]

        def part(q):
            return pl.ds(pl.multiple_of(q * chunk, chunk), chunk)

        for step in range(1, size):
            _, there, peer = stage_peer(stage, step)
            remote(src.at[part(there), :], buf.at[step - 1], rs_s.at[0], rs_r.at[0], {"blk": peer}).start()
        if stage == 0:
            for b in range(blocks - 2):
                finish(b)
        digit, _, _ = stage_peer(stage, 1)
        if stage == 0:
            total = gw[part(digit), :]
        else:
            total = src[part(digit), :].astype(F32)
        remote(buf, buf, rs_s.at[0], rs_r.at[0], owner_at(PAIR)).wait_recv()
        for step in range(1, size):
            total = total + buf[step - 1].astype(F32)
        out[part(digit), :] = total.astype(BF)
        for step in range(1, size):
            _, _, peer = stage_peer(stage, step)
            piece = out.at[part(digit), :]
            remote(piece, piece, ag_s.at[0], ag_r.at[0], {"blk": peer}).start()
        if stage == 0:
            for b in range(max(blocks - 2, 0), blocks):
                finish(b)
        piece = out.at[pl.ds(0, height - chunk), :]
        remote(piece, piece, ag_s.at[0], ag_r.at[0], owner_at(PAIR)).wait_recv()
    gw[...] = (summed[-1] if stages else gwb)[...].astype(F32)

    for stage in range(stages):
        buf, out = gathered[stage], summed[stage]
        rs_s, rs_r, ag_s, ag_r = psems[4 * stage : 4 * stage + 4]
        remote(buf, buf, rs_s.at[0], rs_r.at[0], owner_at(PAIR)).wait_send()
        piece = out.at[pl.ds(0, height - height // factors[stage]), :]
        remote(piece, piece, ag_s.at[0], ag_r.at[0], owner_at(PAIR)).wait_send()

    def sent_all(ref, sem):
        remote(ref, ref, sem, ger.at[0], owner_at(PAIR)).wait_send()

    sent_all(gg.at[:, ocols(me)], zs.at[1])

    @pl.when(is_inner)
    def _():
        sent_all(x, xs.at[1])
        for j in ends:
            sent_all(pe.at[j - 1], es.at[j - 1])
            sent_all(ge.at[j - 1], ges.at[j - 1])
            sent_all(xg.at[:, pl.ds(0, (nz - 1) * width)], xb.at[j - 1])

    @pl.when(jnp.logical_not(is_inner))
    def _():
        sent_all(x, xs.at[1])
        sent_all(x, xs.at[0])
        sent_all(gg.at[:, ocols(me)], zs.at[0])
        remote(gx, gx, ges.at[0], ger.at[0], {"feat": inner}).wait_recv()

    for role in (PAIR, CROSS, AHEAD, BEHIND):
        sent_all(hid[role], hs.at[role])
        sent_all(sent.at[role], gs.at[role])

    @pl.when(is_inner)
    def _():
        w_swap(True).wait_send()
        for j in ends:
            w_across(end_at(j)).wait_send()

    @pl.when(jnp.logical_not(is_inner))
    def _():
        w_up().wait_send()


def write_out(*refs):
    count = (len(refs) - 1) // 2
    done = refs[-1]
    copies = [pltpu.make_async_copy(refs[i], refs[count + i], done.at[i]) for i in range(count)]
    for copy in copies:
        copy.start()
    for copy in copies:
        copy.wait()


def on_device(nb, nz, x, w, tv, tr, tc, cnt, go):
    offs, slots, side = tv.shape[1], tv.shape[2], tv.shape[-1]
    height, width = x.shape
    blocks = height // side
    depth, ow = w.shape
    factors = stage_factors(nb, depth)
    dims = (nb, nz, offs, slots, blocks, side, width, ow, tuple(factors))
    spare = max(nz // 2 - 1, 1)
    vmem = pl.BlockSpec(memory_space=pltpu.VMEM)
    hbm = pl.BlockSpec(memory_space=pltpu.HBM)
    dma = pltpu.SemaphoreType.DMA
    psems = []
    for f in factors:
        psems += [dma((1,))] * 4
    block = (side, ow)
    results = pl.pallas_call(
        functools.partial(layer_kernel, dims),
        out_shape=(
            pltpu.VMEM((height, ow), BF),
            pltpu.VMEM((height, width), BF),
            pltpu.VMEM((depth, ow), F32),
        ),
        in_specs=[hbm] * 7,
        out_specs=(vmem, vmem, vmem),
        scratch_shapes=[
            pltpu.SMEM((offs, 1, slots), tr.dtype),
            pltpu.SMEM((offs, 1, slots), tc.dtype),
            pltpu.SMEM(cnt.shape, cnt.dtype),
            pltpu.VMEM((height, nz * width), BF),
            pltpu.VMEM((depth, nz * ow), BF),
            pltpu.VMEM((offs, slots, side, side), BF),
            pltpu.VMEM((height, ow), BF),
            pltpu.VMEM((offs, slots, side, side), BF),
            pltpu.VMEM((offs, slots, *block), F32),
            pltpu.VMEM((blocks, *block), F32),
            pltpu.VMEM((blocks, *block), BF),
            pltpu.VMEM((offs, blocks, *block), BF),
            pltpu.VMEM((offs, blocks, *block), BF),
            pltpu.VMEM((height, nz * ow), BF),
            pltpu.VMEM((depth, ow), BF),
            pltpu.VMEM((spare, blocks, *block), BF),
            pltpu.VMEM((spare, blocks, side, width), BF),
        ]
        + [pltpu.VMEM((blocks, *block), BF)] * offs
        + [pltpu.VMEM((f - 1, depth // f, ow), BF) for f in factors]
        + [pltpu.VMEM((depth, ow), BF) for f in factors]
        + [dma((2,)), dma((blocks,)), dma((spare,))]
        + [dma((offs,)), dma((2, blocks)), dma((offs,))]
        + [dma((offs,)), dma((2, blocks))]
        + [dma((2,)), dma((blocks,))]
        + [dma((spare,)), dma((spare,)), dma((1,))]
        + [dma((2, nz)), dma((nz, 2)), dma((1,)), dma((1,)), dma((7,))]
        + psems,
        compiler_params=pltpu.CompilerParams(
            collective_id=0, has_side_effects=True, vmem_limit_bytes=32 * 1024 * 1024
        ),
    )(*[pltpu.with_memory_space_constraint(a, pltpu.HBM) for a in (x, w, tv, jnp.swapaxes(tr, 0, 1), jnp.swapaxes(tc, 0, 1), cnt, go)])
    return pl.pallas_call(
        write_out,
        out_shape=tuple(jax.ShapeDtypeStruct(r.shape, r.dtype) for r in results),
        in_specs=[vmem] * len(results),
        out_specs=(hbm,) * len(results),
        scratch_shapes=[dma((len(results),))],
    )(*[pltpu.with_memory_space_constraint(r, pltpu.VMEM) for r in results])


def solution(mesh):
    return jax.shard_map(
        functools.partial(on_device, mesh.shape["blk"], mesh.shape["feat"]),
        mesh=mesh,
        in_specs=(
            P("blk", "feat"),
            P(None, "feat"),
            P("blk", None, None, None, None),
            P("blk", None, None),
            P("blk", None, None),
            P("blk", None),
            P("blk", "feat"),
        ),
        out_specs=(P("blk", "feat"), P("blk", "feat"), P(None, "feat")),
        check_vma=False,
    )
```

```python
import functools

import jax
import jax.numpy as jnp
from jax import lax
from jax.experimental import pallas as pl
from jax.experimental.pallas import tpu as pltpu
from jax.sharding import PartitionSpec as P

MESH = pl.DeviceIdType.MESH
BF = jnp.bfloat16
F32 = jnp.float32


def stage_factors(count, rows):
    factors = []
    while count > 1:
        size = max(f for f in range(2, 17) if count % f == 0 and rows % (16 * f) == 0)
        factors.append(size)
        count //= size
    return factors


def remote(src, dst, send, recv, where):
    return pltpu.make_async_remote_copy(
        src_ref=src, dst_ref=dst, send_sem=send, recv_sem=recv, device_id=where, device_id_type=MESH
    )


def layer_kernel(
    dims, x, w_in, tv_in, tr_in, tc_in, cnt_in, go_in, y, gx, gw,
    tr, tc, cnt, xg, wg, tv, go, tt, prod, acc, gp, sent, got, gg, gwb, pe, ge, wt, *rest
):
    nb, nz, offs, slots, blocks, side, width, ow, factors = dims
    stages = len(factors)
    hid, hid_far, rest = rest[:3], rest[3], rest[4:]
    gathered, summed = rest[:stages], rest[stages : 2 * stages]
    (xs, xr, xb, hs, hr, hf, hall, gs, gr, zs, zr, zl, ze, es, ges, ger, ws, wr, ks, kr, near) = rest[2 * stages : 2 * stages + 21]
    psems = rest[2 * stages + 21 :]
    reach = (offs - 1) // 2
    half = nz // 2
    me = lax.axis_index("feat")
    own = lax.axis_index("blk")
    core = lax.rem(own, 2)
    turn = 1 - 2 * core
    OWN, PAIR, CROSS, AHEAD, BEHIND = range(5)
    lean = (0, 1, -1, 2, -2)
    lower = me < half
    inner = jnp.where(lower, half - 1, half)
    other = nz - 1 - inner
    is_inner = me == inner
    ends = range(1, half)
    mine = jnp.where(lower, half - 1 - me, me - half)
    straight = min(3, blocks)
    passed = blocks // 2
    wound = blocks // 2

    def end_at(j):
        return jnp.where(lower, half - 1 - j, half + j)

    def offset_of(role):
        return reach + lean[role] * turn

    def owner_at(role):
        return {"blk": lax.rem(own + lean[role] * turn + nb, nb)}

    chip = own // 2
    ahead_near = lax.rem(chip + own, 2) == 0
    near_role = jnp.where(ahead_near, AHEAD, BEHIND)
    far_role = AHEAD + BEHIND - near_role
    near_lean = jnp.where(ahead_near, lean[AHEAD], lean[BEHIND]) * turn
    near_owner = {"blk": lax.rem(own + near_lean + nb, nb)}
    skip = 2 * lean[AHEAD] * (2 * lax.rem(chip, 2) - 1)
    side_owner = {"blk": lax.rem(own + skip + nb, nb)}
    side_source = {"blk": lax.rem(own - skip + nb, nb)}

    def rows(b):
        return pl.ds(pl.multiple_of(b * side, side), side)

    def xcols(z):
        return pl.ds(pl.multiple_of(z * width, width), width)

    def ocols(z):
        return pl.ds(pl.multiple_of(z * ow, ow), ow)

    local = [
        pltpu.make_async_copy(w_in, wg.at[:, ocols(me)], near.at[0]),
        pltpu.make_async_copy(x, xg.at[:, xcols(me)], near.at[1]),
        pltpu.make_async_copy(tv_in.at[0], tv, near.at[2]),
        pltpu.make_async_copy(go_in, go, near.at[3]),
        pltpu.make_async_copy(tr_in, tr, near.at[4]),
        pltpu.make_async_copy(tc_in, tc, near.at[5]),
        pltpu.make_async_copy(cnt_in, cnt, near.at[6]),
    ]
    for copy in local:
        copy.start()

    def stage_peer(stage, step):
        stride = 1
        for f in factors[:stage]:
            stride *= f
        size = factors[stage]
        digit = lax.rem(own // stride, size)
        there = lax.rem(digit + step, size)
        return digit, there, own + (there - digit) * stride

    barrier = pltpu.get_barrier_semaphore()
    greeted = 0
    for step in range(1, nz):
        pl.semaphore_signal(barrier, inc=1, device_id={"feat": lax.rem(me + step, nz)}, device_id_type=MESH)
        greeted += 1
    around = [owner_at(PAIR), owner_at(AHEAD), owner_at(BEHIND), side_owner, side_source]
    for peer in around if stages > 1 else ():
        pl.semaphore_signal(barrier, inc=1, device_id=peer, device_id_type=MESH)
        greeted += 1
    for stage in range(stages):
        for step in range(1, factors[stage]):
            _, _, peer = stage_peer(stage, step)
            pl.semaphore_signal(barrier, inc=1, device_id={"blk": peer}, device_id_type=MESH)
            greeted += 1
    pl.semaphore_wait(barrier, greeted)

    depth = w_in.shape[0]

    group = factors[0] if stages else 1

    def part_of(digit):
        return pl.ds(pl.multiple_of(digit * (depth // group), depth // group), depth // group)

    my_part = part_of(stage_peer(0, 0)[0] if stages else 0)

    def x_copy(way, b):
        return remote(
            x.at[rows(b), :], xg.at[rows(b), xcols(me)], xs.at[way], xr.at[b], {"feat": (inner, other)[way]}
        )

    def x_back(s, e, j, b):
        piece = xg.at[rows(b), xcols(s)]
        return remote(piece, piece, xb.at[j - 1], xr.at[b], {"feat": e})

    def x_wait(b):
        piece = xg.at[rows(b), pl.ds(0, (nz - 1) * width)]
        remote(piece, piece, xs.at[0], xr.at[b], {"feat": other}).wait_recv()

    def w_up():
        return remote(w_in.at[my_part, :], wg.at[my_part, ocols(me)], ws.at[0], wr.at[mine - 1, 0], {"feat": inner})

    def w_around(j):
        piece = wg.at[my_part, ocols(end_at(j))]
        remote(piece, piece, ws.at[j], wr.at[j - 1, 0], owner_at(PAIR)).wait_recv()
        for step in range(1, group):
            peer = {"blk": stage_peer(0, step)[2]}
            remote(piece, piece, ws.at[j], wr.at[j - 1, 1], peer).start()

    def w_rest(j):
        return wg.at[pl.ds(0, depth - depth // group), ocols(end_at(j))]

    def w_wait(j):
        if group > 1:
            remote(w_rest(j), w_rest(j), ws.at[j], wr.at[j - 1, 1], owner_at(PAIR)).wait_recv()

    def w_swap(sending):
        there = jnp.where(lower, half, 0)
        here = half - there
        r, c = (there, here) if sending else (here, there)
        piece = wg.at[
            pl.ds(pl.multiple_of(r * width, width), half * width), pl.ds(pl.multiple_of(c * ow, ow), half * ow)
        ]
        return remote(piece, piece, ks.at[0], kr.at[0], {"feat": other})

    @pl.when(is_inner)
    def _():
        for b in range(min(6, blocks)):
            x_copy(1, b).start()

    @pl.when(jnp.logical_not(is_inner))
    def _():
        for b in range(blocks):
            x_copy(1, b).start()
            if b == 0 and half > 1:
                w_up().start()
            x_copy(0, b).start()

    for copy in local[:3]:
        copy.wait()

    near_slot = jnp.where(ahead_near, 0, 1)
    far_slot = 1 - near_slot

    def hid_pair(b):
        return remote(hid[OWN].at[b], hid[PAIR].at[b], hs.at[PAIR], hall.at[PAIR], owner_at(PAIR))

    def hid_straight(role, b):
        slot = int(role == AHEAD)
        return remote(hid[OWN].at[b], hid_far.at[slot, b], hs.at[role], hf.at[slot, b], owner_at(role))

    def hid_near(b):
        return remote(hid[OWN].at[b], hid_far.at[far_slot, b], hs.at[OWN], hf.at[far_slot, b], near_owner)

    def hid_side(b):
        return remote(
            hid_far.at[near_slot, b], hid_far.at[far_slot, b], hs.at[offs], hf.at[far_slot, b], side_source
        )

    def hid_passed(b):
        return remote(hid_far.at[0, b], hid[CROSS].at[b], hs.at[CROSS], hall.at[CROSS], owner_at(PAIR))

    def hid_landed(slot, b):
        piece = hid_far.at[slot, b]
        remote(piece, piece, hs.at[OWN], hf.at[slot, b], owner_at(PAIR)).wait_recv()

    def hid_whole(role):
        remote(hid[role], hid[role], hs.at[role], hall.at[role], owner_at(PAIR)).wait_recv()

    def take_near(b):
        hid_landed(near_slot, b)

        @pl.when(b < wound)
        def _():
            hid_side(b).start()

        @pl.when(ahead_near)
        def _():
            hid_passed(b).start()

    def take_far(b):
        hid_landed(far_slot, b)

        @pl.when(jnp.logical_not(ahead_near))
        def _():
            hid_passed(b).start()

    def hid_down(j, b):
        return remote(pe.at[j - 1, b], hid[OWN].at[b], es.at[j - 1], hr.at[b], {"feat": end_at(j)})

    def spread(b):
        hid_pair(b).start()

        @pl.when(b < wound)
        def _():
            hid_near(b).start()

        @pl.when(b >= wound)
        def _():
            hid_straight(AHEAD, b).start()
            hid_straight(BEHIND, b).start()

    def hidden_of(z, b):
        return jnp.dot(xg[rows(b), :], wg[:, ocols(z)], preferred_element_type=F32).astype(BF)

    def serve_ends(b):
        for j in ends:
            pe[j - 1, b] = hidden_of(end_at(j), b)
            hid_down(j, b).start()

    lag = min(3, blocks)
    first = min(2, blocks - 1)

    def forward_step(b, carry):
        @pl.when(is_inner)
        def _():
            @pl.when(b + 6 < blocks)
            def _():
                x_copy(1, b + 6).start()

        per_block = slots // blocks
        for role in range(offs):
            for s in range(per_block):
                slot = b * per_block + s
                tt[role, slot] = tv[offset_of(role), slot].T

        @pl.when(is_inner)
        def _():
            x_wait(b)

            @pl.when(b > first)
            def _():
                serve_ends(b)

            hid[OWN][b] = hidden_of(me, b)
            spread(b)

            @pl.when(b == first)
            def _():
                for j in ends:
                    w_wait(j)
                for early in range(first + 1):
                    serve_ends(early)

        @pl.when(jnp.logical_not(is_inner))
        def _():
            remote(hid[OWN].at[b], hid[OWN].at[b], es.at[0], hr.at[b], {"feat": inner}).wait_recv()
            spread(b)

        @pl.when(b >= lag)
        def _():
            take_near(b - lag)

        return carry

    @pl.when(is_inner)
    def _():
        for j in ends:
            w_around(j)

    lax.fori_loop(0, blocks, forward_step, 0)

    @pl.when(is_inner)
    def _():
        w_swap(True).start()
        for j in ends:
            for b in range(blocks):
                for step in range(nz):
                    s = lax.rem(me + step, nz)

                    @pl.when(s != end_at(j))
                    def _():
                        x_back(s, end_at(j), j, b).start()

    for copy in local[4:]:
        copy.wait()

    def forward_products(role):
        k = offset_of(role)
        for s in range(slots):
            c = tc[k, 0, s]
            source = hid[role][c] if role < AHEAD else hid_far[role - AHEAD, c]
            prod[role, s] = jnp.dot(tv[k, s], source, preferred_element_type=F32)

    def weight_of(table, k, s, b):
        return jnp.where((table[k, 0, s] == b) & (s < cnt[0, k]), 1.0, 0.0).astype(F32)

    def row_sum(role, b, total):
        for s in range(slots):
            total = total + prod[role, s] * weight_of(tr, offset_of(role), s, b)
        return total

    def gather_role(role):
        forward_products(role)

        def add(b, carry):
            start = hid[OWN][b].astype(F32) if role == OWN else acc[b]
            acc[b] = row_sum(role, b, start)
            return carry

        lax.fori_loop(0, blocks, add, 0)

    gather_role(OWN)
    hid_whole(PAIR)
    gather_role(PAIR)
    for b in range(max(blocks - lag, 0), blocks):
        take_near(b)
    for b in range(blocks):
        take_far(b)

    gather_role(AHEAD)
    gather_role(BEHIND)
    local[3].wait()
    hid_whole(CROSS)
    forward_products(CROSS)

    def pointwise(b, carry):
        v = row_sum(CROSS, b, acc[b])
        sigma = jax.nn.sigmoid(v)
        y[rows(b), :] = (v * sigma).astype(BF)
        slope = sigma * (1.0 + v * (1.0 - sigma))
        gp[b] = (go[rows(b), :].astype(F32) * slope).astype(BF)
        return carry

    lax.fori_loop(0, blocks, pointwise, 0)

    def backward_products(role):
        for s in range(slots):
            prod[role, s] = jnp.dot(tt[role, s], gp[tr[offset_of(role), 0, s]], preferred_element_type=F32)

    def column_sum(role, offset, c, start):
        total = start
        for s in range(slots):
            term = prod[role, s] * weight_of(tc, offset, s, c)
            total = term if total is None else total + term
        return total

    target = {PAIR: PAIR, CROSS: PAIR, AHEAD: AHEAD, BEHIND: BEHIND}
    arrives = {PAIR: PAIR, CROSS: CROSS, AHEAD: BEHIND, BEHIND: AHEAD}

    def sum_copy(role, c):
        return remote(
            sent.at[role, c], got.at[arrives[role], c], gs.at[role], gr.at[int(role == CROSS), c], owner_at(target[role])
        )

    def cross_wait(c):
        piece = got.at[CROSS, c]
        remote(piece, piece, gs.at[CROSS], gr.at[1, c], owner_at(PAIR)).wait_recv()

    def send_sum(role, c):
        sent[role, c] = column_sum(role, offset_of(role), c, None).astype(BF)
        sum_copy(role, c).start()

    def send_joint(c):
        cross_wait(c)
        start = got[CROSS, c].astype(F32)
        sent[AHEAD, c] = column_sum(AHEAD, offset_of(AHEAD), c, start).astype(BF)
        sum_copy(AHEAD, c).start()

    crossing_near = jnp.where(ahead_near, 1.0, 0.0).astype(F32)

    def send_side(c):
        cross_wait(c)
        start = got[CROSS, c].astype(F32) * (1.0 - crossing_near)
        sent[far_role, c] = column_sum(far_role, reach - near_lean, c, start).astype(BF)
        remote(sent.at[far_role, c], got.at[OWN, c], gs.at[OWN], gr.at[2, c], side_owner).start()

    def send_near(c):
        start = got[CROSS, c].astype(F32) * crossing_near
        total = column_sum(near_role, reach + near_lean, c, start)
        piece = got.at[OWN, c]
        remote(piece, piece, gs.at[OWN], gr.at[2, c], side_owner).wait_recv()
        sent[near_role, c] = (total + got[OWN, c].astype(F32)).astype(BF)
        remote(sent.at[near_role, c], got.at[AHEAD, c], gs.at[offs], gr.at[0, c], near_owner).start()

    def loop(low, high, step):
        def body(c, carry):
            step(c)
            return carry

        lax.fori_loop(low, high, body, 0)

    backward_products(CROSS)
    loop(0, blocks, lambda c: send_sum(CROSS, c))
    backward_products(BEHIND)
    for c in range(straight):
        send_sum(BEHIND, c)
    backward_products(AHEAD)
    for c in range(straight):
        send_joint(c)
    loop(straight, blocks, send_side)
    backward_products(PAIR)
    loop(0, blocks, lambda c: send_sum(PAIR, c))
    backward_products(OWN)

    gw[...] = jnp.zeros_like(gw)

    def g_copy(way, b, landed):
        piece = gg.at[rows(b), ocols(me)]
        return remote(piece, piece, zs.at[way], landed, {"feat": (inner, other)[way]})

    def g_wait(b):
        piece = gg.at[rows(b), pl.ds(0, (half if b < passed else nz - 1) * ow)]
        remote(piece, piece, zs.at[0], zr.at[b], {"feat": other}).wait_recv()

    def g_pass(b):
        for j in ends:
            piece = gg.at[rows(b), ocols(end_at(j))]
            remote(piece, piece, zl.at[0], ze.at[j - 1, b], {"feat": other}).wait_recv()
            remote(piece, piece, zl.at[0], zr.at[b], {"feat": other}).start()

    def make_grad(b, two):
        pieces = got.at[pl.ds(0, 3 if two else 2), b]
        total = column_sum(OWN, reach, b, gp[b].astype(F32))
        remote(pieces, pieces, gs.at[PAIR], gr.at[0, b], owner_at(PAIR)).wait_recv()
        for role in (PAIR, AHEAD, BEHIND)[: 3 if two else 2]:
            total = total + got[role, b].astype(F32)
        grad = total.astype(BF)
        gg[rows(b), ocols(me)] = grad

        @pl.when(is_inner)
        def _():
            g_copy(1, b, zr.at[b]).start()

        if half > 1:
            @pl.when(jnp.logical_not(is_inner))
            def _():
                @pl.when(b < passed)
                def _():
                    g_copy(0, b, ze.at[mine - 1, b]).start()

                @pl.when(b >= passed)
                def _():
                    g_copy(1, b, zr.at[b]).start()
                    g_copy(0, b, zr.at[b]).start()

                x_wait(b)

        gw[...] += lax.dot_general(xg[rows(b), :], grad, (((0,), (0,)), ((), ())), preferred_element_type=F32)

    def gx_down(j, b):
        return remote(ge.at[j - 1, b], gx.at[rows(b), :], ges.at[j - 1], ger.at[0], {"feat": end_at(j)})

    def turn_weight():
        w_swap(False).wait_recv()
        for j in range(half):
            wt[:, pl.ds(j * width, width)] = wg[xcols(end_at(j)), :].T

    def finish(b):
        @pl.when(is_inner)
        def _():
            g_wait(b)
            grads = jnp.dot(gg[rows(b), :], wt[...], preferred_element_type=F32).astype(BF)
            for j in ends:
                ge[j - 1, b] = grads[:, j * width : (j + 1) * width]
                gx_down(j, b).start()
            gx[rows(b), :] = grads[:, :width]

    def backward_step(c):
        @pl.when(c + straight + 1 < blocks)
        def _():
            send_near(c + straight + 1)

        make_grad(c, False)

    for c in range(straight):
        make_grad(c, True)
        for ahead in ((straight, straight + 1) if c == 0 else (c + straight + 1,)):
            if ahead < blocks:
                send_near(ahead)
    loop(straight, blocks, backward_step)

    gwb[...] = gw[...].astype(BF)
    height = gw.shape[0]
    for stage in range(stages):
        size = factors[stage]
        chunk = height // size
        src, buf, out = gwb if stage == 0 else summed[stage - 1], gathered[stage], summed[stage]
        rs_s, rs_r, ag_s, ag_r = psems[4 * stage : 4 * stage + 4]

        def part(q):
            return pl.ds(pl.multiple_of(q * chunk, chunk), chunk)

        for step in range(1, size):
            _, there, peer = stage_peer(stage, step)
            remote(src.at[part(there), :], buf.at[step - 1], rs_s.at[0], rs_r.at[0], {"blk": peer}).start()
        if stage == 0:
            @pl.when(is_inner)
            def _():
                for b in range(passed):
                    g_pass(b)
                turn_weight()

            for b in range(straight):
                finish(b)
        digit, _, _ = stage_peer(stage, 1)
        if stage == 0:
            total = gw[part(digit), :]
        else:
            total = src[part(digit), :].astype(F32)
        remote(buf, buf, rs_s.at[0], rs_r.at[0], owner_at(PAIR)).wait_recv()
        for step in range(1, size):
            total = total + buf[step - 1].astype(F32)
        out[part(digit), :] = total.astype(BF)
        for step in range(1, size):
            _, _, peer = stage_peer(stage, step)
            piece = out.at[part(digit), :]
            remote(piece, piece, ag_s.at[0], ag_r.at[0], {"blk": peer}).start()
        if stage == 0:
            for b in range(straight, blocks):
                finish(b)
        piece = out.at[pl.ds(0, height - chunk), :]
        remote(piece, piece, ag_s.at[0], ag_r.at[0], owner_at(PAIR)).wait_recv()
    gw[...] = (summed[-1] if stages else gwb)[...].astype(F32)

    for stage in range(stages):
        buf, out = gathered[stage], summed[stage]
        rs_s, rs_r, ag_s, ag_r = psems[4 * stage : 4 * stage + 4]
        remote(buf, buf, rs_s.at[0], rs_r.at[0], owner_at(PAIR)).wait_send()
        piece = out.at[pl.ds(0, height - height // factors[stage]), :]
        remote(piece, piece, ag_s.at[0], ag_r.at[0], owner_at(PAIR)).wait_send()

    def sent_all(ref, sem):
        remote(ref, ref, sem, ger.at[0], owner_at(PAIR)).wait_send()

    @pl.when(is_inner)
    def _():
        sent_all(x, xs.at[1])
        sent_all(gg.at[:, ocols(me)], zs.at[1])
        if half > 1:
            sent_all(gg.at[pl.ds(0, passed * side), pl.ds(0, (half - 1) * ow)], zl.at[0])
        for j in ends:
            sent_all(pe.at[j - 1], es.at[j - 1])
            sent_all(ge.at[j - 1], ges.at[j - 1])
            sent_all(xg.at[:, pl.ds(0, (nz - 1) * width)], xb.at[j - 1])

    @pl.when(jnp.logical_not(is_inner))
    def _():
        sent_all(x, xs.at[1])
        sent_all(x, xs.at[0])
        sent_all(gg.at[pl.ds(0, (blocks - passed) * side), ocols(me)], zs.at[1])
        sent_all(gg.at[:, ocols(me)], zs.at[0])
        remote(gx, gx, ges.at[0], ger.at[0], {"feat": inner}).wait_recv()

    for role in (PAIR, CROSS):
        sent_all(hid[role], hs.at[role])
    for role, count in ((OWN, wound), (offs, wound), (AHEAD, blocks - wound), (BEHIND, blocks - wound)):
        if count:
            sent_all(hid[OWN].at[pl.ds(0, count)], hs.at[role])
    for role in (PAIR, CROSS):
        sent_all(sent.at[role], gs.at[role])
    for role in (AHEAD, BEHIND):
        sent_all(sent.at[role, pl.ds(0, straight)], gs.at[role])
    if straight < blocks:
        sent_all(sent.at[OWN, pl.ds(straight, blocks - straight)], gs.at[OWN])
        sent_all(sent.at[OWN, pl.ds(straight, blocks - straight)], gs.at[offs])

    @pl.when(is_inner)
    def _():
        w_swap(True).wait_send()
        for j in ends if group > 1 else ():
            sent_all(w_rest(j), ws.at[j])

    @pl.when(jnp.logical_not(is_inner))
    def _():
        if half > 1:
            w_up().wait_send()


def write_out(*refs):
    count = (len(refs) - 1) // 2
    done = refs[-1]
    copies = [pltpu.make_async_copy(refs[i], refs[count + i], done.at[i]) for i in range(count)]
    for copy in copies:
        copy.start()
    for copy in copies:
        copy.wait()


def on_device(nb, nz, x, w, tv, tr, tc, cnt, go):
    offs, slots, side = tv.shape[1], tv.shape[2], tv.shape[-1]
    height, width = x.shape
    blocks = height // side
    depth, ow = w.shape
    factors = stage_factors(nb, depth)
    dims = (nb, nz, offs, slots, blocks, side, width, ow, tuple(factors))
    spare = max(nz // 2 - 1, 1)
    vmem = pl.BlockSpec(memory_space=pltpu.VMEM)
    hbm = pl.BlockSpec(memory_space=pltpu.HBM)
    dma = pltpu.SemaphoreType.DMA
    psems = []
    for f in factors:
        psems += [dma((1,))] * 4
    block = (side, ow)
    results = pl.pallas_call(
        functools.partial(layer_kernel, dims),
        out_shape=(
            pltpu.VMEM((height, ow), BF),
            pltpu.VMEM((height, width), BF),
            pltpu.VMEM((depth, ow), F32),
        ),
        in_specs=[hbm] * 7,
        out_specs=(vmem, vmem, vmem),
        scratch_shapes=[
            pltpu.SMEM((offs, 1, slots), tr.dtype),
            pltpu.SMEM((offs, 1, slots), tc.dtype),
            pltpu.SMEM(cnt.shape, cnt.dtype),
            pltpu.VMEM((height, nz * width), BF),
            pltpu.VMEM((depth, nz * ow), BF),
            pltpu.VMEM((offs, slots, side, side), BF),
            pltpu.VMEM((height, ow), BF),
            pltpu.VMEM((offs, slots, side, side), BF),
            pltpu.VMEM((offs, slots, *block), F32),
            pltpu.VMEM((blocks, *block), F32),
            pltpu.VMEM((blocks, *block), BF),
            pltpu.VMEM((offs, blocks, *block), BF),
            pltpu.VMEM((offs, blocks, *block), BF),
            pltpu.VMEM((height, nz * ow), BF),
            pltpu.VMEM((depth, ow), BF),
            pltpu.VMEM((spare, blocks, *block), BF),
            pltpu.VMEM((spare, blocks, side, width), BF),
            pltpu.VMEM((nz * ow, nz // 2 * width), BF),
        ]
        + [pltpu.VMEM((blocks, *block), BF)] * 3
        + [pltpu.VMEM((2, blocks, *block), BF)]
        + [pltpu.VMEM((f - 1, depth // f, ow), BF) for f in factors]
        + [pltpu.VMEM((depth, ow), BF) for f in factors]
        + [dma((2,)), dma((blocks,)), dma((spare,))]
        + [dma((offs + 1,)), dma((blocks,)), dma((2, blocks)), dma((offs,))]
        + [dma((offs + 1,)), dma((3, blocks))]
        + [dma((2,)), dma((blocks,)), dma((1,)), dma((spare, blocks))]
        + [dma((spare,)), dma((spare,)), dma((1,))]
        + [dma((spare + 1,)), dma((spare, 2)), dma((1,)), dma((1,)), dma((7,))]
        + psems,
        compiler_params=pltpu.CompilerParams(
            collective_id=0, has_side_effects=True, vmem_limit_bytes=32 * 1024 * 1024
        ),
    )(*[pltpu.with_memory_space_constraint(a, pltpu.HBM) for a in (x, w, tv, jnp.swapaxes(tr, 0, 1), jnp.swapaxes(tc, 0, 1), cnt, go)])
    return pl.pallas_call(
        write_out,
        out_shape=tuple(jax.ShapeDtypeStruct(r.shape, r.dtype) for r in results),
        in_specs=[vmem] * len(results),
        out_specs=(hbm,) * len(results),
        scratch_shapes=[dma((len(results),))],
    )(*[pltpu.with_memory_space_constraint(r, pltpu.VMEM) for r in results])


def solution(mesh):
    return jax.shard_map(
        functools.partial(on_device, mesh.shape["blk"], mesh.shape["feat"]),
        mesh=mesh,
        in_specs=(
            P("blk", "feat"),
            P(None, "feat"),
            P("blk", None, None, None, None),
            P("blk", None, None),
            P("blk", None, None),
            P("blk", None),
            P("blk", "feat"),
        ),
        out_specs=(P("blk", "feat"), P("blk", "feat"), P(None, "feat")),
        check_vma=False,
    )
```

```python
import functools

import jax
import jax.numpy as jnp
from jax import lax
from jax.experimental import pallas as pl
from jax.experimental.pallas import tpu as pltpu
from jax.sharding import PartitionSpec as P

MESH = pl.DeviceIdType.MESH
BF = jnp.bfloat16
F32 = jnp.float32


def stage_factors(count, rows):
    factors = []
    while count > 1:
        size = max(f for f in range(2, 17) if count % f == 0 and rows % (16 * f) == 0)
        factors.append(size)
        count //= size
    return factors


def remote(src, dst, send, recv, where):
    return pltpu.make_async_remote_copy(
        src_ref=src, dst_ref=dst, send_sem=send, recv_sem=recv, device_id=where, device_id_type=MESH
    )


def layer_kernel(
    dims, x, w_in, tv_in, tr_in, tc_in, cnt_in, go_in, y, gx, gw,
    tr, tc, cnt, xg, wg, tv, go, tt, prod, acc, gp, sent, got, gg, gwb, pe, ge, wt, *rest
):
    nb, nz, offs, slots, blocks, side, width, ow, factors = dims
    stages = len(factors)
    hid, hid_two, rest = rest[:3], rest[3:5], rest[5:]
    gathered, summed = rest[:stages], rest[stages : 2 * stages]
    (xs, xr, xb, hs, hr, hf, hall, gs, gr, zs, zr, zl, ze, es, ges, ger, ws, wr, ks, kr, near) = rest[2 * stages : 2 * stages + 21]
    psems = rest[2 * stages + 21 :]
    reach = (offs - 1) // 2
    half = nz // 2
    me = lax.axis_index("feat")
    own = lax.axis_index("blk")
    core = lax.rem(own, 2)
    turn = 1 - 2 * core
    OWN, PAIR, CROSS, AHEAD, BEHIND = range(5)
    lean = (0, 1, -1, 2, -2)
    lower = me < half
    inner = jnp.where(lower, half - 1, half)
    other = nz - 1 - inner
    is_inner = me == inner
    ends = range(1, half)
    mine = jnp.where(lower, half - 1 - me, me - half)
    straight = min(3, blocks)
    wound = min(blocks // 2 + 1, blocks)
    passing = range(straight, max(blocks - 2, straight))

    def end_at(j):
        return jnp.where(lower, half - 1 - j, half + j)

    def offset_of(role):
        return reach + lean[role] * turn

    def owner_at(role):
        return {"blk": lax.rem(own + lean[role] * turn + nb, nb)}

    chip = own // 2
    ahead_near = lax.rem(chip + own, 2) == 0
    near_role = jnp.where(ahead_near, AHEAD, BEHIND)
    far_role = AHEAD + BEHIND - near_role
    near_lean = jnp.where(ahead_near, lean[AHEAD], lean[BEHIND]) * turn
    near_owner = {"blk": lax.rem(own + near_lean + nb, nb)}
    skip = 2 * lean[AHEAD] * (2 * lax.rem(chip, 2) - 1)
    side_owner = {"blk": lax.rem(own + skip + nb, nb)}
    side_source = {"blk": lax.rem(own - skip + nb, nb)}

    def rows(b):
        return pl.ds(pl.multiple_of(b * side, side), side)

    def xcols(z):
        return pl.ds(pl.multiple_of(z * width, width), width)

    def ocols(z):
        return pl.ds(pl.multiple_of(z * ow, ow), ow)

    local = [
        pltpu.make_async_copy(w_in, wg.at[:, ocols(me)], near.at[0]),
        pltpu.make_async_copy(x, xg.at[:, xcols(me)], near.at[1]),
        pltpu.make_async_copy(tv_in.at[0], tv, near.at[2]),
        pltpu.make_async_copy(go_in, go, near.at[3]),
        pltpu.make_async_copy(tr_in, tr, near.at[4]),
        pltpu.make_async_copy(tc_in, tc, near.at[5]),
        pltpu.make_async_copy(cnt_in, cnt, near.at[6]),
    ]
    for copy in local:
        copy.start()

    def stage_peer(stage, step):
        stride = 1
        for f in factors[:stage]:
            stride *= f
        size = factors[stage]
        digit = lax.rem(own // stride, size)
        there = lax.rem(digit + step, size)
        return digit, there, own + (there - digit) * stride

    barrier = pltpu.get_barrier_semaphore()
    greeted = 0
    for step in range(1, nz):
        pl.semaphore_signal(barrier, inc=1, device_id={"feat": lax.rem(me + step, nz)}, device_id_type=MESH)
        greeted += 1
    around = [owner_at(PAIR), owner_at(AHEAD), owner_at(BEHIND), side_owner, side_source]
    for peer in around if stages > 1 else ():
        pl.semaphore_signal(barrier, inc=1, device_id=peer, device_id_type=MESH)
        greeted += 1
    for stage in range(stages):
        for step in range(1, factors[stage]):
            _, _, peer = stage_peer(stage, step)
            pl.semaphore_signal(barrier, inc=1, device_id={"blk": peer}, device_id_type=MESH)
            greeted += 1
    pl.semaphore_wait(barrier, greeted)

    depth = w_in.shape[0]

    group = factors[0] if stages else 1

    def part_of(digit):
        return pl.ds(pl.multiple_of(digit * (depth // group), depth // group), depth // group)

    my_part = part_of(stage_peer(0, 0)[0] if stages else 0)

    def x_copy(way, b):
        return remote(
            x.at[rows(b), :], xg.at[rows(b), xcols(me)], xs.at[way], xr.at[b], {"feat": (inner, other)[way]}
        )

    def x_back(s, e, j, b):
        piece = xg.at[rows(b), xcols(s)]
        return remote(piece, piece, xb.at[j - 1], xr.at[b], {"feat": e})

    def x_wait(b):
        piece = xg.at[rows(b), pl.ds(0, (nz - 1) * width)]
        remote(piece, piece, xs.at[0], xr.at[b], {"feat": other}).wait_recv()

    def w_up():
        return remote(w_in.at[my_part, :], wg.at[my_part, ocols(me)], ws.at[0], wr.at[mine - 1, 0], {"feat": inner})

    def w_around(j):
        piece = wg.at[my_part, ocols(end_at(j))]
        remote(piece, piece, ws.at[j], wr.at[j - 1, 0], owner_at(PAIR)).wait_recv()
        for step in range(1, group):
            peer = {"blk": stage_peer(0, step)[2]}
            remote(piece, piece, ws.at[j], wr.at[j - 1, 1], peer).start()

    def w_rest(j):
        return wg.at[pl.ds(0, depth - depth // group), ocols(end_at(j))]

    def w_wait(j):
        if group > 1:
            remote(w_rest(j), w_rest(j), ws.at[j], wr.at[j - 1, 1], owner_at(PAIR)).wait_recv()

    def w_swap(sending):
        there = jnp.where(lower, half, 0)
        here = half - there
        r, c = (there, here) if sending else (here, there)
        piece = wg.at[
            pl.ds(pl.multiple_of(r * width, width), half * width), pl.ds(pl.multiple_of(c * ow, ow), half * ow)
        ]
        return remote(piece, piece, ks.at[0], kr.at[0], {"feat": other})

    @pl.when(is_inner)
    def _():
        for b in range(min(6, blocks)):
            x_copy(1, b).start()

    @pl.when(jnp.logical_not(is_inner))
    def _():
        for b in range(blocks):
            x_copy(1, b).start()
            if b == 0 and half > 1:
                w_up().start()
            x_copy(0, b).start()

    for copy in local[:3]:
        copy.wait()

    def by_side(run):
        pl.when(ahead_near)(functools.partial(run, 0))
        pl.when(jnp.logical_not(ahead_near))(functools.partial(run, 1))

    def hid_pair(b):
        return remote(hid[OWN].at[b], hid[PAIR].at[b], hs.at[PAIR], hall.at[PAIR], owner_at(PAIR))

    def hid_straight(role, b):
        slot = int(role == AHEAD)
        return remote(hid[OWN].at[b], hid_two[slot].at[b], hs.at[role], hf.at[slot, b], owner_at(role))

    def hid_near(near, b):
        return remote(hid[OWN].at[b], hid_two[1 - near].at[b], hs.at[OWN], hf.at[1 - near, b], near_owner)

    def hid_side(near, b):
        return remote(hid_two[near].at[b], hid_two[1 - near].at[b], hs.at[offs], hf.at[1 - near, b], side_source)

    def hid_passed(b):
        return remote(hid_two[0].at[b], hid[CROSS].at[b], hs.at[CROSS], hall.at[CROSS], owner_at(PAIR))

    def hid_landed(slot, b):
        piece = hid_two[slot].at[b]
        remote(piece, piece, hs.at[OWN], hf.at[slot, b], owner_at(PAIR)).wait_recv()

    def hid_whole(role):
        remote(hid[role], hid[role], hs.at[role], hall.at[role], owner_at(PAIR)).wait_recv()

    def take_near(b):
        def run(near):
            hid_landed(near, b)
            hid_side(near, b).start()
            if near == 0:
                hid_passed(b).start()

        by_side(run)

    def take_far(b):
        def run(near):
            hid_landed(1 - near, b)
            if near == 1:
                hid_passed(b).start()

        by_side(run)

    def hid_down(j, b):
        return remote(pe.at[j - 1, b], hid[OWN].at[b], es.at[j - 1], hr.at[b], {"feat": end_at(j)})

    def spread(b):
        hid_pair(b).start()

        @pl.when(b < wound)
        def _():
            by_side(lambda near: hid_near(near, b).start())

        @pl.when(b >= wound)
        def _():
            hid_straight(AHEAD, b).start()
            hid_straight(BEHIND, b).start()

    def hidden_of(z, b):
        return jnp.dot(xg[rows(b), :], wg[:, ocols(z)], preferred_element_type=F32).astype(BF)

    def serve_ends(b):
        for j in ends:
            pe[j - 1, b] = hidden_of(end_at(j), b)
            hid_down(j, b).start()

    lag = min(4, blocks)
    first = min(2, blocks - 1)

    def forward_step(b, carry):
        @pl.when(is_inner)
        def _():
            @pl.when(b + 6 < blocks)
            def _():
                x_copy(1, b + 6).start()

        per_block = slots // blocks
        for role in range(offs):
            for s in range(per_block):
                slot = b * per_block + s
                tt[role, slot] = tv[offset_of(role), slot].T

        @pl.when(is_inner)
        def _():
            x_wait(b)

            @pl.when(b > first)
            def _():
                serve_ends(b)

            hid[OWN][b] = hidden_of(me, b)
            spread(b)

            @pl.when(b == first)
            def _():
                for j in ends:
                    w_wait(j)
                for early in range(first + 1):
                    serve_ends(early)

        @pl.when(jnp.logical_not(is_inner))
        def _():
            remote(hid[OWN].at[b], hid[OWN].at[b], es.at[0], hr.at[b], {"feat": inner}).wait_recv()
            spread(b)

        @pl.when(b >= lag)
        def _():
            take_near(b - lag)

        return carry

    @pl.when(is_inner)
    def _():
        for j in ends:
            w_around(j)

    lax.fori_loop(0, blocks, forward_step, 0)

    @pl.when(is_inner)
    def _():
        w_swap(True).start()
        for j in ends:
            for b in range(blocks):
                for step in range(nz):
                    s = lax.rem(me + step, nz)

                    @pl.when(s != end_at(j))
                    def _():
                        x_back(s, end_at(j), j, b).start()

    for copy in local[4:]:
        copy.wait()

    def forward_products(role):
        k = offset_of(role)
        for s in range(slots):
            c = tc[k, 0, s]
            source = (hid[role] if role < AHEAD else hid_two[role - AHEAD])[c]
            prod[role, s] = jnp.dot(tv[k, s], source, preferred_element_type=F32)

    def weight_of(table, k, s, b):
        return jnp.where((table[k, 0, s] == b) & (s < cnt[0, k]), 1.0, 0.0).astype(F32)

    def row_sum(role, b, total):
        for s in range(slots):
            total = total + prod[role, s] * weight_of(tr, offset_of(role), s, b)
        return total

    def gather_role(role):
        forward_products(role)

        def add(b, carry):
            start = hid[OWN][b].astype(F32) if role == OWN else acc[b]
            acc[b] = row_sum(role, b, start)
            return carry

        lax.fori_loop(0, blocks, add, 0)

    gather_role(OWN)
    for b in range(blocks - lag, wound):
        take_near(b)
    hid_whole(PAIR)
    gather_role(PAIR)
    for b in range(wound):
        take_far(b)
    for b in range(wound, blocks):
        hid_landed(0, b)
        hid_passed(b).start()
    gather_role(AHEAD)
    for b in range(wound, blocks):
        hid_landed(1, b)
    gather_role(BEHIND)
    local[3].wait()
    hid_whole(CROSS)
    forward_products(CROSS)

    def pointwise(b, carry):
        v = row_sum(CROSS, b, acc[b])
        sigma = jax.nn.sigmoid(v)
        y[rows(b), :] = (v * sigma).astype(BF)
        slope = sigma * (1.0 + v * (1.0 - sigma))
        gp[b] = (go[rows(b), :].astype(F32) * slope).astype(BF)
        return carry

    lax.fori_loop(0, blocks, pointwise, 0)

    def backward_products(role):
        for s in range(slots):
            prod[role, s] = jnp.dot(tt[role, s], gp[tr[offset_of(role), 0, s]], preferred_element_type=F32)

    def column_sum(role, offset, c, start):
        total = start
        for s in range(slots):
            term = prod[role, s] * weight_of(tc, offset, s, c)
            total = term if total is None else total + term
        return total

    target = {PAIR: PAIR, CROSS: PAIR, AHEAD: AHEAD, BEHIND: BEHIND}
    arrives = {PAIR: PAIR, CROSS: CROSS, AHEAD: BEHIND, BEHIND: AHEAD}

    def sum_copy(role, c):
        return remote(
            sent.at[role, c], got.at[arrives[role], c], gs.at[role], gr.at[int(role == CROSS), c], owner_at(target[role])
        )

    def cross_wait(c):
        piece = got.at[CROSS, c]
        remote(piece, piece, gs.at[CROSS], gr.at[1, c], owner_at(PAIR)).wait_recv()

    def send_sum(role, c):
        sent[role, c] = column_sum(role, offset_of(role), c, None).astype(BF)
        sum_copy(role, c).start()

    def send_joint(c):
        cross_wait(c)
        start = got[CROSS, c].astype(F32)
        sent[AHEAD, c] = column_sum(AHEAD, offset_of(AHEAD), c, start).astype(BF)
        sum_copy(AHEAD, c).start()

    def side_copy(c):
        return remote(sent.at[far_role, c], got.at[OWN, c], gs.at[OWN], gr.at[2, c], side_owner)

    def send_side_early(c):
        sent[BEHIND, c] = column_sum(BEHIND, offset_of(BEHIND), c, None).astype(BF)
        side_copy(c).start()

    def send_side_late(c):
        cross_wait(c)
        start = got[CROSS, c].astype(F32)
        sent[AHEAD, c] = column_sum(AHEAD, offset_of(AHEAD), c, start).astype(BF)
        side_copy(c).start()

    crossing_near = jnp.where(ahead_near, 1.0, 0.0).astype(F32)

    def send_near(c):
        @pl.when(ahead_near)
        def _():
            cross_wait(c)

        start = got[CROSS, c].astype(F32) * crossing_near
        total = column_sum(near_role, reach + near_lean, c, start)
        piece = got.at[OWN, c]
        remote(piece, piece, gs.at[OWN], gr.at[2, c], side_owner).wait_recv()
        sent[near_role, c] = (total + got[OWN, c].astype(F32)).astype(BF)
        remote(sent.at[near_role, c], got.at[AHEAD, c], gs.at[offs], gr.at[0, c], near_owner).start()

    def loop(low, high, step):
        def body(c, carry):
            step(c)
            return carry

        lax.fori_loop(low, high, body, 0)

    backward_products(CROSS)
    loop(0, blocks, lambda c: send_sum(CROSS, c))
    backward_products(BEHIND)
    send_sum(BEHIND, 0)

    @pl.when(ahead_near)
    def _():
        for c in range(straight, blocks):
            send_side_early(c)

    backward_products(AHEAD)
    send_joint(0)

    @pl.when(jnp.logical_not(ahead_near))
    def _():
        for c in range(straight, blocks):
            send_side_late(c)

    for c in range(1, straight):
        send_sum(BEHIND, c)
        send_joint(c)
    backward_products(PAIR)
    loop(0, blocks, lambda c: send_sum(PAIR, c))
    backward_products(OWN)

    gw[...] = jnp.zeros_like(gw)

    def g_copy(way, b, landed):
        piece = gg.at[rows(b), ocols(me)]
        return remote(piece, piece, zs.at[way], landed, {"feat": (inner, other)[way]})

    def g_wait(b):
        piece = gg.at[rows(b), pl.ds(0, (half if b in passing else nz - 1) * ow)]
        remote(piece, piece, zs.at[0], zr.at[b], {"feat": other}).wait_recv()

    def g_pass(b):
        for j in ends:
            piece = gg.at[rows(b), ocols(end_at(j))]
            remote(piece, piece, zl.at[0], ze.at[j - 1, b], {"feat": other}).wait_recv()
            remote(piece, piece, zl.at[0], zr.at[b], {"feat": other}).start()

    def pass_on(some):
        @pl.when(is_inner)
        def _():
            for b in some:
                g_pass(b)

    def make_grad(b, two):
        pieces = got.at[pl.ds(0, 3 if two else 2), b]
        total = column_sum(OWN, reach, b, gp[b].astype(F32))
        remote(pieces, pieces, gs.at[PAIR], gr.at[0, b], owner_at(PAIR)).wait_recv()
        for role in (PAIR, AHEAD, BEHIND)[: 3 if two else 2]:
            total = total + got[role, b].astype(F32)
        grad = total.astype(BF)
        gg[rows(b), ocols(me)] = grad

        @pl.when(is_inner)
        def _():
            g_copy(1, b, zr.at[b]).start()

        if half > 1:
            @pl.when(jnp.logical_not(is_inner))
            def _():
                passes = (b >= passing.start) & (b < passing.stop)

                @pl.when(passes)
                def _():
                    g_copy(0, b, ze.at[mine - 1, b]).start()

                @pl.when(jnp.logical_not(passes))
                def _():
                    g_copy(1, b, zr.at[b]).start()
                    g_copy(0, b, zr.at[b]).start()

                x_wait(b)

        gw[...] += lax.dot_general(xg[rows(b), :], grad, (((0,), (0,)), ((), ())), preferred_element_type=F32)

    def gx_down(j, b):
        return remote(ge.at[j - 1, b], gx.at[rows(b), :], ges.at[j - 1], ger.at[0], {"feat": end_at(j)})

    def turn_weight():
        w_swap(False).wait_recv()
        for j in range(half):
            wt[:, pl.ds(j * width, width)] = wg[xcols(end_at(j)), :].T

    def finish(b):
        @pl.when(is_inner)
        def _():
            g_wait(b)
            grads = jnp.dot(gg[rows(b), :], wt[...], preferred_element_type=F32).astype(BF)
            for j in ends:
                ge[j - 1, b] = grads[:, j * width : (j + 1) * width]
                gx_down(j, b).start()
            gx[rows(b), :] = grads[:, :width]

    @pl.when(is_inner)
    def _():
        turn_weight()

    waiting = list(range(straight, blocks))
    for c in range(blocks):
        for later in waiting[c : c + 1]:
            send_near(later)
        make_grad(c, c < straight)

    gwb[...] = gw[...].astype(BF)
    height = gw.shape[0]
    for stage in range(stages):
        size = factors[stage]
        chunk = height // size
        src, buf, out = gwb if stage == 0 else summed[stage - 1], gathered[stage], summed[stage]
        rs_s, rs_r, ag_s, ag_r = psems[4 * stage : 4 * stage + 4]

        def part(q):
            return pl.ds(pl.multiple_of(q * chunk, chunk), chunk)

        for step in range(1, size):
            _, there, peer = stage_peer(stage, step)
            remote(src.at[part(there), :], buf.at[step - 1], rs_s.at[0], rs_r.at[0], {"blk": peer}).start()
        if stage == 0:
            for b in range(straight):
                finish(b)
            pass_on(passing)
        digit, _, _ = stage_peer(stage, 1)
        if stage == 0:
            total = gw[part(digit), :]
        else:
            total = src[part(digit), :].astype(F32)
        remote(buf, buf, rs_s.at[0], rs_r.at[0], owner_at(PAIR)).wait_recv()
        for step in range(1, size):
            total = total + buf[step - 1].astype(F32)
        out[part(digit), :] = total.astype(BF)
        for step in range(1, size):
            _, _, peer = stage_peer(stage, step)
            piece = out.at[part(digit), :]
            remote(piece, piece, ag_s.at[0], ag_r.at[0], {"blk": peer}).start()
        if stage == 0:
            late = list(range(passing.stop, blocks))
            for b in passing:
                finish(b)
                if late:
                    finish(late.pop(0))
            for b in late:
                finish(b)
        piece = out.at[pl.ds(0, height - chunk), :]
        remote(piece, piece, ag_s.at[0], ag_r.at[0], owner_at(PAIR)).wait_recv()
    gw[...] = (summed[-1] if stages else gwb)[...].astype(F32)

    for stage in range(stages):
        buf, out = gathered[stage], summed[stage]
        rs_s, rs_r, ag_s, ag_r = psems[4 * stage : 4 * stage + 4]
        remote(buf, buf, rs_s.at[0], rs_r.at[0], owner_at(PAIR)).wait_send()
        piece = out.at[pl.ds(0, height - height // factors[stage]), :]
        remote(piece, piece, ag_s.at[0], ag_r.at[0], owner_at(PAIR)).wait_send()

    def sent_all(ref, sem):
        remote(ref, ref, sem, ger.at[0], owner_at(PAIR)).wait_send()

    @pl.when(is_inner)
    def _():
        sent_all(x, xs.at[1])
        sent_all(gg.at[:, ocols(me)], zs.at[1])
        if half > 1 and passing:
            sent_all(gg.at[pl.ds(0, len(passing) * side), pl.ds(0, (half - 1) * ow)], zl.at[0])
        for j in ends:
            sent_all(pe.at[j - 1], es.at[j - 1])
            sent_all(ge.at[j - 1], ges.at[j - 1])
            sent_all(xg.at[:, pl.ds(0, (nz - 1) * width)], xb.at[j - 1])

    @pl.when(jnp.logical_not(is_inner))
    def _():
        sent_all(x, xs.at[1])
        sent_all(x, xs.at[0])
        sent_all(gg.at[pl.ds(0, (blocks - len(passing)) * side), ocols(me)], zs.at[1])
        sent_all(gg.at[:, ocols(me)], zs.at[0])
        remote(gx, gx, ges.at[0], ger.at[0], {"feat": inner}).wait_recv()

    for role in (PAIR, CROSS):
        sent_all(hid[role], hs.at[role])
    for role, count in ((OWN, wound), (offs, wound), (AHEAD, blocks - wound), (BEHIND, blocks - wound)):
        if count:
            sent_all(hid[OWN].at[pl.ds(0, count)], hs.at[role])
    for role in (PAIR, CROSS):
        sent_all(sent.at[role], gs.at[role])
    for role in (AHEAD, BEHIND):
        sent_all(sent.at[role, pl.ds(0, straight)], gs.at[role])
    if straight < blocks:
        sent_all(sent.at[OWN, pl.ds(straight, blocks - straight)], gs.at[OWN])
        sent_all(sent.at[OWN, pl.ds(straight, blocks - straight)], gs.at[offs])

    @pl.when(is_inner)
    def _():
        w_swap(True).wait_send()
        for j in ends if group > 1 else ():
            sent_all(w_rest(j), ws.at[j])

    @pl.when(jnp.logical_not(is_inner))
    def _():
        if half > 1:
            w_up().wait_send()


def write_out(*refs):
    count = (len(refs) - 1) // 2
    done = refs[-1]
    copies = [pltpu.make_async_copy(refs[i], refs[count + i], done.at[i]) for i in range(count)]
    for copy in copies:
        copy.start()
    for copy in copies:
        copy.wait()


def on_device(nb, nz, x, w, tv, tr, tc, cnt, go):
    offs, slots, side = tv.shape[1], tv.shape[2], tv.shape[-1]
    height, width = x.shape
    blocks = height // side
    depth, ow = w.shape
    factors = stage_factors(nb, depth)
    dims = (nb, nz, offs, slots, blocks, side, width, ow, tuple(factors))
    spare = max(nz // 2 - 1, 1)
    vmem = pl.BlockSpec(memory_space=pltpu.VMEM)
    hbm = pl.BlockSpec(memory_space=pltpu.HBM)
    dma = pltpu.SemaphoreType.DMA
    psems = []
    for f in factors:
        psems += [dma((1,))] * 4
    block = (side, ow)
    results = pl.pallas_call(
        functools.partial(layer_kernel, dims),
        out_shape=(
            pltpu.VMEM((height, ow), BF),
            pltpu.VMEM((height, width), BF),
            pltpu.VMEM((depth, ow), F32),
        ),
        in_specs=[hbm] * 7,
        out_specs=(vmem, vmem, vmem),
        scratch_shapes=[
            pltpu.SMEM((offs, 1, slots), tr.dtype),
            pltpu.SMEM((offs, 1, slots), tc.dtype),
            pltpu.SMEM(cnt.shape, cnt.dtype),
            pltpu.VMEM((height, nz * width), BF),
            pltpu.VMEM((depth, nz * ow), BF),
            pltpu.VMEM((offs, slots, side, side), BF),
            pltpu.VMEM((height, ow), BF),
            pltpu.VMEM((offs, slots, side, side), BF),
            pltpu.VMEM((offs, slots, *block), F32),
            pltpu.VMEM((blocks, *block), F32),
            pltpu.VMEM((blocks, *block), BF),
            pltpu.VMEM((offs, blocks, *block), BF),
            pltpu.VMEM((offs, blocks, *block), BF),
            pltpu.VMEM((height, nz * ow), BF),
            pltpu.VMEM((depth, ow), BF),
            pltpu.VMEM((spare, blocks, *block), BF),
            pltpu.VMEM((spare, blocks, side, width), BF),
            pltpu.VMEM((nz * ow, nz // 2 * width), BF),
        ]
        + [pltpu.VMEM((blocks, *block), BF)] * 5
        + [pltpu.VMEM((f - 1, depth // f, ow), BF) for f in factors]
        + [pltpu.VMEM((depth, ow), BF) for f in factors]
        + [dma((2,)), dma((blocks,)), dma((spare,))]
        + [dma((offs + 1,)), dma((blocks,)), dma((2, blocks)), dma((offs,))]
        + [dma((offs + 1,)), dma((3, blocks))]
        + [dma((2,)), dma((blocks,)), dma((1,)), dma((spare, blocks))]
        + [dma((spare,)), dma((spare,)), dma((1,))]
        + [dma((spare + 1,)), dma((spare, 2)), dma((1,)), dma((1,)), dma((7,))]
        + psems,
        compiler_params=pltpu.CompilerParams(
            collective_id=0, has_side_effects=True, vmem_limit_bytes=32 * 1024 * 1024
        ),
    )(*[pltpu.with_memory_space_constraint(a, pltpu.HBM) for a in (x, w, tv, jnp.swapaxes(tr, 0, 1), jnp.swapaxes(tc, 0, 1), cnt, go)])
    return pl.pallas_call(
        write_out,
        out_shape=tuple(jax.ShapeDtypeStruct(r.shape, r.dtype) for r in results),
        in_specs=[vmem] * len(results),
        out_specs=(hbm,) * len(results),
        scratch_shapes=[dma((len(results),))],
    )(*[pltpu.with_memory_space_constraint(r, pltpu.VMEM) for r in results])


def solution(mesh):
    return jax.shard_map(
        functools.partial(on_device, mesh.shape["blk"], mesh.shape["feat"]),
        mesh=mesh,
        in_specs=(
            P("blk", "feat"),
            P(None, "feat"),
            P("blk", None, None, None, None),
            P("blk", None, None),
            P("blk", None, None),
            P("blk", None),
            P("blk", "feat"),
        ),
        out_specs=(P("blk", "feat"), P("blk", "feat"), P(None, "feat")),
        check_vma=False,
    )
```

```python
import functools

import jax
import jax.numpy as jnp
from jax import lax
from jax.experimental import pallas as pl
from jax.experimental.pallas import tpu as pltpu
from jax.sharding import PartitionSpec as P

MESH = pl.DeviceIdType.MESH
BF = jnp.bfloat16
F32 = jnp.float32


def stage_factors(count, rows):
    factors = []
    while count > 1:
        size = max(f for f in range(2, 17) if count % f == 0 and rows % (16 * f) == 0)
        factors.append(size)
        count //= size
    return factors


def remote(src, dst, send, recv, where):
    return pltpu.make_async_remote_copy(
        src_ref=src, dst_ref=dst, send_sem=send, recv_sem=recv, device_id=where, device_id_type=MESH
    )


def layer_kernel(
    dims, x, w_in, tv_in, tr_in, tc_in, cnt_in, go_in, y, gx, gw,
    tr, tc, cnt, xg, wg, tv, go, tt, prod, acc, gp, sent, got, gg, gwb, pe, ge, wt, *rest
):
    nb, nz, offs, slots, blocks, side, width, ow, factors = dims
    stages = len(factors)
    hid, hid_two, rest = rest[:3], rest[3:5], rest[5:]
    gathered, summed = rest[:stages], rest[stages : 2 * stages]
    (xs, xr, xb, hs, hr, hf, hall, gs, gr, gy, zs, zr, zl, ze, es, ges, ger, ws, wr, ks, kr, near) = rest[2 * stages : 2 * stages + 22]
    psems = rest[2 * stages + 22 :]
    reach = (offs - 1) // 2
    half = nz // 2
    me = lax.axis_index("feat")
    own = lax.axis_index("blk")
    core = lax.rem(own, 2)
    turn = 1 - 2 * core
    OWN, PAIR, CROSS, AHEAD, BEHIND = range(5)
    lean = (0, 1, -1, 2, -2)
    lower = me < half
    inner = jnp.where(lower, half - 1, half)
    other = nz - 1 - inner
    is_inner = me == inner
    ends = range(1, half)
    mine = jnp.where(lower, half - 1 - me, me - half)
    straight = min(3, blocks)
    wound = min(blocks // 2 + 1, blocks)
    passing = range(min(2, blocks), max(blocks - 2, 2))
    last = blocks - 1

    def end_at(j):
        return jnp.where(lower, half - 1 - j, half + j)

    def offset_of(role):
        return reach + lean[role] * turn

    def owner_at(role):
        return {"blk": lax.rem(own + lean[role] * turn + nb, nb)}

    chip = own // 2
    ahead_near = lax.rem(chip + own, 2) == 0
    near_role = jnp.where(ahead_near, AHEAD, BEHIND)
    far_role = AHEAD + BEHIND - near_role
    near_lean = jnp.where(ahead_near, lean[AHEAD], lean[BEHIND]) * turn
    near_owner = {"blk": lax.rem(own + near_lean + nb, nb)}
    skip = 2 * lean[AHEAD] * (2 * lax.rem(chip, 2) - 1)
    side_owner = {"blk": lax.rem(own + skip + nb, nb)}
    side_source = {"blk": lax.rem(own - skip + nb, nb)}

    def rows(b):
        return pl.ds(pl.multiple_of(b * side, side), side)

    def xcols(z):
        return pl.ds(pl.multiple_of(z * width, width), width)

    def ocols(z):
        return pl.ds(pl.multiple_of(z * ow, ow), ow)

    local = [
        pltpu.make_async_copy(w_in, wg.at[:, ocols(me)], near.at[0]),
        pltpu.make_async_copy(x, xg.at[:, xcols(me)], near.at[1]),
        pltpu.make_async_copy(tv_in.at[0], tv, near.at[2]),
        pltpu.make_async_copy(go_in, go, near.at[3]),
        pltpu.make_async_copy(tr_in, tr, near.at[4]),
        pltpu.make_async_copy(tc_in, tc, near.at[5]),
        pltpu.make_async_copy(cnt_in, cnt, near.at[6]),
    ]
    for copy in local:
        copy.start()

    def stage_peer(stage, step):
        stride = 1
        for f in factors[:stage]:
            stride *= f
        size = factors[stage]
        digit = lax.rem(own // stride, size)
        there = lax.rem(digit + step, size)
        return digit, there, own + (there - digit) * stride

    barrier = pltpu.get_barrier_semaphore()
    greeted = 0
    for step in range(1, nz):
        pl.semaphore_signal(barrier, inc=1, device_id={"feat": lax.rem(me + step, nz)}, device_id_type=MESH)
        greeted += 1
    around = [owner_at(PAIR), owner_at(AHEAD), owner_at(BEHIND), side_owner, side_source]
    for peer in around if stages > 1 else ():
        pl.semaphore_signal(barrier, inc=1, device_id=peer, device_id_type=MESH)
        greeted += 1
    for stage in range(stages):
        for step in range(1, factors[stage]):
            _, _, peer = stage_peer(stage, step)
            pl.semaphore_signal(barrier, inc=1, device_id={"blk": peer}, device_id_type=MESH)
            greeted += 1
    pl.semaphore_wait(barrier, greeted)

    depth = w_in.shape[0]

    group = factors[0] if stages else 1

    def part_of(digit):
        return pl.ds(pl.multiple_of(digit * (depth // group), depth // group), depth // group)

    my_part = part_of(stage_peer(0, 0)[0] if stages else 0)

    def x_copy(way, b):
        return remote(
            x.at[rows(b), :], xg.at[rows(b), xcols(me)], xs.at[way], xr.at[b], {"feat": (inner, other)[way]}
        )

    def x_own(j, b):
        piece = xg.at[rows(b), xcols(me)]
        return remote(x.at[rows(b), :], piece, xb.at[j - 1], xr.at[b], {"feat": end_at(j)})

    def x_back(s, e, j, b):
        piece = xg.at[rows(b), xcols(s)]
        return remote(piece, piece, xb.at[j - 1], xr.at[b], {"feat": e})

    def x_wait(b):
        piece = xg.at[rows(b), pl.ds(0, (nz - 1) * width)]
        remote(piece, piece, xs.at[0], xr.at[b], {"feat": other}).wait_recv()

    def w_up():
        return remote(w_in.at[my_part, :], wg.at[my_part, ocols(me)], ws.at[0], wr.at[mine - 1, 0], {"feat": inner})

    def w_around(j):
        piece = wg.at[my_part, ocols(end_at(j))]
        remote(piece, piece, ws.at[j], wr.at[j - 1, 0], owner_at(PAIR)).wait_recv()
        for step in range(1, group):
            peer = {"blk": stage_peer(0, step)[2]}
            remote(piece, piece, ws.at[j], wr.at[j - 1, 1], peer).start()

    def w_rest(j):
        return wg.at[pl.ds(0, depth - depth // group), ocols(end_at(j))]

    def w_wait(j):
        if group > 1:
            remote(w_rest(j), w_rest(j), ws.at[j], wr.at[j - 1, 1], owner_at(PAIR)).wait_recv()

    def w_swap(sending):
        there = jnp.where(lower, half, 0)
        here = half - there
        r, c = (there, here) if sending else (here, there)
        piece = wg.at[
            pl.ds(pl.multiple_of(r * width, width), half * width), pl.ds(pl.multiple_of(c * ow, ow), half * ow)
        ]
        return remote(piece, piece, ks.at[0], kr.at[0], {"feat": other})

    @pl.when(is_inner)
    def _():
        for b in range(min(6, blocks)):
            x_copy(1, b).start()
            for j in ends:
                x_own(j, b).start()

    @pl.when(jnp.logical_not(is_inner))
    def _():
        for b in range(blocks):
            x_copy(1, b).start()
            if b == 0 and half > 1:
                w_up().start()
            x_copy(0, b).start()

    for copy in local[:3]:
        copy.wait()

    def by_side(run):
        pl.when(ahead_near)(functools.partial(run, 0))
        pl.when(jnp.logical_not(ahead_near))(functools.partial(run, 1))

    def hid_pair(b):
        return remote(hid[OWN].at[b], hid[PAIR].at[b], hs.at[0], hall.at[0], owner_at(PAIR))

    def hid_straight(role, b):
        slot = int(role == AHEAD)
        return remote(hid[OWN].at[b], hid_two[slot].at[b], hs.at[0], hf.at[slot, b], owner_at(role))

    def hid_near(near, b):
        return remote(hid[OWN].at[b], hid_two[1 - near].at[b], hs.at[0], hf.at[1 - near, b], near_owner)

    def hid_side(near, b):
        return remote(hid_two[near].at[b], hid_two[1 - near].at[b], hs.at[0], hf.at[1 - near, b], side_source)

    def hid_passed(b):
        return remote(hid_two[0].at[b], hid[CROSS].at[b], hs.at[0], hall.at[1], owner_at(PAIR))

    def hid_landed(slot, b):
        piece = hid_two[slot].at[b]
        remote(piece, piece, hs.at[0], hf.at[slot, b], owner_at(PAIR)).wait_recv()

    def hid_whole(role):
        remote(hid[role], hid[role], hs.at[0], hall.at[int(role == CROSS)], owner_at(PAIR)).wait_recv()

    def take_near(b):
        def run(near):
            hid_landed(near, b)
            hid_side(near, b).start()
            if near == 0:
                hid_passed(b).start()

        by_side(run)

    def take_far(b):
        def run(near):
            hid_landed(1 - near, b)
            if near == 1:
                hid_passed(b).start()

        by_side(run)

    def hid_down(j, b):
        return remote(pe.at[j - 1, b], hid[OWN].at[b], es.at[j - 1], hr.at[b], {"feat": end_at(j)})

    def spread(b):
        hid_pair(b).start()

        @pl.when(b < wound)
        def _():
            by_side(lambda near: hid_near(near, b).start())

        @pl.when(b >= wound)
        def _():
            hid_straight(AHEAD, b).start()
            hid_straight(BEHIND, b).start()

    def hidden_of(z, b):
        return jnp.dot(xg[rows(b), :], wg[:, ocols(z)], preferred_element_type=F32).astype(BF)

    def serve_ends(b):
        for j in ends:
            pe[j - 1, b] = hidden_of(end_at(j), b)
            hid_down(j, b).start()

    lag = min(4, blocks)
    first = min(2, blocks - 1)

    def forward_step(b, carry):
        @pl.when(is_inner)
        def _():
            @pl.when(b + 6 < blocks)
            def _():
                x_copy(1, b + 6).start()
                for j in ends:
                    x_own(j, b + 6).start()

        per_block = slots // blocks
        for role in range(offs):
            for s in range(per_block):
                slot = b * per_block + s
                tt[role, slot] = tv[offset_of(role), slot].T

        @pl.when(is_inner)
        def _():
            x_wait(b)

            @pl.when(b > first)
            def _():
                serve_ends(b)

            hid[OWN][b] = hidden_of(me, b)
            spread(b)

            @pl.when(b == first)
            def _():
                for j in ends:
                    w_wait(j)
                for early in range(first + 1):
                    serve_ends(early)

        @pl.when(jnp.logical_not(is_inner))
        def _():
            remote(hid[OWN].at[b], hid[OWN].at[b], es.at[0], hr.at[b], {"feat": inner}).wait_recv()
            spread(b)

        @pl.when(b >= lag)
        def _():
            take_near(b - lag)

        return carry

    @pl.when(is_inner)
    def _():
        for j in ends:
            w_around(j)

    lax.fori_loop(0, blocks, forward_step, 0)

    @pl.when(is_inner)
    def _():
        w_swap(True).start()
        for j in ends:
            for b in range(blocks):
                for step in range(1, nz):
                    s = lax.rem(me + step, nz)

                    @pl.when(s != end_at(j))
                    def _():
                        x_back(s, end_at(j), j, b).start()

    for copy in local[4:]:
        copy.wait()

    def forward_products(role):
        k = offset_of(role)
        for s in range(slots):
            c = tc[k, 0, s]
            source = (hid[role] if role < AHEAD else hid_two[role - AHEAD])[c]
            prod[role, s] = jnp.dot(tv[k, s], source, preferred_element_type=F32)

    def weight_of(table, k, s, b):
        return jnp.where((table[k, 0, s] == b) & (s < cnt[0, k]), 1.0, 0.0).astype(F32)

    def row_sum(role, b, total):
        for s in range(slots):
            total = total + prod[role, s] * weight_of(tr, offset_of(role), s, b)
        return total

    def gather_role(role):
        forward_products(role)

        def add(b, carry):
            start = hid[OWN][b].astype(F32) if role == OWN else acc[b]
            acc[b] = row_sum(role, b, start)
            return carry

        lax.fori_loop(0, blocks, add, 0)

    gather_role(OWN)
    for b in range(blocks - lag, wound):
        take_near(b)
    hid_whole(PAIR)
    gather_role(PAIR)
    for b in range(wound):
        take_far(b)
    for b in range(wound, blocks):
        hid_landed(0, b)
        hid_passed(b).start()
    gather_role(AHEAD)
    for b in range(wound, blocks):
        hid_landed(1, b)
    gather_role(BEHIND)
    local[3].wait()
    hid_whole(CROSS)
    forward_products(CROSS)

    def pointwise(b, carry):
        v = row_sum(CROSS, b, acc[b])
        sigma = jax.nn.sigmoid(v)
        y[rows(b), :] = (v * sigma).astype(BF)
        slope = sigma * (1.0 + v * (1.0 - sigma))
        gp[b] = (go[rows(b), :].astype(F32) * slope).astype(BF)
        return carry

    lax.fori_loop(0, blocks, pointwise, 0)

    def backward_products(role):
        for s in range(slots):
            prod[role, s] = jnp.dot(tt[role, s], gp[tr[offset_of(role), 0, s]], preferred_element_type=F32)

    def column_sum(role, offset, c, start):
        total = start
        for s in range(slots):
            term = prod[role, s] * weight_of(tc, offset, s, c)
            total = term if total is None else total + term
        return total

    target = {PAIR: PAIR, CROSS: PAIR, AHEAD: AHEAD, BEHIND: BEHIND}
    arrives = {PAIR: PAIR, CROSS: CROSS, AHEAD: BEHIND, BEHIND: AHEAD}

    def sum_copy(role, c):
        return remote(
            sent.at[role, c], got.at[arrives[role], c], gs.at[0], gr.at[int(role == CROSS), c], owner_at(target[role])
        )

    def cross_wait(c):
        piece = got.at[CROSS, c]
        remote(piece, piece, gs.at[0], gr.at[1, c], owner_at(PAIR)).wait_recv()

    def send_sum(role, c):
        sent[role, c] = column_sum(role, offset_of(role), c, None).astype(BF)
        sum_copy(role, c).start()

    def send_joint(c):
        cross_wait(c)
        start = got[CROSS, c].astype(F32)
        sent[AHEAD, c] = column_sum(AHEAD, offset_of(AHEAD), c, start).astype(BF)
        sum_copy(AHEAD, c).start()

    def side_copy(c):
        return remote(sent.at[far_role, c], got.at[OWN, c], gs.at[0], gy.at[c - straight], side_owner)

    def send_side_early(c):
        sent[BEHIND, c] = column_sum(BEHIND, offset_of(BEHIND), c, None).astype(BF)
        side_copy(c).start()

    def send_side_late(c):
        cross_wait(c)
        start = got[CROSS, c].astype(F32)
        sent[AHEAD, c] = column_sum(AHEAD, offset_of(AHEAD), c, start).astype(BF)
        side_copy(c).start()

    crossing_near = jnp.where(ahead_near, 1.0, 0.0).astype(F32)

    def send_near(c):
        @pl.when(ahead_near)
        def _():
            cross_wait(c)

        start = got[CROSS, c].astype(F32) * crossing_near
        total = column_sum(near_role, reach + near_lean, c, start)
        piece = got.at[OWN, c]
        remote(piece, piece, gs.at[0], gy.at[c - straight], side_owner).wait_recv()
        sent[near_role, c] = (total + got[OWN, c].astype(F32)).astype(BF)
        remote(sent.at[near_role, c], got.at[AHEAD, c], gs.at[0], gr.at[0, c], near_owner).start()

    def loop(low, high, step):
        def body(c, carry):
            step(c)
            return carry

        lax.fori_loop(low, high, body, 0)

    backward_products(CROSS)
    loop(0, blocks, lambda c: send_sum(CROSS, c))
    backward_products(BEHIND)
    send_sum(BEHIND, 0)

    @pl.when(ahead_near)
    def _():
        for c in range(straight, blocks):
            send_side_early(c)

    backward_products(AHEAD)
    send_joint(0)

    @pl.when(jnp.logical_not(ahead_near))
    def _():
        for c in range(straight, blocks):
            send_side_late(c)

    for c in range(1, straight):
        send_sum(BEHIND, c)
        send_joint(c)
    backward_products(PAIR)
    loop(0, blocks, lambda c: send_sum(PAIR, c))
    backward_products(OWN)

    gw[...] = jnp.zeros_like(gw)

    def g_copy(way, b, landed):
        piece = gg.at[rows(b), ocols(me)]
        return remote(piece, piece, zs.at[way], landed, {"feat": (inner, other)[way]})

    def g_wait(b):
        piece = gg.at[rows(b), pl.ds(0, (half if b in passing else nz - 1) * ow)]
        remote(piece, piece, zs.at[0], zr.at[b], {"feat": other}).wait_recv()

    def g_pass(b):
        for j in ends:
            piece = gg.at[rows(b), ocols(end_at(j))]
            remote(piece, piece, zl.at[0], ze.at[j - 1, b - passing.start], {"feat": other}).wait_recv()
            remote(piece, piece, zl.at[0], zr.at[b], {"feat": other}).start()

    def pass_on(some):
        @pl.when(is_inner)
        def _():
            for b in some:
                g_pass(b)

    def make_grad(b, two):
        pieces = got.at[pl.ds(0, 3 if two else 2), b]
        total = column_sum(OWN, reach, b, gp[b].astype(F32))
        remote(pieces, pieces, gs.at[0], gr.at[0, b], owner_at(PAIR)).wait_recv()
        for role in (PAIR, AHEAD, BEHIND)[: 3 if two else 2]:
            total = total + got[role, b].astype(F32)
        grad = total.astype(BF)
        gg[rows(b), ocols(me)] = grad

        @pl.when(is_inner)
        def _():
            g_copy(1, b, zr.at[b]).start()

        if half > 1:
            @pl.when(jnp.logical_not(is_inner))
            def _():
                passes = (b >= passing.start) & (b < passing.stop)

                @pl.when(passes)
                def _():
                    g_copy(0, b, ze.at[mine - 1, b - passing.start]).start()

                @pl.when(jnp.logical_not(passes))
                def _():
                    g_copy(1, b, zr.at[b]).start()
                    g_copy(0, b, zr.at[b]).start()

                x_wait(b)

        gw[...] += lax.dot_general(xg[rows(b), :], grad, (((0,), (0,)), ((), ())), preferred_element_type=F32)

    def gx_down(j, b):
        return remote(ge.at[j - 1, b], gx.at[rows(b), :], ges.at[j - 1], ger.at[0], {"feat": end_at(j)})

    def turn_weight():
        w_swap(False).wait_recv()
        for j in range(half):
            wt[:, pl.ds(j * width, width)] = wg[xcols(end_at(j)), :].T

    def finish(b):
        @pl.when(is_inner)
        def _():
            g_wait(b)
            grads = jnp.dot(gg[rows(b), :], wt[...], preferred_element_type=F32).astype(BF)
            for j in ends:
                ge[j - 1, b] = grads[:, j * width : (j + 1) * width]
                gx_down(j, b).start()
            gx[rows(b), :] = grads[:, :width]

    @pl.when(is_inner)
    def _():
        turn_weight()

    waiting = list(range(straight, blocks))
    for c in range(blocks):
        for later in waiting[c : c + 1]:
            send_near(later)
        make_grad(c, c < straight)

    gwb[...] = gw[...].astype(BF)
    height = gw.shape[0]
    for stage in range(stages):
        size = factors[stage]
        chunk = height // size
        src, buf, out = gwb if stage == 0 else summed[stage - 1], gathered[stage], summed[stage]
        rs_s, rs_r, ag_s, ag_r = psems[4 * stage : 4 * stage + 4]

        def part(q):
            return pl.ds(pl.multiple_of(q * chunk, chunk), chunk)

        steps = range(1, size)
        if stage == 0 and size % 4 == 0 and size >= 8:
            near_step = 2 * (1 - 2 * lax.rem(chip, 2))
            hops = [-near_step, near_step] + [2 * h for h in range(2, size // 2 - 1)]
            steps = [lax.rem(h + t + size, size) for h in hops for t in (0, turn)] + [lax.rem(turn + size, size)]
        for step in steps:
            _, there, peer = stage_peer(stage, step)
            remote(src.at[part(there), :], buf.at[step - 1], rs_s.at[0], rs_r.at[0], {"blk": peer}).start()
        if stage == 0:
            for b in range(passing.start):
                finish(b)
            pass_on(passing)
        digit, _, _ = stage_peer(stage, 1)
        if stage == 0:
            total = gw[part(digit), :]
        else:
            total = src[part(digit), :].astype(F32)
        remote(buf, buf, rs_s.at[0], rs_r.at[0], owner_at(PAIR)).wait_recv()
        for step in range(1, size):
            total = total + buf[step - 1].astype(F32)
        out[part(digit), :] = total.astype(BF)
        for step in steps:
            _, _, peer = stage_peer(stage, step)
            piece = out.at[part(digit), :]
            remote(piece, piece, ag_s.at[0], ag_r.at[0], {"blk": peer}).start()
        if stage == 0:
            late = list(range(passing.stop, blocks))
            for b in passing:
                finish(b)
                if b != passing.start and late:
                    finish(late.pop(0))
            for b in late:
                finish(b)
        piece = out.at[pl.ds(0, height - chunk), :]
        remote(piece, piece, ag_s.at[0], ag_r.at[0], owner_at(PAIR)).wait_recv()
    gw[...] = (summed[-1] if stages else gwb)[...].astype(F32)

    for stage in range(stages):
        buf, out = gathered[stage], summed[stage]
        rs_s, rs_r, ag_s, ag_r = psems[4 * stage : 4 * stage + 4]
        remote(buf, buf, rs_s.at[0], rs_r.at[0], owner_at(PAIR)).wait_send()
        piece = out.at[pl.ds(0, height - height // factors[stage]), :]
        remote(piece, piece, ag_s.at[0], ag_r.at[0], owner_at(PAIR)).wait_send()

    def sent_all(ref, sem):
        remote(ref, ref, sem, ger.at[0], owner_at(PAIR)).wait_send()

    @pl.when(is_inner)
    def _():
        sent_all(x, xs.at[1])
        sent_all(gg.at[:, ocols(me)], zs.at[1])
        if half > 1 and passing:
            sent_all(gg.at[pl.ds(0, len(passing) * side), pl.ds(0, (half - 1) * ow)], zl.at[0])
        for j in ends:
            sent_all(pe.at[j - 1], es.at[j - 1])
            sent_all(ge.at[j - 1], ges.at[j - 1])
            sent_all(xg.at[:, pl.ds(0, (nz - 1) * width)], xb.at[j - 1])

    @pl.when(jnp.logical_not(is_inner))
    def _():
        sent_all(x, xs.at[1])
        sent_all(x, xs.at[0])
        sent_all(gg.at[pl.ds(0, (blocks - len(passing)) * side), ocols(me)], zs.at[1])
        sent_all(gg.at[:, ocols(me)], zs.at[0])
        remote(gx, gx, ges.at[0], ger.at[0], {"feat": inner}).wait_recv()

    sent_all(got.at[pl.ds(0, 4)], hs.at[0])
    sent_all(got.at[pl.ds(0, 4)], gs.at[0])

    @pl.when(is_inner)
    def _():
        w_swap(True).wait_send()
        for j in ends if group > 1 else ():
            sent_all(w_rest(j), ws.at[j])

    @pl.when(jnp.logical_not(is_inner))
    def _():
        if half > 1:
            w_up().wait_send()


def write_out(*refs):
    count = (len(refs) - 1) // 2
    done = refs[-1]
    copies = [pltpu.make_async_copy(refs[i], refs[count + i], done.at[i]) for i in range(count)]
    for copy in copies:
        copy.start()
    for copy in copies:
        copy.wait()


def on_device(nb, nz, x, w, tv, tr, tc, cnt, go):
    offs, slots, side = tv.shape[1], tv.shape[2], tv.shape[-1]
    height, width = x.shape
    blocks = height // side
    depth, ow = w.shape
    factors = stage_factors(nb, depth)
    dims = (nb, nz, offs, slots, blocks, side, width, ow, tuple(factors))
    spare = max(nz // 2 - 1, 1)
    vmem = pl.BlockSpec(memory_space=pltpu.VMEM)
    hbm = pl.BlockSpec(memory_space=pltpu.HBM)
    dma = pltpu.SemaphoreType.DMA
    psems = []
    for f in factors:
        psems += [dma((1,))] * 4
    block = (side, ow)
    results = pl.pallas_call(
        functools.partial(layer_kernel, dims),
        out_shape=(
            pltpu.VMEM((height, ow), BF),
            pltpu.VMEM((height, width), BF),
            pltpu.VMEM((depth, ow), F32),
        ),
        in_specs=[hbm] * 7,
        out_specs=(vmem, vmem, vmem),
        scratch_shapes=[
            pltpu.SMEM((offs, 1, slots), tr.dtype),
            pltpu.SMEM((offs, 1, slots), tc.dtype),
            pltpu.SMEM(cnt.shape, cnt.dtype),
            pltpu.VMEM((height, nz * width), BF),
            pltpu.VMEM((depth, nz * ow), BF),
            pltpu.VMEM((offs, slots, side, side), BF),
            pltpu.VMEM((height, ow), BF),
            pltpu.VMEM((offs, slots, side, side), BF),
            pltpu.VMEM((offs, slots, *block), F32),
            pltpu.VMEM((blocks, *block), F32),
            pltpu.VMEM((blocks, *block), BF),
            pltpu.VMEM((offs, blocks, *block), BF),
            pltpu.VMEM((offs, blocks, *block), BF),
            pltpu.VMEM((height, nz * ow), BF),
            pltpu.VMEM((depth, ow), BF),
            pltpu.VMEM((spare, blocks, *block), BF),
            pltpu.VMEM((spare, blocks, side, width), BF),
            pltpu.VMEM((nz * ow, nz // 2 * width), BF),
        ]
        + [pltpu.VMEM((blocks, *block), BF)] * 5
        + [pltpu.VMEM((f - 1, depth // f, ow), BF) for f in factors]
        + [pltpu.VMEM((depth, ow), BF) for f in factors]
        + [dma((2,)), dma((blocks,)), dma((spare,))]
        + [dma((1,)), dma((blocks,)), dma((2, blocks)), dma((2,))]
        + [dma((1,)), dma((2, blocks)), dma((max(blocks - 3, 1),))]
        + [dma((2,)), dma((blocks,)), dma((1,)), dma((spare, max(blocks - 4, 1)))]
        + [dma((spare,)), dma((spare,)), dma((1,))]
        + [dma((spare + 1,)), dma((spare, 2)), dma((1,)), dma((1,)), dma((7,))]
        + psems,
        compiler_params=pltpu.CompilerParams(
            collective_id=0, has_side_effects=True, vmem_limit_bytes=32 * 1024 * 1024
        ),
    )(*[pltpu.with_memory_space_constraint(a, pltpu.HBM) for a in (x, w, tv, jnp.swapaxes(tr, 0, 1), jnp.swapaxes(tc, 0, 1), cnt, go)])
    return pl.pallas_call(
        write_out,
        out_shape=tuple(jax.ShapeDtypeStruct(r.shape, r.dtype) for r in results),
        in_specs=[vmem] * len(results),
        out_specs=(hbm,) * len(results),
        scratch_shapes=[dma((len(results),))],
    )(*[pltpu.with_memory_space_constraint(r, pltpu.VMEM) for r in results])


def solution(mesh):
    return jax.shard_map(
        functools.partial(on_device, mesh.shape["blk"], mesh.shape["feat"]),
        mesh=mesh,
        in_specs=(
            P("blk", "feat"),
            P(None, "feat"),
            P("blk", None, None, None, None),
            P("blk", None, None),
            P("blk", None, None),
            P("blk", None),
            P("blk", "feat"),
        ),
        out_specs=(P("blk", "feat"), P("blk", "feat"), P(None, "feat")),
        check_vma=False,
    )
```

```python
import functools

import jax
import jax.numpy as jnp
from jax import lax
from jax.experimental import pallas as pl
from jax.experimental.pallas import tpu as pltpu
from jax.sharding import PartitionSpec as P

MESH = pl.DeviceIdType.MESH
BF = jnp.bfloat16
F32 = jnp.float32


def stage_factors(count, rows):
    factors = []
    while count > 1:
        size = max(f for f in range(2, 17) if count % f == 0 and rows % (16 * f) == 0)
        factors.append(size)
        count //= size
    return factors


def remote(src, dst, send, recv, where):
    return pltpu.make_async_remote_copy(
        src_ref=src, dst_ref=dst, send_sem=send, recv_sem=recv, device_id=where, device_id_type=MESH
    )


def layer_kernel(
    dims, x, w_in, tv_in, tr_in, tc_in, cnt_in, go_in, y, gx, gw,
    tr, tc, cnt, xg, wg, tv, go, tt, prod, acc, gp, sent, got, gg, gwb, pe, ge, wt, *rest
):
    nb, nz, offs, slots, blocks, side, width, ow, factors = dims
    stages = len(factors)
    hid, hid_two, rest = rest[:3], rest[3:5], rest[5:]
    gathered, summed = rest[:stages], rest[stages : 2 * stages]
    (xs, xr, xb, hs, hr, hf, hall, gs, gr, gy, zs, zr, zl, ze, es, ges, ger, ws, wr, ks, kr, near) = rest[2 * stages : 2 * stages + 22]
    psems = rest[2 * stages + 22 :]
    reach = (offs - 1) // 2
    half = nz // 2
    me = lax.axis_index("feat")
    own = lax.axis_index("blk")
    core = lax.rem(own, 2)
    turn = 1 - 2 * core
    OWN, PAIR, CROSS, AHEAD, BEHIND = range(5)
    lean = (0, 1, -1, 2, -2)
    lower = me < half
    inner = jnp.where(lower, half - 1, half)
    other = nz - 1 - inner
    is_inner = me == inner
    ends = range(1, half)
    mine = jnp.where(lower, half - 1 - me, me - half)
    straight = min(2, blocks)
    wound = min(blocks // 2, blocks)
    passing = range(min(2, blocks), max(blocks - 2, 2))
    last = blocks - 1

    def end_at(j):
        return jnp.where(lower, half - 1 - j, half + j)

    def offset_of(role):
        return reach + lean[role] * turn

    def owner_at(role):
        return {"blk": lax.rem(own + lean[role] * turn + nb, nb)}

    chip = own // 2
    ahead_near = lax.rem(chip + own, 2) == 0
    near_role = jnp.where(ahead_near, AHEAD, BEHIND)
    far_role = AHEAD + BEHIND - near_role
    near_lean = jnp.where(ahead_near, lean[AHEAD], lean[BEHIND]) * turn
    near_owner = {"blk": lax.rem(own + near_lean + nb, nb)}
    skip = 2 * lean[AHEAD] * (2 * lax.rem(chip, 2) - 1)
    side_owner = {"blk": lax.rem(own + skip + nb, nb)}
    side_source = {"blk": lax.rem(own - skip + nb, nb)}

    def rows(b):
        return pl.ds(pl.multiple_of(b * side, side), side)

    def xcols(z):
        return pl.ds(pl.multiple_of(z * width, width), width)

    def ocols(z):
        return pl.ds(pl.multiple_of(z * ow, ow), ow)

    local = [
        pltpu.make_async_copy(w_in, wg.at[:, ocols(me)], near.at[0]),
        pltpu.make_async_copy(x, xg.at[:, xcols(me)], near.at[1]),
        pltpu.make_async_copy(tv_in.at[0], tv, near.at[2]),
        pltpu.make_async_copy(go_in, go, near.at[3]),
        pltpu.make_async_copy(tr_in, tr, near.at[4]),
        pltpu.make_async_copy(tc_in, tc, near.at[5]),
        pltpu.make_async_copy(cnt_in, cnt, near.at[6]),
    ]
    for copy in local:
        copy.start()

    def stage_peer(stage, step):
        stride = 1
        for f in factors[:stage]:
            stride *= f
        size = factors[stage]
        digit = lax.rem(own // stride, size)
        there = lax.rem(digit + step, size)
        return digit, there, own + (there - digit) * stride

    barrier = pltpu.get_barrier_semaphore()
    greeted = 0
    for step in range(1, nz):
        pl.semaphore_signal(barrier, inc=1, device_id={"feat": lax.rem(me + step, nz)}, device_id_type=MESH)
        greeted += 1
    around = [owner_at(PAIR), owner_at(AHEAD), owner_at(BEHIND), side_owner, side_source]
    for peer in around if stages > 1 else ():
        pl.semaphore_signal(barrier, inc=1, device_id=peer, device_id_type=MESH)
        greeted += 1
    for stage in range(stages):
        for step in range(1, factors[stage]):
            _, _, peer = stage_peer(stage, step)
            pl.semaphore_signal(barrier, inc=1, device_id={"blk": peer}, device_id_type=MESH)
            greeted += 1
    pl.semaphore_wait(barrier, greeted)

    depth = w_in.shape[0]

    group = factors[0] if stages else 1

    def part_of(digit):
        return pl.ds(pl.multiple_of(digit * (depth // group), depth // group), depth // group)

    my_part = part_of(stage_peer(0, 0)[0] if stages else 0)

    def x_copy(way, b):
        return remote(
            x.at[rows(b), :], xg.at[rows(b), xcols(me)], xs.at[way], xr.at[b], {"feat": (inner, other)[way]}
        )

    def x_own(j, b):
        piece = xg.at[rows(b), xcols(me)]
        return remote(x.at[rows(b), :], piece, xb.at[j - 1], xr.at[b], {"feat": end_at(j)})

    def x_back(s, e, j, b):
        piece = xg.at[rows(b), xcols(s)]
        return remote(piece, piece, xb.at[j - 1], xr.at[b], {"feat": e})

    def x_wait(b):
        piece = xg.at[rows(b), pl.ds(0, (nz - 1) * width)]
        remote(piece, piece, xs.at[0], xr.at[b], {"feat": other}).wait_recv()

    def w_up():
        return remote(w_in.at[my_part, :], wg.at[my_part, ocols(me)], ws.at[0], wr.at[mine - 1, 0], {"feat": inner})

    def w_around(j):
        piece = wg.at[my_part, ocols(end_at(j))]
        remote(piece, piece, ws.at[j], wr.at[j - 1, 0], owner_at(PAIR)).wait_recv()
        for step in range(1, group):
            peer = {"blk": stage_peer(0, step)[2]}
            remote(piece, piece, ws.at[j], wr.at[j - 1, 1], peer).start()

    def w_rest(j):
        return wg.at[pl.ds(0, depth - depth // group), ocols(end_at(j))]

    def w_wait(j):
        if group > 1:
            remote(w_rest(j), w_rest(j), ws.at[j], wr.at[j - 1, 1], owner_at(PAIR)).wait_recv()

    def w_swap(sending):
        there = jnp.where(lower, half, 0)
        here = half - there
        r, c = (there, here) if sending else (here, there)
        piece = wg.at[
            pl.ds(pl.multiple_of(r * width, width), half * width), pl.ds(pl.multiple_of(c * ow, ow), half * ow)
        ]
        return remote(piece, piece, ks.at[0], kr.at[0], {"feat": other})

    @pl.when(is_inner)
    def _():
        for b in range(min(6, blocks)):
            x_copy(1, b).start()
            for j in ends:
                x_own(j, b).start()

    @pl.when(jnp.logical_not(is_inner))
    def _():
        for b in range(blocks):
            x_copy(1, b).start()
            if b == 0 and half > 1:
                w_up().start()
            x_copy(0, b).start()

    for copy in local[:3]:
        copy.wait()

    def by_side(run):
        pl.when(ahead_near)(functools.partial(run, 0))
        pl.when(jnp.logical_not(ahead_near))(functools.partial(run, 1))

    def hid_pair(b):
        return remote(hid[OWN].at[b], hid[PAIR].at[b], hs.at[0], hall.at[0], owner_at(PAIR))

    def hid_straight(role, b):
        slot = int(role == AHEAD)
        return remote(hid[OWN].at[b], hid_two[slot].at[b], hs.at[0], hf.at[slot, b], owner_at(role))

    def hid_near(near, b):
        return remote(hid[OWN].at[b], hid_two[1 - near].at[b], hs.at[0], hf.at[1 - near, b], near_owner)

    def hid_side(near, b):
        return remote(hid_two[near].at[b], hid_two[1 - near].at[b], hs.at[0], hf.at[1 - near, b], side_source)

    def hid_passed(b):
        return remote(hid_two[0].at[b], hid[CROSS].at[b], hs.at[0], hall.at[1], owner_at(PAIR))

    def hid_landed(slot, b):
        piece = hid_two[slot].at[b]
        remote(piece, piece, hs.at[0], hf.at[slot, b], owner_at(PAIR)).wait_recv()

    def hid_whole(role):
        remote(hid[role], hid[role], hs.at[0], hall.at[int(role == CROSS)], owner_at(PAIR)).wait_recv()

    def take_near(b):
        def run(near):
            hid_landed(near, b)
            hid_side(near, b).start()
            if near == 0:
                hid_passed(b).start()

        by_side(run)

    def take_far(b):
        def run(near):
            hid_landed(1 - near, b)
            if near == 1:
                hid_passed(b).start()

        by_side(run)

    def hid_down(j, b):
        return remote(pe.at[j - 1, b], hid[OWN].at[b], es.at[j - 1], hr.at[b], {"feat": end_at(j)})

    def spread(b):
        hid_pair(b).start()

        @pl.when(b < wound)
        def _():
            by_side(lambda near: hid_near(near, b).start())

        @pl.when(b >= wound)
        def _():
            hid_straight(AHEAD, b).start()

        @pl.when(b >= wound)
        def _():
            hid_straight(BEHIND, b).start()

    def hidden_of(z, b):
        return jnp.dot(xg[rows(b), :], wg[:, ocols(z)], preferred_element_type=F32).astype(BF)

    def serve_ends(b):
        for j in ends:
            pe[j - 1, b] = hidden_of(end_at(j), b)
            hid_down(j, b).start()

    lag = min(4, blocks)
    first = min(2, blocks - 1)

    def forward_step(b, carry):
        @pl.when(is_inner)
        def _():
            @pl.when(b + 6 < blocks)
            def _():
                x_copy(1, b + 6).start()
                for j in ends:
                    x_own(j, b + 6).start()

        per_block = slots // blocks
        for role in range(offs):
            for s in range(per_block):
                slot = b * per_block + s
                tt[role, slot] = tv[offset_of(role), slot].T

        @pl.when(is_inner)
        def _():
            x_wait(b)

            @pl.when(b > first)
            def _():
                serve_ends(b)

            hid[OWN][b] = hidden_of(me, b)
            spread(b)

            @pl.when(b == first)
            def _():
                for j in ends:
                    w_wait(j)
                for early in range(first + 1):
                    serve_ends(early)

        @pl.when(jnp.logical_not(is_inner))
        def _():
            remote(hid[OWN].at[b], hid[OWN].at[b], es.at[0], hr.at[b], {"feat": inner}).wait_recv()
            spread(b)

        @pl.when(b >= lag)
        def _():
            take_near(b - lag)

        return carry

    @pl.when(is_inner)
    def _():
        for j in ends:
            w_around(j)

    lax.fori_loop(0, blocks, forward_step, 0)

    @pl.when(is_inner)
    def _():
        w_swap(True).start()
        for j in ends:
            for b in range(blocks):
                for step in range(1, nz):
                    s = lax.rem(me + step, nz)

                    @pl.when(s != end_at(j))
                    def _():
                        x_back(s, end_at(j), j, b).start()

    for copy in local[4:]:
        copy.wait()

    def forward_products(role):
        k = offset_of(role)
        for s in range(slots):
            c = tc[k, 0, s]
            source = (hid[role] if role < AHEAD else hid_two[role - AHEAD])[c]
            prod[role, s] = jnp.dot(tv[k, s], source, preferred_element_type=F32)

    def weight_of(table, k, s, b):
        return jnp.where((table[k, 0, s] == b) & (s < cnt[0, k]), 1.0, 0.0).astype(F32)

    def row_sum(role, b, total):
        for s in range(slots):
            total = total + prod[role, s] * weight_of(tr, offset_of(role), s, b)
        return total

    def gather_role(role):
        forward_products(role)

        def add(b, carry):
            start = hid[OWN][b].astype(F32) if role == OWN else acc[b]
            acc[b] = row_sum(role, b, start)
            return carry

        lax.fori_loop(0, blocks, add, 0)

    for b in range(blocks - lag, wound):
        take_near(b)
    gather_role(OWN)
    hid_whole(PAIR)
    gather_role(PAIR)
    for b in range(wound):
        take_far(b)
    for b in range(wound, blocks):
        hid_landed(0, b)
        hid_passed(b).start()
    gather_role(AHEAD)
    for b in range(wound, blocks):
        hid_landed(1, b)
    gather_role(BEHIND)
    local[3].wait()
    hid_whole(CROSS)
    forward_products(CROSS)

    def pointwise(b, carry):
        v = row_sum(CROSS, b, acc[b])
        sigma = jax.nn.sigmoid(v)
        y[rows(b), :] = (v * sigma).astype(BF)
        slope = sigma * (1.0 + v * (1.0 - sigma))
        gp[b] = (go[rows(b), :].astype(F32) * slope).astype(BF)
        return carry

    lax.fori_loop(0, blocks, pointwise, 0)

    def backward_products(role):
        for s in range(slots):
            prod[role, s] = jnp.dot(tt[role, s], gp[tr[offset_of(role), 0, s]], preferred_element_type=F32)

    def column_sum(role, offset, c, start):
        total = start
        for s in range(slots):
            term = prod[role, s] * weight_of(tc, offset, s, c)
            total = term if total is None else total + term
        return total

    target = {PAIR: PAIR, CROSS: PAIR, AHEAD: AHEAD, BEHIND: BEHIND}
    arrives = {PAIR: PAIR, CROSS: CROSS, AHEAD: BEHIND, BEHIND: AHEAD}

    def sum_copy(role, c):
        return remote(
            sent.at[role, c], got.at[arrives[role], c], gs.at[0], gr.at[int(role == CROSS), c], owner_at(target[role])
        )

    def cross_wait(c):
        piece = got.at[CROSS, c]
        remote(piece, piece, gs.at[0], gr.at[1, c], owner_at(PAIR)).wait_recv()

    def send_sum(role, c):
        sent[role, c] = column_sum(role, offset_of(role), c, None).astype(BF)
        sum_copy(role, c).start()

    def send_joint(c):
        cross_wait(c)
        start = got[CROSS, c].astype(F32)
        sent[AHEAD, c] = column_sum(AHEAD, offset_of(AHEAD), c, start).astype(BF)
        sum_copy(AHEAD, c).start()

    def side_copy(c):
        return remote(sent.at[far_role, c], got.at[OWN, c], gs.at[0], gy.at[c - straight], side_owner)

    def send_side_early(c):
        sent[BEHIND, c] = column_sum(BEHIND, offset_of(BEHIND), c, None).astype(BF)
        side_copy(c).start()

    def send_side_late(c):
        cross_wait(c)
        start = got[CROSS, c].astype(F32)
        sent[AHEAD, c] = column_sum(AHEAD, offset_of(AHEAD), c, start).astype(BF)
        side_copy(c).start()

    crossing_near = jnp.where(ahead_near, 1.0, 0.0).astype(F32)

    def send_near(c):
        @pl.when(ahead_near)
        def _():
            cross_wait(c)

        start = got[CROSS, c].astype(F32) * crossing_near
        total = column_sum(near_role, reach + near_lean, c, start)
        piece = got.at[OWN, c]
        remote(piece, piece, gs.at[0], gy.at[c - straight], side_owner).wait_recv()
        sent[near_role, c] = (total + got[OWN, c].astype(F32)).astype(BF)
        remote(sent.at[near_role, c], got.at[AHEAD, c], gs.at[0], gr.at[0, c], near_owner).start()

    def loop(low, high, step):
        def body(c, carry):
            step(c)
            return carry

        lax.fori_loop(low, high, body, 0)

    backward_products(CROSS)
    loop(0, blocks, lambda c: send_sum(CROSS, c))
    backward_products(BEHIND)
    send_sum(BEHIND, 0)

    @pl.when(ahead_near)
    def _():
        for c in range(straight, blocks):
            send_side_early(c)

    backward_products(AHEAD)
    send_joint(0)

    @pl.when(jnp.logical_not(ahead_near))
    def _():
        for c in range(straight, blocks):
            send_side_late(c)

    for c in range(1, straight):
        send_sum(BEHIND, c)
        send_joint(c)
    backward_products(PAIR)
    loop(0, blocks, lambda c: send_sum(PAIR, c))
    backward_products(OWN)

    gw[...] = jnp.zeros_like(gw)

    def g_copy(way, b, landed):
        piece = gg.at[rows(b), ocols(me)]
        return remote(piece, piece, zs.at[way], landed, {"feat": (inner, other)[way]})

    def g_wait(b):
        piece = gg.at[rows(b), pl.ds(0, (half if b in passing else nz - 1) * ow)]
        remote(piece, piece, zs.at[0], zr.at[b], {"feat": other}).wait_recv()

    def g_pass(b):
        for j in ends:
            piece = gg.at[rows(b), ocols(end_at(j))]
            remote(piece, piece, zl.at[0], ze.at[j - 1, b - passing.start], {"feat": other}).wait_recv()
            remote(piece, piece, zl.at[0], zr.at[b], {"feat": other}).start()

    def pass_on(some):
        @pl.when(is_inner)
        def _():
            for b in some:
                g_pass(b)

    def make_grad(b, two):
        pieces = got.at[pl.ds(0, 3 if two else 2), b]
        total = column_sum(OWN, reach, b, gp[b].astype(F32))
        remote(pieces, pieces, gs.at[0], gr.at[0, b], owner_at(PAIR)).wait_recv()
        for role in (PAIR, AHEAD, BEHIND)[: 3 if two else 2]:
            total = total + got[role, b].astype(F32)
        grad = total.astype(BF)
        gg[rows(b), ocols(me)] = grad

        @pl.when(is_inner)
        def _():
            g_copy(1, b, zr.at[b]).start()

        if half > 1:
            @pl.when(jnp.logical_not(is_inner))
            def _():
                passes = (b >= passing.start) & (b < passing.stop)

                @pl.when(passes)
                def _():
                    g_copy(0, b, ze.at[mine - 1, b - passing.start]).start()

                @pl.when(jnp.logical_not(passes))
                def _():
                    g_copy(1, b, zr.at[b]).start()
                    g_copy(0, b, zr.at[b]).start()

                x_wait(b)

        gw[...] += lax.dot_general(xg[rows(b), :], grad, (((0,), (0,)), ((), ())), preferred_element_type=F32)

    def gx_down(j, b):
        return remote(ge.at[j - 1, b], gx.at[rows(b), :], ges.at[j - 1], ger.at[0], {"feat": end_at(j)})

    def turn_weight():
        w_swap(False).wait_recv()
        for j in range(half):
            wt[:, pl.ds(j * width, width)] = wg[xcols(end_at(j)), :].T

    def finish(b):
        @pl.when(is_inner)
        def _():
            g_wait(b)
            grads = jnp.dot(gg[rows(b), :], wt[...], preferred_element_type=F32).astype(BF)
            for j in ends:
                ge[j - 1, b] = grads[:, j * width : (j + 1) * width]
                gx_down(j, b).start()
            gx[rows(b), :] = grads[:, :width]

    @pl.when(is_inner)
    def _():
        turn_weight()

    waiting = list(range(straight, blocks))
    for c in range(blocks):
        for later in waiting[c : c + 1]:
            send_near(later)
        make_grad(c, c < straight)

    gwb[...] = gw[...].astype(BF)
    height = gw.shape[0]
    for stage in range(stages):
        size = factors[stage]
        chunk = height // size
        src, buf, out = gwb if stage == 0 else summed[stage - 1], gathered[stage], summed[stage]
        rs_s, rs_r, ag_s, ag_r = psems[4 * stage : 4 * stage + 4]

        def part(q):
            return pl.ds(pl.multiple_of(q * chunk, chunk), chunk)

        steps = range(1, size)
        if stage == 0 and size % 4 == 0 and size >= 8:
            near_step = 2 * (1 - 2 * lax.rem(chip, 2))
            hops = [-near_step, near_step] + [2 * h for h in range(2, size // 2 - 1)]
            steps = [lax.rem(h + t + size, size) for h in hops for t in (0, turn)] + [lax.rem(turn + size, size)]
        for step in steps:
            _, there, peer = stage_peer(stage, step)
            remote(src.at[part(there), :], buf.at[step - 1], rs_s.at[0], rs_r.at[0], {"blk": peer}).start()
        if stage == 0:
            for b in range(passing.start):
                finish(b)
            pass_on(passing)
        digit, _, _ = stage_peer(stage, 1)
        if stage == 0:
            total = gw[part(digit), :]
        else:
            total = src[part(digit), :].astype(F32)
        remote(buf, buf, rs_s.at[0], rs_r.at[0], owner_at(PAIR)).wait_recv()
        for step in range(1, size):
            total = total + buf[step - 1].astype(F32)
        out[part(digit), :] = total.astype(BF)
        for step in steps:
            _, _, peer = stage_peer(stage, step)
            piece = out.at[part(digit), :]
            remote(piece, piece, ag_s.at[0], ag_r.at[0], {"blk": peer}).start()
        if stage == 0:
            late = list(range(passing.stop, blocks))
            for b in passing:
                finish(b)
                if b != passing.start and late:
                    finish(late.pop(0))
            for b in late:
                finish(b)
        piece = out.at[pl.ds(0, height - chunk), :]
        remote(piece, piece, ag_s.at[0], ag_r.at[0], owner_at(PAIR)).wait_recv()
    gw[...] = (summed[-1] if stages else gwb)[...].astype(F32)

    for stage in range(stages):
        buf, out = gathered[stage], summed[stage]
        rs_s, rs_r, ag_s, ag_r = psems[4 * stage : 4 * stage + 4]
        remote(buf, buf, rs_s.at[0], rs_r.at[0], owner_at(PAIR)).wait_send()
        piece = out.at[pl.ds(0, height - height // factors[stage]), :]
        remote(piece, piece, ag_s.at[0], ag_r.at[0], owner_at(PAIR)).wait_send()

    def sent_all(ref, sem):
        remote(ref, ref, sem, ger.at[0], owner_at(PAIR)).wait_send()

    @pl.when(is_inner)
    def _():
        sent_all(x, xs.at[1])
        sent_all(gg.at[:, ocols(me)], zs.at[1])
        if half > 1 and passing:
            sent_all(gg.at[pl.ds(0, len(passing) * side), pl.ds(0, (half - 1) * ow)], zl.at[0])
        for j in ends:
            sent_all(pe.at[j - 1], es.at[j - 1])
            sent_all(ge.at[j - 1], ges.at[j - 1])
            sent_all(xg.at[:, pl.ds(0, (nz - 1) * width)], xb.at[j - 1])

    @pl.when(jnp.logical_not(is_inner))
    def _():
        sent_all(x, xs.at[1])
        sent_all(x, xs.at[0])
        sent_all(gg.at[pl.ds(0, (blocks - len(passing)) * side), ocols(me)], zs.at[1])
        sent_all(gg.at[:, ocols(me)], zs.at[0])
        remote(gx, gx, ges.at[0], ger.at[0], {"feat": inner}).wait_recv()

    sent_all(got.at[pl.ds(0, 4)], hs.at[0])
    sent_all(got.at[pl.ds(0, 4)], gs.at[0])

    @pl.when(is_inner)
    def _():
        w_swap(True).wait_send()
        for j in ends if group > 1 else ():
            sent_all(w_rest(j), ws.at[j])

    @pl.when(jnp.logical_not(is_inner))
    def _():
        if half > 1:
            w_up().wait_send()


def write_out(*refs):
    count = (len(refs) - 1) // 2
    done = refs[-1]
    copies = [pltpu.make_async_copy(refs[i], refs[count + i], done.at[i]) for i in range(count)]
    for copy in copies:
        copy.start()
    for copy in copies:
        copy.wait()


def on_device(nb, nz, x, w, tv, tr, tc, cnt, go):
    offs, slots, side = tv.shape[1], tv.shape[2], tv.shape[-1]
    height, width = x.shape
    blocks = height // side
    depth, ow = w.shape
    factors = stage_factors(nb, depth)
    dims = (nb, nz, offs, slots, blocks, side, width, ow, tuple(factors))
    spare = max(nz // 2 - 1, 1)
    vmem = pl.BlockSpec(memory_space=pltpu.VMEM)
    hbm = pl.BlockSpec(memory_space=pltpu.HBM)
    dma = pltpu.SemaphoreType.DMA
    psems = []
    for f in factors:
        psems += [dma((1,))] * 4
    block = (side, ow)
    results = pl.pallas_call(
        functools.partial(layer_kernel, dims),
        out_shape=(
            pltpu.VMEM((height, ow), BF),
            pltpu.VMEM((height, width), BF),
            pltpu.VMEM((depth, ow), F32),
        ),
        in_specs=[hbm] * 7,
        out_specs=(vmem, vmem, vmem),
        scratch_shapes=[
            pltpu.SMEM((offs, 1, slots), tr.dtype),
            pltpu.SMEM((offs, 1, slots), tc.dtype),
            pltpu.SMEM(cnt.shape, cnt.dtype),
            pltpu.VMEM((height, nz * width), BF),
            pltpu.VMEM((depth, nz * ow), BF),
            pltpu.VMEM((offs, slots, side, side), BF),
            pltpu.VMEM((height, ow), BF),
            pltpu.VMEM((offs, slots, side, side), BF),
            pltpu.VMEM((offs, slots, *block), F32),
            pltpu.VMEM((blocks, *block), F32),
            pltpu.VMEM((blocks, *block), BF),
            pltpu.VMEM((offs, blocks, *block), BF),
            pltpu.VMEM((offs, blocks, *block), BF),
            pltpu.VMEM((height, nz * ow), BF),
            pltpu.VMEM((depth, ow), BF),
            pltpu.VMEM((spare, blocks, *block), BF),
            pltpu.VMEM((spare, blocks, side, width), BF),
            pltpu.VMEM((nz * ow, nz // 2 * width), BF),
        ]
        + [pltpu.VMEM((blocks, *block), BF)] * 5
        + [pltpu.VMEM((f - 1, depth // f, ow), BF) for f in factors]
        + [pltpu.VMEM((depth, ow), BF) for f in factors]
        + [dma((2,)), dma((blocks,)), dma((spare,))]
        + [dma((1,)), dma((blocks,)), dma((2, blocks)), dma((2,))]
        + [dma((1,)), dma((2, blocks)), dma((blocks,))]
        + [dma((2,)), dma((blocks,)), dma((1,)), dma((spare, max(blocks - 4, 1)))]
        + [dma((spare,)), dma((spare,)), dma((1,))]
        + [dma((spare + 1,)), dma((spare, 2)), dma((1,)), dma((1,)), dma((7,))]
        + psems,
        compiler_params=pltpu.CompilerParams(
            collective_id=0, has_side_effects=True, vmem_limit_bytes=32 * 1024 * 1024
        ),
    )(*[pltpu.with_memory_space_constraint(a, pltpu.HBM) for a in (x, w, tv, jnp.swapaxes(tr, 0, 1), jnp.swapaxes(tc, 0, 1), cnt, go)])
    return pl.pallas_call(
        write_out,
        out_shape=tuple(jax.ShapeDtypeStruct(r.shape, r.dtype) for r in results),
        in_specs=[vmem] * len(results),
        out_specs=(hbm,) * len(results),
        scratch_shapes=[dma((len(results),))],
    )(*[pltpu.with_memory_space_constraint(r, pltpu.VMEM) for r in results])


def solution(mesh):
    return jax.shard_map(
        functools.partial(on_device, mesh.shape["blk"], mesh.shape["feat"]),
        mesh=mesh,
        in_specs=(
            P("blk", "feat"),
            P(None, "feat"),
            P("blk", None, None, None, None),
            P("blk", None, None),
            P("blk", None, None),
            P("blk", None),
            P("blk", "feat"),
        ),
        out_specs=(P("blk", "feat"), P("blk", "feat"), P(None, "feat")),
        check_vma=False,
    )
```

```python
import functools

import jax
import jax.numpy as jnp
from jax import lax
from jax.experimental import pallas as pl
from jax.experimental.pallas import tpu as pltpu
from jax.sharding import PartitionSpec as P

MESH = pl.DeviceIdType.MESH
BF = jnp.bfloat16
F32 = jnp.float32


def stage_factors(count, rows):
    factors = []
    while count > 1:
        size = max(f for f in range(2, 17) if count % f == 0 and rows % (16 * f) == 0)
        factors.append(size)
        count //= size
    return factors


def remote(src, dst, send, recv, where):
    return pltpu.make_async_remote_copy(
        src_ref=src, dst_ref=dst, send_sem=send, recv_sem=recv, device_id=where, device_id_type=MESH
    )


def layer_kernel(
    dims, x, w_in, tv_in, tr_in, tc_in, cnt_in, go_in, y, gx, gw,
    tr, tc, cnt, xg, wg, tv, go, tt, prod, acc, gp, sent, got, gg, gwb, pe, ge, wt, *rest
):
    nb, nz, offs, slots, blocks, side, width, ow, factors = dims
    stages = len(factors)
    hid, hid_two, rest = rest[:3], rest[3:5], rest[5:]
    gathered, summed = rest[:stages], rest[stages : 2 * stages]
    (xs, xr, xb, hs, hf, hall, gs, gr, gy, zs, zr, zl, ze, es, ges, ger, ws, wr, ks, kr, near) = rest[2 * stages : 2 * stages + 21]
    psems = rest[2 * stages + 21 :]
    reach = (offs - 1) // 2
    half = nz // 2
    me = lax.axis_index("feat")
    own = lax.axis_index("blk")
    core = lax.rem(own, 2)
    turn = 1 - 2 * core
    OWN, PAIR, CROSS, AHEAD, BEHIND = range(5)
    lean = (0, 1, -1, 2, -2)
    lower = me < half
    inner = jnp.where(lower, half - 1, half)
    other = nz - 1 - inner
    is_inner = me == inner
    ends = range(1, half)
    mine = jnp.where(lower, half - 1 - me, me - half)
    straight = min(2, blocks)
    wound = min(blocks // 2, blocks)
    passing = range(min(2, blocks), max(blocks - 2, 2))
    last = blocks - 1

    def end_at(j):
        return jnp.where(lower, half - 1 - j, half + j)

    def offset_of(role):
        return reach + lean[role] * turn

    def owner_at(role):
        return {"blk": lax.rem(own + lean[role] * turn + nb, nb)}

    chip = own // 2
    ahead_near = lax.rem(chip + own, 2) == 0
    near_role = jnp.where(ahead_near, AHEAD, BEHIND)
    far_role = AHEAD + BEHIND - near_role
    near_lean = jnp.where(ahead_near, lean[AHEAD], lean[BEHIND]) * turn
    near_owner = {"blk": lax.rem(own + near_lean + nb, nb)}
    skip = 2 * lean[AHEAD] * (2 * lax.rem(chip, 2) - 1)
    side_owner = {"blk": lax.rem(own + skip + nb, nb)}
    side_source = {"blk": lax.rem(own - skip + nb, nb)}

    def rows(b):
        return pl.ds(pl.multiple_of(b * side, side), side)

    def xcols(z):
        return pl.ds(pl.multiple_of(z * width, width), width)

    def ocols(z):
        return pl.ds(pl.multiple_of(z * ow, ow), ow)

    local = [
        pltpu.make_async_copy(w_in, wg.at[:, ocols(me)], near.at[0]),
        pltpu.make_async_copy(x, xg.at[:, xcols(me)], near.at[1]),
        pltpu.make_async_copy(tv_in.at[0], tv, near.at[2]),
        pltpu.make_async_copy(go_in, go, near.at[3]),
        pltpu.make_async_copy(tr_in, tr, near.at[4]),
        pltpu.make_async_copy(tc_in, tc, near.at[5]),
        pltpu.make_async_copy(cnt_in, cnt, near.at[6]),
    ]
    for copy in local:
        copy.start()

    def stage_peer(stage, step):
        stride = 1
        for f in factors[:stage]:
            stride *= f
        size = factors[stage]
        digit = lax.rem(own // stride, size)
        there = lax.rem(digit + step, size)
        return digit, there, own + (there - digit) * stride

    barrier = pltpu.get_barrier_semaphore()
    greeted = 0
    for step in range(1, nz):
        pl.semaphore_signal(barrier, inc=1, device_id={"feat": lax.rem(me + step, nz)}, device_id_type=MESH)
        greeted += 1
    around = [owner_at(PAIR), owner_at(AHEAD), owner_at(BEHIND), side_owner, side_source]
    for peer in around if stages > 1 else ():
        pl.semaphore_signal(barrier, inc=1, device_id=peer, device_id_type=MESH)
        greeted += 1
    for stage in range(stages):
        for step in range(1, factors[stage]):
            _, _, peer = stage_peer(stage, step)
            pl.semaphore_signal(barrier, inc=1, device_id={"blk": peer}, device_id_type=MESH)
            greeted += 1
    pl.semaphore_wait(barrier, greeted)

    depth = w_in.shape[0]

    group = factors[0] if stages else 1

    def part_of(digit):
        return pl.ds(pl.multiple_of(digit * (depth // group), depth // group), depth // group)

    my_part = part_of(stage_peer(0, 0)[0] if stages else 0)

    def x_copy(way, b):
        return remote(
            x.at[rows(b), :], xg.at[rows(b), xcols(me)], xs.at[way], xr.at[b], {"feat": (inner, other)[way]}
        )

    def x_own(j, b):
        piece = xg.at[rows(b), xcols(me)]
        return remote(x.at[rows(b), :], piece, xb.at[j - 1], xr.at[b], {"feat": end_at(j)})

    def x_back(s, e, j, b):
        piece = xg.at[rows(b), xcols(s)]
        return remote(piece, piece, xb.at[j - 1], xr.at[b], {"feat": e})

    def x_wait(b):
        piece = xg.at[rows(b), pl.ds(0, (nz - 1) * width)]
        remote(piece, piece, xs.at[0], xr.at[b], {"feat": other}).wait_recv()

    def w_up():
        return remote(w_in.at[my_part, :], wg.at[my_part, ocols(me)], ws.at[0], wr.at[mine - 1, 0], {"feat": inner})

    def w_around(j):
        piece = wg.at[my_part, ocols(end_at(j))]
        remote(piece, piece, ws.at[j], wr.at[j - 1, 0], owner_at(PAIR)).wait_recv()
        for step in range(1, group):
            peer = {"blk": stage_peer(0, step)[2]}
            remote(piece, piece, ws.at[j], wr.at[j - 1, 1], peer).start()

    def w_rest(j):
        return wg.at[pl.ds(0, depth - depth // group), ocols(end_at(j))]

    def w_wait(j):
        if group > 1:
            remote(w_rest(j), w_rest(j), ws.at[j], wr.at[j - 1, 1], owner_at(PAIR)).wait_recv()

    def w_swap(sending):
        there = jnp.where(lower, half, 0)
        here = half - there
        r, c = (there, here) if sending else (here, there)
        piece = wg.at[
            pl.ds(pl.multiple_of(r * width, width), half * width), pl.ds(pl.multiple_of(c * ow, ow), half * ow)
        ]
        return remote(piece, piece, ks.at[0], kr.at[0], {"feat": other})

    @pl.when(is_inner)
    def _():
        for b in range(min(6, blocks)):
            x_copy(1, b).start()
            for j in ends:
                x_own(j, b).start()

    @pl.when(jnp.logical_not(is_inner))
    def _():
        for b in range(blocks):
            x_copy(1, b).start()
            if b == 0 and half > 1:
                w_up().start()
            x_copy(0, b).start()

    for copy in local[:3]:
        copy.wait()

    def by_side(run):
        pl.when(ahead_near)(functools.partial(run, 0))
        pl.when(jnp.logical_not(ahead_near))(functools.partial(run, 1))

    def hid_pair(b):
        return remote(hid[OWN].at[b], hid[PAIR].at[b], hs.at[0], hall.at[0], owner_at(PAIR))

    def hid_straight(role, b):
        slot = int(role == AHEAD)
        return remote(hid[OWN].at[b], hid_two[slot].at[b], hs.at[0], hf.at[slot, b], owner_at(role))

    def hid_near(near, b):
        return remote(hid[OWN].at[b], hid_two[1 - near].at[b], hs.at[0], hf.at[1 - near, b], near_owner)

    def hid_side(near, b):
        return remote(hid_two[near].at[b], hid_two[1 - near].at[b], hs.at[0], hf.at[1 - near, b], side_source)

    def hid_passed(b):
        return remote(hid_two[0].at[b], hid[CROSS].at[b], hs.at[0], hall.at[1], owner_at(PAIR))

    def hid_landed(slot, b):
        piece = hid_two[slot].at[b]
        remote(piece, piece, hs.at[0], hf.at[slot, b], owner_at(PAIR)).wait_recv()

    def hid_whole(role):
        remote(hid[role], hid[role], hs.at[0], hall.at[int(role == CROSS)], owner_at(PAIR)).wait_recv()

    def take_near(b):
        def run(near):
            hid_landed(near, b)
            hid_side(near, b).start()
            if near == 0:
                hid_passed(b).start()

        by_side(run)

    def take_far(b):
        def run(near):
            hid_landed(1 - near, b)
            if near == 1:
                hid_passed(b).start()

        by_side(run)

    def hid_down(j, b):
        return remote(pe.at[j - 1, b], hid[OWN].at[b], es.at[j - 1], ze.at[0, b], {"feat": end_at(j)})

    def spread(b):
        hid_pair(b).start()

        @pl.when(b < wound)
        def _():
            by_side(lambda near: hid_near(near, b).start())

        @pl.when(b >= wound)
        def _():
            hid_straight(AHEAD, b).start()

        @pl.when(b >= wound)
        def _():
            hid_straight(BEHIND, b).start()

    def hidden_of(z, b):
        return jnp.dot(xg[rows(b), :], wg[:, ocols(z)], preferred_element_type=F32).astype(BF)

    def serve_ends(b):
        for j in ends:
            pe[j - 1, b] = hidden_of(end_at(j), b)
            hid_down(j, b).start()

    lag = min(4, blocks)
    first = min(2, blocks - 1)

    def forward_step(b, carry):
        @pl.when(is_inner)
        def _():
            @pl.when(b + 6 < blocks)
            def _():
                x_copy(1, b + 6).start()
                for j in ends:
                    x_own(j, b + 6).start()

        per_block = slots // blocks
        for role in range(offs):
            for s in range(per_block):
                slot = b * per_block + s
                tt[role, slot] = tv[offset_of(role), slot].T

        @pl.when(is_inner)
        def _():
            x_wait(b)

            @pl.when(b > first)
            def _():
                serve_ends(b)

            hid[OWN][b] = hidden_of(me, b)
            spread(b)

            @pl.when(b == first)
            def _():
                for j in ends:
                    w_wait(j)
                for early in range(first + 1):
                    serve_ends(early)

        @pl.when(jnp.logical_not(is_inner))
        def _():
            remote(hid[OWN].at[b], hid[OWN].at[b], es.at[0], ze.at[0, b], {"feat": inner}).wait_recv()
            spread(b)

        @pl.when(b >= lag)
        def _():
            take_near(b - lag)

        return carry

    @pl.when(is_inner)
    def _():
        for j in ends:
            w_around(j)

    lax.fori_loop(0, blocks, forward_step, 0)

    @pl.when(is_inner)
    def _():
        w_swap(True).start()
        for j in ends:
            for b in range(blocks):
                for step in range(1, nz):
                    s = lax.rem(me + step, nz)

                    @pl.when(s != end_at(j))
                    def _():
                        x_back(s, end_at(j), j, b).start()

    for copy in local[4:]:
        copy.wait()

    def forward_products(role):
        k = offset_of(role)
        for s in range(slots):
            c = tc[k, 0, s]
            source = (hid[role] if role < AHEAD else hid_two[role - AHEAD])[c]
            prod[role, s] = jnp.dot(tv[k, s], source, preferred_element_type=F32)

    def weight_of(table, k, s, b):
        return jnp.where((table[k, 0, s] == b) & (s < cnt[0, k]), 1.0, 0.0).astype(F32)

    def row_sum(role, b, total):
        for s in range(slots):
            total = total + prod[role, s] * weight_of(tr, offset_of(role), s, b)
        return total

    def gather_role(role):
        forward_products(role)

        def add(b, carry):
            start = hid[OWN][b].astype(F32) if role == OWN else acc[b]
            acc[b] = row_sum(role, b, start)
            return carry

        lax.fori_loop(0, blocks, add, 0)

    for b in range(blocks - lag, wound):
        take_near(b)
    gather_role(OWN)
    hid_whole(PAIR)
    gather_role(PAIR)
    for b in range(wound):
        take_far(b)
    for b in range(wound, blocks):
        hid_landed(0, b)
        hid_passed(b).start()
    gather_role(AHEAD)
    for b in range(wound, blocks):
        hid_landed(1, b)
    gather_role(BEHIND)
    local[3].wait()
    hid_whole(CROSS)
    forward_products(CROSS)

    def pointwise(b, carry):
        v = row_sum(CROSS, b, acc[b])
        sigma = jax.nn.sigmoid(v)
        y[rows(b), :] = (v * sigma).astype(BF)
        slope = sigma * (1.0 + v * (1.0 - sigma))
        gp[b] = (go[rows(b), :].astype(F32) * slope).astype(BF)
        return carry

    lax.fori_loop(0, blocks, pointwise, 0)

    def backward_products(role):
        for s in range(slots):
            prod[role, s] = jnp.dot(tt[role, s], gp[tr[offset_of(role), 0, s]], preferred_element_type=F32)

    def column_sum(role, offset, c, start):
        total = start
        for s in range(slots):
            term = prod[role, s] * weight_of(tc, offset, s, c)
            total = term if total is None else total + term
        return total

    target = {PAIR: PAIR, CROSS: PAIR, AHEAD: AHEAD, BEHIND: BEHIND}
    arrives = {PAIR: PAIR, CROSS: CROSS, AHEAD: BEHIND, BEHIND: AHEAD}

    def sum_copy(role, c):
        return remote(
            sent.at[role, c], got.at[arrives[role], c], gs.at[0], gr.at[int(role == CROSS), c], owner_at(target[role])
        )

    def cross_wait(c):
        piece = got.at[CROSS, c]
        remote(piece, piece, gs.at[0], gr.at[1, c], owner_at(PAIR)).wait_recv()

    def send_sum(role, c):
        sent[role, c] = column_sum(role, offset_of(role), c, None).astype(BF)
        sum_copy(role, c).start()

    def send_joint(c):
        cross_wait(c)
        start = got[CROSS, c].astype(F32)
        sent[AHEAD, c] = column_sum(AHEAD, offset_of(AHEAD), c, start).astype(BF)
        sum_copy(AHEAD, c).start()

    def side_copy(c):
        return remote(sent.at[far_role, c], got.at[OWN, c], gs.at[0], gy.at[c - straight], side_owner)

    def send_side_early(c):
        sent[BEHIND, c] = column_sum(BEHIND, offset_of(BEHIND), c, None).astype(BF)
        side_copy(c).start()

    def send_side_late(c):
        cross_wait(c)
        start = got[CROSS, c].astype(F32)
        sent[AHEAD, c] = column_sum(AHEAD, offset_of(AHEAD), c, start).astype(BF)
        side_copy(c).start()

    crossing_near = jnp.where(ahead_near, 1.0, 0.0).astype(F32)

    def send_near(c):
        @pl.when(ahead_near)
        def _():
            cross_wait(c)

        start = got[CROSS, c].astype(F32) * crossing_near
        total = column_sum(near_role, reach + near_lean, c, start)
        piece = got.at[OWN, c]
        remote(piece, piece, gs.at[0], gy.at[c - straight], side_owner).wait_recv()
        sent[near_role, c] = (total + got[OWN, c].astype(F32)).astype(BF)
        remote(sent.at[near_role, c], got.at[AHEAD, c], gs.at[0], gr.at[0, c], near_owner).start()

    def loop(low, high, step):
        def body(c, carry):
            step(c)
            return carry

        lax.fori_loop(low, high, body, 0)

    backward_products(CROSS)
    loop(0, blocks, lambda c: send_sum(CROSS, c))
    backward_products(BEHIND)
    send_sum(BEHIND, 0)

    @pl.when(ahead_near)
    def _():
        for c in range(straight, blocks):
            send_side_early(c)

    backward_products(AHEAD)
    send_joint(0)

    @pl.when(jnp.logical_not(ahead_near))
    def _():
        for c in range(straight, blocks):
            send_side_late(c)

    for c in range(1, straight):
        send_sum(BEHIND, c)
        send_joint(c)
    backward_products(PAIR)
    loop(0, blocks, lambda c: send_sum(PAIR, c))
    backward_products(OWN)

    gw[...] = jnp.zeros_like(gw)

    def g_copy(way, b, landed):
        piece = gg.at[rows(b), ocols(me)]
        return remote(piece, piece, zs.at[way], landed, {"feat": (inner, other)[way]})

    def g_wait(b):
        piece = gg.at[rows(b), pl.ds(0, (half if b in passing else nz - 1) * ow)]
        remote(piece, piece, zs.at[0], zr.at[b], {"feat": other}).wait_recv()

    def g_pass(b):
        for j in ends:
            piece = gg.at[rows(b), ocols(end_at(j))]
            remote(piece, piece, zl.at[0], ze.at[j - 1, b - passing.start], {"feat": other}).wait_recv()
            remote(piece, piece, zl.at[0], zr.at[b], {"feat": other}).start()

    def pass_on(some):
        @pl.when(is_inner)
        def _():
            for b in some:
                g_pass(b)

    def make_grad(b, two):
        pieces = got.at[pl.ds(0, 3 if two else 2), b]
        total = column_sum(OWN, reach, b, gp[b].astype(F32))
        remote(pieces, pieces, gs.at[0], gr.at[0, b], owner_at(PAIR)).wait_recv()
        for role in (PAIR, AHEAD, BEHIND)[: 3 if two else 2]:
            total = total + got[role, b].astype(F32)
        grad = total.astype(BF)
        gg[rows(b), ocols(me)] = grad

        @pl.when(is_inner)
        def _():
            g_copy(1, b, zr.at[b]).start()

        if half > 1:
            @pl.when(jnp.logical_not(is_inner))
            def _():
                passes = (b >= passing.start) & (b < passing.stop)

                @pl.when(passes)
                def _():
                    g_copy(0, b, ze.at[mine - 1, b - passing.start]).start()

                @pl.when(jnp.logical_not(passes))
                def _():
                    g_copy(1, b, zr.at[b]).start()
                    g_copy(0, b, zr.at[b]).start()

                x_wait(b)

        gw[...] += lax.dot_general(xg[rows(b), :], grad, (((0,), (0,)), ((), ())), preferred_element_type=F32)

    def gx_down(j, b):
        return remote(ge.at[j - 1, b], gx.at[rows(b), :], ges.at[j - 1], ger.at[0], {"feat": end_at(j)})

    def turn_weight():
        w_swap(False).wait_recv()
        for j in range(half):
            wt[:, pl.ds(j * width, width)] = wg[xcols(end_at(j)), :].T

    def finish(b):
        @pl.when(is_inner)
        def _():
            g_wait(b)
            grads = jnp.dot(gg[rows(b), :], wt[...], preferred_element_type=F32).astype(BF)
            for j in ends:
                ge[j - 1, b] = grads[:, j * width : (j + 1) * width]
                gx_down(j, b).start()
            gx[rows(b), :] = grads[:, :width]

    @pl.when(is_inner)
    def _():
        turn_weight()

    waiting = list(range(straight, blocks))
    for c in range(blocks):
        for later in waiting[c : c + 1]:
            send_near(later)
        make_grad(c, c < straight)

    gwb[...] = gw[...].astype(BF)
    height = gw.shape[0]
    for stage in range(stages):
        size = factors[stage]
        chunk = height // size
        src, buf, out = gwb if stage == 0 else summed[stage - 1], gathered[stage], summed[stage]
        rs_s, rs_r, ag_s, ag_r = psems[4 * stage : 4 * stage + 4]

        def part(q):
            return pl.ds(pl.multiple_of(q * chunk, chunk), chunk)

        steps = range(1, size)
        if stage == 0 and size % 4 == 0 and size >= 8:
            near_step = 2 * (1 - 2 * lax.rem(chip, 2))
            hops = [-near_step, near_step] + [2 * h for h in range(2, size // 2 - 1)]
            steps = [lax.rem(h + t + size, size) for h in hops for t in (0, turn)] + [lax.rem(turn + size, size)]
        for step in steps:
            _, there, peer = stage_peer(stage, step)
            remote(src.at[part(there), :], buf.at[step - 1], rs_s.at[0], rs_r.at[0], {"blk": peer}).start()
        if stage == 0:
            for b in range(passing.start):
                finish(b)
            pass_on(passing)
        digit, _, _ = stage_peer(stage, 1)
        if stage == 0:
            total = gw[part(digit), :]
        else:
            total = src[part(digit), :].astype(F32)
        remote(buf, buf, rs_s.at[0], rs_r.at[0], owner_at(PAIR)).wait_recv()
        for step in range(1, size):
            total = total + buf[step - 1].astype(F32)
        out[part(digit), :] = total.astype(BF)
        for step in steps:
            _, _, peer = stage_peer(stage, step)
            piece = out.at[part(digit), :]
            remote(piece, piece, ag_s.at[0], ag_r.at[0], {"blk": peer}).start()
        if stage == 0:
            late = list(range(passing.stop, blocks))
            for b in passing:
                finish(b)
                if b != passing.start and late:
                    finish(late.pop(0))
            for b in late:
                finish(b)
        piece = out.at[pl.ds(0, height - chunk), :]
        remote(piece, piece, ag_s.at[0], ag_r.at[0], owner_at(PAIR)).wait_recv()
    gw[...] = (summed[-1] if stages else gwb)[...].astype(F32)

    for stage in range(stages):
        buf, out = gathered[stage], summed[stage]
        rs_s, rs_r, ag_s, ag_r = psems[4 * stage : 4 * stage + 4]
        remote(buf, buf, rs_s.at[0], rs_r.at[0], owner_at(PAIR)).wait_send()
        piece = out.at[pl.ds(0, height - height // factors[stage]), :]
        remote(piece, piece, ag_s.at[0], ag_r.at[0], owner_at(PAIR)).wait_send()

    def sent_all(ref, sem):
        remote(ref, ref, sem, ger.at[0], owner_at(PAIR)).wait_send()

    @pl.when(is_inner)
    def _():
        sent_all(x, xs.at[1])
        sent_all(gg.at[:, ocols(me)], zs.at[1])
        if half > 1 and passing:
            sent_all(gg.at[pl.ds(0, len(passing) * side), pl.ds(0, (half - 1) * ow)], zl.at[0])
        for j in ends:
            sent_all(pe.at[j - 1], es.at[j - 1])
            sent_all(ge.at[j - 1], ges.at[j - 1])
            sent_all(xg.at[:, pl.ds(0, (nz - 1) * width)], xb.at[j - 1])

    @pl.when(jnp.logical_not(is_inner))
    def _():
        sent_all(x, xs.at[1])
        sent_all(x, xs.at[0])
        sent_all(gg.at[pl.ds(0, (blocks - len(passing)) * side), ocols(me)], zs.at[1])
        sent_all(gg.at[:, ocols(me)], zs.at[0])
        remote(gx, gx, ges.at[0], ger.at[0], {"feat": inner}).wait_recv()

    sent_all(got.at[pl.ds(0, 4)], hs.at[0])
    sent_all(got.at[pl.ds(0, 4)], gs.at[0])

    @pl.when(is_inner)
    def _():
        w_swap(True).wait_send()
        for j in ends if group > 1 else ():
            sent_all(w_rest(j), ws.at[j])

    @pl.when(jnp.logical_not(is_inner))
    def _():
        if half > 1:
            w_up().wait_send()


def write_out(*refs):
    count = (len(refs) - 1) // 2
    done = refs[-1]
    copies = [pltpu.make_async_copy(refs[i], refs[count + i], done.at[i]) for i in range(count)]
    for copy in copies:
        copy.start()
    for copy in copies:
        copy.wait()


def on_device(nb, nz, x, w, tv, tr, tc, cnt, go):
    offs, slots, side = tv.shape[1], tv.shape[2], tv.shape[-1]
    height, width = x.shape
    blocks = height // side
    depth, ow = w.shape
    factors = stage_factors(nb, depth)
    dims = (nb, nz, offs, slots, blocks, side, width, ow, tuple(factors))
    spare = max(nz // 2 - 1, 1)
    vmem = pl.BlockSpec(memory_space=pltpu.VMEM)
    hbm = pl.BlockSpec(memory_space=pltpu.HBM)
    dma = pltpu.SemaphoreType.DMA
    psems = []
    for f in factors:
        psems += [dma((1,))] * 4
    block = (side, ow)
    results = pl.pallas_call(
        functools.partial(layer_kernel, dims),
        out_shape=(
            pltpu.VMEM((height, ow), BF),
            pltpu.VMEM((height, width), BF),
            pltpu.VMEM((depth, ow), F32),
        ),
        in_specs=[hbm] * 7,
        out_specs=(vmem, vmem, vmem),
        scratch_shapes=[
            pltpu.SMEM((offs, 1, slots), tr.dtype),
            pltpu.SMEM((offs, 1, slots), tc.dtype),
            pltpu.SMEM(cnt.shape, cnt.dtype),
            pltpu.VMEM((height, nz * width), BF),
            pltpu.VMEM((depth, nz * ow), BF),
            pltpu.VMEM((offs, slots, side, side), BF),
            pltpu.VMEM((height, ow), BF),
            pltpu.VMEM((offs, slots, side, side), BF),
            pltpu.VMEM((offs, slots, *block), F32),
            pltpu.VMEM((blocks, *block), F32),
            pltpu.VMEM((blocks, *block), BF),
            pltpu.VMEM((offs, blocks, *block), BF),
            pltpu.VMEM((offs, blocks, *block), BF),
            pltpu.VMEM((height, nz * ow), BF),
            pltpu.VMEM((depth, ow), BF),
            pltpu.VMEM((spare, blocks, *block), BF),
            pltpu.VMEM((spare, blocks, side, width), BF),
            pltpu.VMEM((nz * ow, nz // 2 * width), BF),
        ]
        + [pltpu.VMEM((blocks, *block), BF)] * 5
        + [pltpu.VMEM((f - 1, depth // f, ow), BF) for f in factors]
        + [pltpu.VMEM((depth, ow), BF) for f in factors]
        + [dma((2,)), dma((blocks,)), dma((spare,))]
        + [dma((1,)), dma((2, blocks)), dma((2,))]
        + [dma((1,)), dma((2, blocks)), dma((max(blocks - 2, 1),))]
        + [dma((2,)), dma((blocks,)), dma((1,)), dma((spare, blocks))]
        + [dma((spare,)), dma((spare,)), dma((1,))]
        + [dma((spare + 1,)), dma((spare, 2)), dma((1,)), dma((1,)), dma((7,))]
        + psems,
        compiler_params=pltpu.CompilerParams(
            collective_id=0, has_side_effects=True, vmem_limit_bytes=32 * 1024 * 1024
        ),
    )(*[pltpu.with_memory_space_constraint(a, pltpu.HBM) for a in (x, w, tv, jnp.swapaxes(tr, 0, 1), jnp.swapaxes(tc, 0, 1), cnt, go)])
    return pl.pallas_call(
        write_out,
        out_shape=tuple(jax.ShapeDtypeStruct(r.shape, r.dtype) for r in results),
        in_specs=[vmem] * len(results),
        out_specs=(hbm,) * len(results),
        scratch_shapes=[dma((len(results),))],
    )(*[pltpu.with_memory_space_constraint(r, pltpu.VMEM) for r in results])


def solution(mesh):
    return jax.shard_map(
        functools.partial(on_device, mesh.shape["blk"], mesh.shape["feat"]),
        mesh=mesh,
        in_specs=(
            P("blk", "feat"),
            P(None, "feat"),
            P("blk", None, None, None, None),
            P("blk", None, None),
            P("blk", None, None),
            P("blk", None),
            P("blk", "feat"),
        ),
        out_specs=(P("blk", "feat"), P("blk", "feat"), P(None, "feat")),
        check_vma=False,
    )
```
